32 devices in a mesh: fsdp: 16 (over z, y, core), sp: 2 (over x).
Axes of the slice: x: 2, y: 2, z: 4, core: 2. Of those that a mesh axis runs over, the one named last changes fastest.
Arguments:
- image: bfloat16 [16, 16, 64, 512], P('fsdp', 'sp'), may hold values from -6 to 6
- embedding: bfloat16 [16, 2048], P('fsdp'), may hold values from -6 to 6
- text: bfloat16 [16, 128, 2048], P('fsdp'), may hold values from -6 to 6
- heights: int32 [16], P('fsdp'), may hold values from 8 to 16, as said below
- gain_one: bfloat16 [512], P('fsdp'), may hold values from 0.099609375 to 1.8984375
- conv_one: bfloat16 [4608, 512], P('fsdp'), may hold values from -0.09375 to 0.09375
- emb_proj: bfloat16 [2048, 1024], P('fsdp'), may hold values from -0.125 to 0.125
- gain_two: bfloat16 [512], P('fsdp'), may hold values from 0.099609375 to 1.8984375
- conv_two: bfloat16 [4608, 512], P('fsdp'), may hold values from -0.09375 to 0.09375
- gain_three: bfloat16 [512], P('fsdp'), may hold values from 0.099609375 to 1.8984375
- qkv_proj: bfloat16 [512, 1536], P('fsdp'), may hold values from -0.25 to 0.25
- text_proj: bfloat16 [2048, 1024], P('fsdp'), may hold values from -0.125 to 0.125
- out_proj: bfloat16 [512, 512], P('fsdp'), may hold values from -6 to 6
- cotangent: bfloat16 [16, 16, 64, 512], P('fsdp', 'sp'), may hold values from -6 to 6
Outputs:
- output: bfloat16 [16, 16, 64, 512], P('fsdp', 'sp')
- image_grad: float32 [16, 16, 64, 512], P('fsdp', 'sp')
- embedding_grad: float32 [16, 2048], P('fsdp')
- text_grad: float32 [16, 128, 2048], P('fsdp')
- gain_one_grad: float32 [512], P('fsdp')
- conv_one_grad: float32 [4608, 512], P('fsdp')
- emb_proj_grad: float32 [2048, 1024], P('fsdp')
- gain_two_grad: float32 [512], P('fsdp')
- conv_two_grad: float32 [4608, 512], P('fsdp')
- gain_three_grad: float32 [512], P('fsdp')
- qkv_proj_grad: float32 [512, 1536], P('fsdp')
- text_proj_grad: float32 [2048, 1024], P('fsdp')
- out_proj_grad: float32 [512, 512], P('fsdp')
The draws below stay inside these ranges and needn't reach their ends.
Inputs may be any that keep to these rules, and one draw needn't show every extreme that they name: `heights`: each item's image has this many rows; some item has 16 rows.
All inputs are finite; a program needn't handle non-finite values.
Results may differ from the reference program's by a relative error of at most 0.015.
Values may be sent and summed in bfloat16 or wider, within the bound.
A program may use at most 192 MiB of HBM per device.

```python
import jax
import jax.numpy as jnp
from jax import lax

C = 512
GROUPS = 32
EMB = 2048
XF = 2048
TEXT = 128
HEAD = 64
W = 64
ROWS_DEV = 8
HMAX = 16
HMIN = 8
ITEMS = 16
N_SP = 2


def draw_heights(key, part):
    first, second = jax.random.split(jax.random.fold_in(key, 7))
    drawn = jax.random.randint(first, (ITEMS,), HMIN, HMAX + 1, dtype=jnp.int32)
    tallest = jax.random.randint(second, (), 0, ITEMS, dtype=jnp.int32)
    return jnp.where(jnp.arange(ITEMS, dtype=jnp.int32) == tallest, HMAX, drawn).astype(jnp.int32)


def shard_levels(key, shape, cuts, low, largest):
    loudness, own = 1.0, jax.random.fold_in(key, 6)
    for dim, blocks in cuts:
        steps = jnp.exp(jax.random.uniform(jax.random.fold_in(own, dim), (blocks,), jnp.float32, low / len(cuts), largest / len(cuts)))
        loudness = loudness * jnp.repeat(steps, shape[dim] // blocks).reshape([-1 if axis == dim else 1 for axis in range(len(shape))])
    return loudness


def centred(own_key, dims, deviation, reach, pieces=(), kind=jnp.bfloat16):
    values = jax.random.normal(own_key, dims, jnp.float32) * deviation
    if len(pieces) > 0:
        values = shard_levels(own_key, dims, pieces, -0.22, 0.18) * values
    return jnp.clip(values, min=-reach, max=reach).astype(kind)


def setup_inputs(seed: int = 0) -> dict:
    key_list = jax.random.split(jax.random.key(seed), 15)
    image = centred(key_list[0], (ITEMS, HMAX, W, C), 1.0, 6.0, ((0, 16), (1, 2)))
    embedding = centred(key_list[1], (ITEMS, EMB), 1.0, 6.0, ((0, 16),))
    text = centred(key_list[2], (ITEMS, TEXT, XF), 1.0, 6.0, ((0, 16),))
    heights = draw_heights(jax.random.fold_in(key_list[14], 71), 0)
    gain_one = jnp.clip(1.0 + 0.18 * jax.random.normal(key_list[4], (C,), jnp.float32), 0.099609375, 1.8984375).astype(jnp.bfloat16)
    conv_one = centred(key_list[5], (9 * C, C), (9 * C) ** -0.5, 0.09375, ((0, 16),))
    emb_proj = centred(key_list[6], (EMB, 2 * C), EMB ** -0.5, 0.125, ((0, 16),))
    gain_two = jnp.clip(1.0 + 0.18 * jax.random.normal(key_list[7], (C,), jnp.float32), 0.099609375, 1.8984375).astype(jnp.bfloat16)
    conv_two = centred(key_list[8], (9 * C, C), (9 * C) ** -0.5, 0.09375, ((0, 16),))
    gain_three = jnp.clip(1.0 + 0.18 * jax.random.normal(key_list[9], (C,), jnp.float32), 0.099609375, 1.8984375).astype(jnp.bfloat16)
    qkv_proj = centred(key_list[10], (C, 3 * C), C ** -0.5, 0.25, ((0, 16),))
    text_proj = centred(key_list[11], (XF, 2 * C), XF ** -0.5, 0.125, ((0, 16),))
    out_proj = centred(key_list[12], (C, C), (0.6 * (ROWS_DEV * W * N_SP + TEXT) ** 0.5 * C ** -0.5), 6.0, ((0, 16),))
    cotangent = centred(key_list[13], (ITEMS, HMAX, W, C), 1.0, 6.0, ((0, 16), (1, 2)))
    return {"image": image, "embedding": embedding, "text": text, "heights": heights, "gain_one": gain_one, "conv_one": conv_one, "emb_proj": emb_proj, "gain_two": gain_two, "conv_two": conv_two, "gain_three": gain_three, "qkv_proj": qkv_proj, "text_proj": text_proj, "out_proj": out_proj, "cotangent": cotangent}


EPSILON = 1e-05
MASKED = -1e+30
EXACT = lax.Precision.HIGHEST

@jax.custom_vjp
def low(v):
    return lax.optimization_barrier(v.astype(jnp.bfloat16)).astype(jnp.float32)

@jax.custom_vjp
def low_back(v):
    return v

def low_keep(v):
    return (low(v), None)

def low_pass(kept, grad):
    return (grad,)

def back_keep(v):
    return (v, None)

def back_low(kept, grad):
    return (low(grad),)
low.defvjp(low_keep, low_pass)
low_back.defvjp(back_keep, back_low)

def group_norm(field, pixel_mask, count, gain):
    grouped = field.reshape(field.shape[0], GROUPS, -1)
    weight = pixel_mask[:, :, None]
    mean = lax.optimization_barrier(jnp.sum(grouped * weight, axis=(0, 2))) / count
    centered = (grouped - mean[:, None]) * weight
    variance = lax.optimization_barrier(jnp.sum(centered * centered, axis=(0, 2))) / count
    return (centered * lax.rsqrt(variance + EPSILON)[:, None]).reshape(field.shape) * gain

def convolve(field, weight, rows, columns):
    padded = jnp.pad(field.reshape(rows, columns, -1), ((1, 1), (1, 1), (0, 0)))
    taps = [padded[down:down + rows, across:across + columns] for down in range(3) for across in range(3)]
    stacked = jnp.concatenate(taps, axis=2).reshape(rows * columns, -1)
    return jnp.dot(stacked, weight, precision=EXACT)

def item_forward(image, embedding, text, height, weights):
    gain_one, conv_one, emb_proj, gain_two, conv_two, gain_three, qkv_proj, text_proj, out_proj = weights
    rows = image.shape[0]
    columns = image.shape[1]
    pixels = rows * columns
    row_valid = (jnp.arange(rows, dtype=jnp.int32) < height).astype(jnp.float32)
    pixel_mask = jnp.repeat(row_valid, columns)[:, None]
    count = (height * columns * (C // GROUPS)).astype(jnp.float32)
    masked = image.reshape(pixels, C) * pixel_mask
    act_one = low(jax.nn.silu(group_norm(masked, pixel_mask, count, gain_one)) * pixel_mask)
    conv_out = low_back(convolve(act_one, conv_one, rows, columns)) * pixel_mask
    scales = low_back(jnp.dot(low(jax.nn.silu(embedding))[None, :], emb_proj, precision=EXACT))
    hidden_two = group_norm(conv_out, pixel_mask, count, gain_two) * (1.0 + scales[:, :C]) + scales[:, C:]
    act_two = low(jax.nn.silu(hidden_two) * pixel_mask)
    resid = masked + low_back(convolve(act_two, conv_two, rows, columns)) * pixel_mask
    normed = low(group_norm(resid, pixel_mask, count, gain_three))
    projected = low(low_back(jnp.dot(normed, qkv_proj, precision=EXACT)))
    text_kv = low(low_back(jnp.dot(text, text_proj, precision=EXACT)))
    keys = jnp.concatenate([projected[:, C:2 * C], text_kv[:, :C]], axis=0)
    values = jnp.concatenate([projected[:, 2 * C:], text_kv[:, C:]], axis=0)
    keep = jnp.concatenate([pixel_mask[:, 0] > 0, jnp.ones((text.shape[0],), dtype=bool)])
    factor = HEAD ** (-0.5)

    def by_head(matrix):
        return matrix.reshape(matrix.shape[0], -1, HEAD).transpose(1, 0, 2)

    def one_head(parts):
        query, key, value = parts
        scores = low_back(jnp.dot(query, key.T, precision=EXACT) * factor)
        scores = jnp.where(keep[None, :], scores, MASKED)
        chances = low(jax.nn.softmax(scores, axis=-1))
        return jnp.dot(chances, value, precision=EXACT)
    attended = lax.map(jax.checkpoint(one_head), (by_head(projected[:, :C]), by_head(keys), by_head(values)))
    merged = low(low_back(attended.transpose(1, 0, 2).reshape(pixels, C)))
    branch = jnp.dot(merged, out_proj, precision=EXACT) * pixel_mask
    return (resid + branch).reshape(rows, columns, C)

def reference(image, embedding, text, heights, gain_one, conv_one, emb_proj, gain_two, conv_two, gain_three, qkv_proj, text_proj, out_proj, cotangent):
    weights = tuple((matrix.astype(jnp.float32) for matrix in (gain_one, conv_one, emb_proj, gain_two, conv_two, gain_three, qkv_proj, text_proj, out_proj)))

    def forward(image_float, emb_float, text_float, *weights_float):

        def one_item(item):
            return item_forward(item[0], item[1], item[2], item[3], weights_float)
        return lax.map(one_item, (image_float, emb_float, text_float, heights))
    output, pullback = jax.vjp(forward, image.astype(jnp.float32), embedding.astype(jnp.float32), text.astype(jnp.float32), *weights)
    grads = pullback(cotangent.astype(jnp.float32))
    return (output.astype(jnp.bfloat16), grads[0], grads[1], grads[2], grads[3], grads[4], grads[5], grads[6], grads[7], grads[8], grads[9], grads[10], grads[11])
```

```python
import functools

import jax
import jax.numpy as jnp
from jax import lax
from jax.experimental import pallas as pl
from jax.experimental.pallas import tpu as pltpu
from jax.sharding import PartitionSpec as P

C = 512
GROUPS = 32
HEAD = 64
EPSILON = 1e-05
MASKED = -1e30
LIMIT = 60 * 1024 * 1024

F32 = jnp.float32
BF16 = jnp.bfloat16
DMA = pltpu.SemaphoreType.DMA
ANY = pl.BlockSpec(memory_space=pl.ANY)
VMEM = pl.BlockSpec(memory_space=pltpu.VMEM)
SMEM = pl.BlockSpec(memory_space=pltpu.SMEM)


def sizes_of(fsdp, sp):
    lines = sp if fsdp % (2 * sp) == 0 else 1
    return fsdp // (2 * lines), lines, 2


def remote(src, dst, send, recv, device):
    return pltpu.make_async_remote_copy(
        src, dst, send, recv, device_id=device, device_id_type=pl.DeviceIdType.MESH
    )


def greet(peers):
    barrier = pltpu.get_barrier_semaphore()
    for peer in peers:
        pl.semaphore_signal(
            barrier, inc=1, device_id=peer, device_id_type=pl.DeviceIdType.MESH
        )
    pl.semaphore_wait(barrier, len(peers))


def params(cid):
    return pltpu.CompilerParams(
        collective_id=cid, has_side_effects=True, vmem_limit_bytes=LIMIT
    )


def tiles_start(fsdp, source, dest, send, recv, pick):
    me, x = lax.axis_index("fsdp"), lax.axis_index("sp")
    copies = []
    for d in range(1, fsdp):
        to = (me + d) % fsdp
        copy = remote(pick(source, to), dest.at[me], send.at[d], recv.at[d], (to, x))
        copy.start()
        copies.append(copy)
    return copies


def gather_kernel(dims, fsdp, sp, shapes, *refs):
    zs, ys, cs = dims
    count = len(shapes)
    shards, tiles, table = refs[:count], refs[count], refs[count + 1]
    refs = refs[count + 2 :]
    outs, tiles_out, scales_out = refs[:count], refs[count], refs[count + 1]
    refs = refs[count + 2 :]
    bufs, got, part, part_in = refs[:count], refs[count], refs[count + 1], refs[count + 2]
    zsend, zrecv, ysend, yrecv, xsend, xrecv, csend, crecv, local, tsem, psem = refs[count + 3 :]
    me, x = lax.axis_index("fsdp"), lax.axis_index("sp")
    z, y, c = me // (ys * cs), (me // cs) % ys, me % cs

    def dev(zz, yy, cc):
        return ((zz * ys + yy) * cs + cc, x)

    peers = [((me + d) % fsdp, x) for d in range(1, fsdp)]
    peers += [(me, (x + d) % sp) for d in range(1, sp)]
    greet(peers)
    flying = tiles_start(fsdp, tiles, got, tsem.at[0], tsem.at[1], lambda ref, to: ref.at[to])

    def owner(dz, dy):
        return (z - dz + zs) % zs, (y - dy + ys) % ys

    def piece(a):
        return x if shapes[a][0] > 1 else 0

    def zcopy(a, dz):
        h = piece(a)
        return remote(
            shards[a].at[h],
            outs[a].at[z, y, c, h],
            zsend.at[a, dz],
            zrecv.at[a, dz],
            dev((z + dz) % zs, y, c),
        )

    def ycopy(a, dz, dy):
        h = piece(a)
        zz, _ = owner(dz, 0)
        src = shards[a].at[h] if dz == 0 else outs[a].at[zz, y, c, h]
        return remote(
            src,
            outs[a].at[zz, y, c, h],
            ysend.at[a, dz, dy],
            yrecv.at[a, dz, dy],
            dev(z, (y + dy) % ys, c),
        )

    def xcopy(a, dz, dy, dx):
        zz, yy = owner(dz, dy)
        return remote(
            outs[a].at[zz, yy, c, x],
            outs[a].at[zz, yy, c, x],
            xsend.at[a, dz, dy, dx],
            xrecv.at[a, dz, dy, dx],
            (me, (x + dx) % sp),
        )

    def ccopy(a, dz, dy, dx):
        zz, yy = owner(dz, dy)
        if dz == 0 and dy == 0:
            src, dst = shards[a], outs[a].at[zz, yy, c]
        else:
            h = (x - dx + sp) % sp if shapes[a][0] > 1 else 0
            src = dst = outs[a].at[zz, yy, c, h]
        return remote(src, dst, csend.at[a, dz, dy, dx], crecv.at[a, dz, dy, dx], dev(z, y, 1 - c))

    def launch(copy):
        copy.start()
        flying.append(copy)

    def onward(a, dz, dy):
        if shapes[a][0] > 1:
            for dx in range(1, sp):
                launch(xcopy(a, dz, dy, dx))
        launch(ccopy(a, dz, dy, 0))

    for a in range(count):
        for dz in range(1, zs):
            launch(zcopy(a, dz))
        for dy in range(1, ys):
            launch(ycopy(a, 0, dy))
        launch(ccopy(a, 0, 0, 0))
        pltpu.make_async_copy(shards[a], bufs[a], local.at[a]).start()

    got[me] = tiles[me]
    for copy in flying[: fsdp - 1]:
        copy.wait_recv()
    rows = got[:, 0, :].astype(BF16)
    for j in range(8):
        part[:, j, :] = jnp.dot(
            rows, table[:, j * 128 : (j + 1) * 128], preferred_element_type=F32
        )
    part_in[me] = part[me]
    for a in range(count):
        pltpu.make_async_copy(shards[a], bufs[a], local.at[a]).wait()
        pltpu.make_async_copy(bufs[a], outs[a].at[z, y, c], local.at[a]).start()
    second = tiles_start(fsdp, part, part_in, psem.at[0], psem.at[1], lambda ref, to: ref.at[to])
    flying += second

    def over_z(a):
        for dz in range(1, zs):
            zcopy(a, dz).wait_recv()
            for dy in range(1, ys):
                launch(ycopy(a, dz, dy))
            onward(a, dz, 0)

    def over_y(a):
        for dz in range(zs):
            for dy in range(1, ys):
                ycopy(a, dz, dy).wait_recv()
                onward(a, dz, dy)

    def over_x(a):
        if shapes[a][0] > 1:
            for dz in range(zs):
                for dy in range(ys):
                    if dz + dy:
                        for dx in range(1, sp):
                            xcopy(a, dz, dy, dx).wait_recv()
                            launch(ccopy(a, dz, dy, dx))

    for step in range(count + 2):
        if step < count:
            over_z(step)
        if 1 <= step <= count:
            over_y(step - 1)
        if step >= 2:
            over_x(step - 2)
    for copy in second:
        copy.wait_recv()
    total = part_in[0]
    for f in range(1, fsdp):
        total = total + part_in[f]
    scales_out[...] = total
    tiles_out[...] = got[...]
    for a in range(count):
        for dz in range(zs):
            for dy in range(ys):
                many = sp if shapes[a][0] > 1 and dz + dy else 1
                for dx in range(many):
                    ccopy(a, dz, dy, dx).wait_recv()
        pltpu.make_async_copy(bufs[a], outs[a].at[z, y, c], local.at[a]).wait()
    for copy in flying:
        copy.wait_send()


def parts_of(rows, sp):
    return sp if rows % (16 * sp) == 0 else 1


def gather(shards, kinds, tiles, table, fsdp, sp):
    dims = sizes_of(fsdp, sp)
    zs, ys, cs = dims
    count = len(shards)
    split = []
    for shard, kind in zip(shards, kinds, strict=True):
        rows, width = shard.shape
        h = parts_of(rows, sp) if kind else 1
        split.append(shard.reshape(h, rows // h, width))
    shapes = [s.shape for s in split]
    outs = pl.pallas_call(
        functools.partial(gather_kernel, dims, fsdp, sp, shapes),
        out_shape=[jax.ShapeDtypeStruct(dims + s, BF16) for s in shapes]
        + [
            jax.ShapeDtypeStruct((fsdp, 8, 128), F32),
            jax.ShapeDtypeStruct((8, 128), F32),
        ],
        in_specs=[ANY] * count + [VMEM] * 2,
        out_specs=[ANY] * count + [VMEM] * 2,
        scratch_shapes=[pltpu.VMEM(s, BF16) for s in shapes]
        + [pltpu.VMEM((fsdp, 8, 128), F32)] * 3
        + [DMA((count, zs))] * 2
        + [DMA((count, zs, ys))] * 2
        + [DMA((count, zs, ys, sp))] * 4
        + [DMA((count,)), DMA((2, fsdp)), DMA((2, fsdp))],
        compiler_params=params(0),
        name="gather",
    )(*split, tiles, table)
    whole = [
        o.reshape(fsdp * s.shape[0], s.shape[1]) for o, s in zip(outs[:count], shards, strict=True)
    ]
    return whole, outs[count], outs[count + 1]


def add_rows(rows, first, second, put):
    step = 32 if rows % 32 == 0 else (16 if rows % 16 == 0 else 8)

    def body(i, _):
        at = pl.ds(pl.multiple_of(i * step, step), step)
        put(at, first[at, :].astype(F32) + second[at, :].astype(F32))
        return 0

    lax.fori_loop(0, rows // step, body, 0)


def scatter_kernel(dims, fsdp, sp, shapes, modes, *refs):
    zs, ys, cs = dims
    count = len(shapes)
    grads, tiles = refs[:count], refs[count]
    refs = refs[count + 1 :]
    outs, tiles_out, small_out = refs[:count], refs[count], refs[count + 1]
    refs = refs[count + 2 :]
    own, crecvd, xrecvd, yrecvd, zrecvd, last = (
        refs[k * count : (k + 1) * count] for k in range(6)
    )
    refs = refs[6 * count :]
    got, small = refs[0], refs[1]
    csem, xsem, ysem, zsem, fsem, lsem, tsem, ssem = refs[2:]
    me, x = lax.axis_index("fsdp"), lax.axis_index("sp")
    z, y, c = me // (ys * cs), (me // cs) % ys, me % cs

    def dev(zz, yy, cc):
        return ((zz * ys + yy) * cs + cc, x)

    peers = [((me + d) % fsdp, x) for d in range(1, fsdp)]
    peers += [(me, (x + d) % sp) for d in range(1, sp)]
    greet(peers)
    flying = []

    def launch(copy):
        copy.start()
        flying.append(copy)

    first = tiles_start(fsdp, tiles, got, tsem.at[0], tsem.at[1], lambda ref, to: ref.at[to])
    flying += first

    order = [(dz, dy) for dz in range(zs - 1, -1, -1) for dy in range(ys - 1, -1, -1)]

    def where(dz, dy):
        return (z + dz) % zs, (y + dy) % ys

    def ccopy(a, dz, dy):
        zz, yy = where(dz, dy)
        return remote(
            grads[a].at[zz, yy, 1 - c],
            crecvd[a].at[dz, dy],
            csem.at[0, a, dz, dy],
            csem.at[1, a, dz, dy],
            dev(z, y, 1 - c),
        )

    def mine(a, dz, dy):
        zz, yy = where(dz, dy)
        return pltpu.make_async_copy(grads[a].at[zz, yy, c], own[a].at[dz, dy], lsem.at[a, dz, dy])

    def xcopy(a, dz, dy, dx):
        to = (x + dx) % sp
        return remote(
            own[a].at[dz, dy, to],
            xrecvd[a].at[dz, dy, dx - 1],
            xsem.at[0, a, dz, dy, dx],
            xsem.at[1, a, dz, dy, dx],
            (me, to),
        )

    def ycopy(a, dz, dy):
        h = x if shapes[a][0] > 1 else 0
        return remote(
            own[a].at[dz, dy, h],
            yrecvd[a].at[dz, dy - 1],
            ysem.at[0, a, dz, dy],
            ysem.at[1, a, dz, dy],
            dev(z, (y + dy) % ys, c),
        )

    def zcopy(a, dz):
        h = x if shapes[a][0] > 1 else 0
        return remote(
            own[a].at[dz, 0, h],
            zrecvd[a].at[dz - 1],
            zsem.at[0, a, dz],
            zsem.at[1, a, dz],
            dev((z + dz) % zs, y, c),
        )

    def fcopy(a, dx):
        return remote(
            last[a].at[x],
            last[a].at[x],
            fsem.at[0, a, dx],
            fsem.at[1, a, dx],
            (me, (x + dx) % sp),
        )

    def into(ref):
        def put(at, value):
            ref[at, :] = value.astype(BF16)

        return put

    for a in range(count):
        for dz, dy in order:
            launch(ccopy(a, dz, dy))
            mine(a, dz, dy).start()

    def over_c(a):
        h, rows, _ = shapes[a]
        for dz, dy in order:
            mine(a, dz, dy).wait()
            ccopy(a, dz, dy).wait_recv()
            for k in range(h):
                ref = own[a].at[dz, dy, k]
                add_rows(rows, ref, crecvd[a].at[dz, dy, k], into(ref))
            if h > 1:
                for dx in range(1, sp):
                    launch(xcopy(a, dz, dy, dx))

    def over_x(a):
        h, rows, _ = shapes[a]
        for dz, dy in order:
            if h > 1:
                ref = own[a].at[dz, dy, x]
                for dx in range(1, sp):
                    xcopy(a, dz, dy, dx).wait_recv()
                    add_rows(rows, ref, xrecvd[a].at[dz, dy, dx - 1], into(ref))
            if dy:
                launch(ycopy(a, dz, dy))

    def over_y(a):
        h, rows, _ = shapes[a]
        k = x if h > 1 else 0
        for dz in range(zs - 1, -1, -1):
            ref = own[a].at[dz, 0, k]
            for dy in range(1, ys):
                ycopy(a, dz, dy).wait_recv()
                add_rows(rows, ref, yrecvd[a].at[dz, dy - 1], into(ref))
            if dz:
                launch(zcopy(a, dz))

    def over_z(a):
        h, rows, _ = shapes[a]
        k = x if h > 1 else 0
        ref = own[a].at[0, 0, k]
        for dz in range(1, zs):
            zcopy(a, dz).wait_recv()
            target = last[a].at[x] if dz == zs - 1 else ref
            add_rows(rows, ref, zrecvd[a].at[dz - 1], into(target))
        if zs == 1:
            last[a][x] = ref[...]
        for dx in range(1, sp):
            launch(fcopy(a, dx))

    for step in range(count + 3):
        if step < count:
            over_c(step)
        if 1 <= step <= count:
            over_x(step - 1)
        if 2 <= step <= count + 1:
            over_y(step - 2)
        if step >= 3:
            over_z(step - 3)

    got[me] = tiles[me]
    for copy in first:
        copy.wait_recv()
    total = got[0]
    for f in range(1, fsdp):
        total = total + got[f]
    small[x] = total
    for dx in range(1, sp):
        launch(remote(small.at[x], small.at[x], ssem.at[0, dx], ssem.at[1, dx], (me, (x + dx) % sp)))
    tiles_out[...] = got[...]
    for a in range(count):
        for dx in range(1, sp):
            fcopy(a, dx).wait_recv()
        if modes[a] == "add" and shapes[a][0] == 1:
            value = last[a][0].astype(F32)
            for k in range(1, sp):
                value = value + last[a][k].astype(F32)
            outs[a][0] = value
        else:
            for k in range(sp):
                outs[a][k] = last[a][k].astype(F32)
    for dx in range(1, sp):
        remote(
            small.at[x], small.at[x], ssem.at[0, dx], ssem.at[1, dx], (me, (x + dx) % sp)
        ).wait_recv()
    total = small[0]
    for k in range(1, sp):
        total = total + small[k]
    small_out[...] = total
    for copy in flying:
        copy.wait_send()


def scatter(grads, modes, tiles, fsdp, sp):
    dims = sizes_of(fsdp, sp)
    zs, ys, cs = dims
    count = len(grads)
    split, shapes, outs = [], [], []
    for grad, mode in zip(grads, modes, strict=True):
        rows, width = grad.shape[0] // fsdp, grad.shape[1]
        h = parts_of(rows, sp) if mode == "add" else 1
        shapes.append((h, rows // h, width))
        split.append(grad.reshape(dims + (h, rows // h, width)))
        copies = 1 if mode == "add" and h == 1 else sp
        outs.append(jax.ShapeDtypeStruct((copies, rows // h, width), F32))

    def scratch(shape):
        return pltpu.VMEM(shape, BF16)

    results = pl.pallas_call(
        functools.partial(scatter_kernel, dims, fsdp, sp, shapes, modes),
        out_shape=outs
        + [jax.ShapeDtypeStruct((fsdp, 8, 128), F32), jax.ShapeDtypeStruct((8, 128), F32)],
        in_specs=[ANY] * count + [VMEM],
        out_specs=[VMEM] * (count + 2),
        scratch_shapes=[scratch((zs, ys) + s) for s in shapes]
        + [scratch((zs, ys) + s) for s in shapes]
        + [scratch((zs, ys, sp - 1) + s[1:] if s[0] > 1 else (1, 1, 1, 16, 128)) for s in shapes]
        + [scratch((zs, max(ys - 1, 1)) + s[1:]) for s in shapes]
        + [scratch((max(zs - 1, 1),) + s[1:]) for s in shapes]
        + [scratch((sp,) + s[1:]) for s in shapes]
        + [pltpu.VMEM((fsdp, 8, 128), F32), pltpu.VMEM((sp, 8, 128), F32)]
        + [
            DMA((2, count, zs, ys)),
            DMA((2, count, zs, ys, sp)),
            DMA((2, count, zs, ys)),
            DMA((2, count, zs)),
            DMA((2, count, sp)),
            DMA((count, zs, ys)),
            DMA((2, fsdp)),
            DMA((2, sp)),
        ],
        compiler_params=params(4),
        name="scatter",
    )(*split, tiles)
    return results[:count], results[count], results[count + 1]


def lane_groups(values):
    lane = lax.broadcasted_iota(jnp.int32, values.shape, 1)
    step = 1
    while step < C // GROUPS:
        up = pltpu.roll(values, step, 1)
        down = pltpu.roll(values, C - step, 1)
        values = values + jnp.where((lane & step) != 0, up, down)
        step *= 2
    return values


def column_sums(rows, fields):
    probe = jax.eval_shape(lambda: fields(0))

    def body(r, sums):
        return tuple(
            s + jnp.sum(v.reshape(-1, 8, C), axis=0) for s, v in zip(sums, fields(r), strict=True)
        )

    sums = lax.fori_loop(0, rows, body, tuple(jnp.zeros((8, C), F32) for _ in probe))
    return [jnp.broadcast_to(jnp.sum(s, axis=0, keepdims=True), (8, C)) for s in sums]


def stack_rows(*values):
    row = lax.broadcasted_iota(jnp.int32, (8, C), 0)
    out = jnp.zeros((8, C), F32)
    for k, value in enumerate(values):
        out = jnp.where(row == k, value, out)
    return out


class Swap:
    def __init__(self, sp, sums, ssem, hsem):
        self.sp, self.sums, self.ssem, self.hsem = sp, sums, ssem, hsem
        self.me, self.x = lax.axis_index("fsdp"), lax.axis_index("sp")

    def peers(self):
        return [(self.me, (self.x + d) % self.sp) for d in range(1, self.sp)]

    def _sums(self, k, d):
        return remote(
            self.sums.at[k, self.x],
            self.sums.at[k, self.x],
            self.ssem.at[0, k, d],
            self.ssem.at[1, k, d],
            (self.me, (self.x + d) % self.sp),
        )

    def sums_start(self, k, value):
        self.sums[k, self.x] = value
        for d in range(1, self.sp):
            self._sums(k, d).start()

    def sums_wait(self, k):
        for d in range(1, self.sp):
            self._sums(k, d).wait()
        return [self.sums[k, i] for i in range(self.sp)]

    def _up(self, k, src, dst):
        to = (self.x + self.sp - 1) % self.sp
        return remote(src, dst.at[1], self.hsem.at[0, k, 0], self.hsem.at[1, k, 0], (self.me, to))

    def _down(self, k, src, dst):
        to = (self.x + 1) % self.sp
        return remote(src, dst.at[0], self.hsem.at[0, k, 1], self.hsem.at[1, k, 1], (self.me, to))

    def edges_start(self, k, top, bottom, dst):
        @pl.when(self.x > 0)
        def _():
            self._up(k, top, dst).start()

        @pl.when(self.x < self.sp - 1)
        def _():
            self._down(k, bottom, dst).start()

    def edges_wait(self, k, top, bottom, dst):
        @pl.when(self.x > 0)
        def _():
            self._up(k, top, dst).wait_send()
            self._down(k, bottom, dst).wait_recv()

        @pl.when(self.x < self.sp - 1)
        def _():
            self._down(k, bottom, dst).wait_send()
            self._up(k, top, dst).wait_recv()


def put_shifted(dst, at, value):
    columns = value.shape[0]
    col = lax.broadcasted_iota(jnp.int32, value.shape, 0)
    dst[1, at] = value.astype(BF16)
    dst[0, at] = jnp.where(col == 0, 0.0, pltpu.roll(value, 1, 0)).astype(BF16)
    dst[2, at] = jnp.where(col == columns - 1, 0.0, pltpu.roll(value, columns - 1, 0)).astype(BF16)


def taps(rows, columns, shifted, weight, acc, back):
    pixels = rows * columns

    def body(t, _):
        total = None
        for dc in range(3):
            if back:
                lhs = shifted[2 - dc, pl.ds(2 - t, rows)].reshape(pixels, C)
            else:
                lhs = shifted[dc, pl.ds(t, rows)].reshape(pixels, C)
            rhs = weight[pl.ds(pl.multiple_of((3 * t + dc) * C, C), C), :]
            out = lax.dot_general(
                lhs, rhs, (((1,), (1 if back else 0,)), ((), ())), preferred_element_type=F32
            )
            total = out if total is None else total + out
        total = total.reshape(rows, columns, C)

        @pl.when(t == 0)
        def _():
            acc[...] = total

        @pl.when(t > 0)
        def _():
            acc[...] += total

        return 0

    lax.fori_loop(0, 3, body, 0)


def numbers(height, rows, columns, sp):
    x = lax.axis_index("sp")
    ids = x * rows + jnp.arange(-1, rows + 1, dtype=jnp.int32)
    valid = ((ids >= 0) & (ids < height)).astype(F32)
    count = (height * columns * (C // GROUPS)).astype(F32)
    held = jnp.clip(height - rows * jnp.arange(sp, dtype=jnp.int32), 0, rows)
    held = (held * columns * (C // GROUPS)).astype(F32)
    bias = jnp.where(jnp.arange(sp * rows, dtype=jnp.int32) < height, 0.0, MASKED).astype(F32)
    return jnp.concatenate([valid, count[None], held, held[x][None], bias])


def local_moments(rows, field, mask, held):
    (total,) = column_sums(rows, lambda r: (field(r),))
    total = lane_groups(total)
    mean = (total / jnp.maximum(held, 1.0))[:1]

    def centred(r):
        v = (field(r) - mean) * mask(r)
        return (v * v,)

    (square,) = column_sums(rows, centred)
    return stack_rows(total, lane_groups(square))


def joint_moments(members, counts, count):
    mean = members[0][:1]
    for m in members[1:]:
        mean = mean + m[:1]
    mean = mean / count
    square = None
    for m, n in zip(members, counts, strict=True):
        off = m[:1] / jnp.maximum(n, 1.0) - mean
        term = m[1:2] + n * off * off
        square = term if square is None else square + term
    return mean, lax.rsqrt(square / count + EPSILON)


def forward_kernel(
    sp,
    nums,
    image,
    gains,
    scales,
    w1,
    w2,
    resid,
    normed,
    conv_out,
    s1,
    s2,
    stats,
    w1v,
    w2v,
    edge1,
    edge2,
    acc,
    sums,
    ssem,
    hsem,
    wsem,
):
    rows, columns = image.shape[0], image.shape[1]
    swap = Swap(sp, sums, ssem, hsem)
    load1 = pltpu.make_async_copy(w1, w1v, wsem.at[0])
    load2 = pltpu.make_async_copy(w2, w2v, wsem.at[1])
    load1.start()
    load2.start()
    edge1[...] = jnp.zeros_like(edge1)
    edge2[...] = jnp.zeros_like(edge2)
    greet(swap.peers())
    swap.edges_start(0, image.at[0], image.at[rows - 1], edge1)
    count = nums[rows + 2]
    counts = [nums[rows + 3 + i] for i in range(sp)]
    held = nums[rows + 3 + sp]

    def mask(r):
        return nums[r + 1]

    def masked(r):
        return image[r].astype(F32) * mask(r)

    swap.sums_start(0, local_moments(rows, masked, mask, held))
    mean1, inv1 = joint_moments(swap.sums_wait(0), counts, count)
    swap.edges_wait(0, image.at[0], image.at[rows - 1], edge1)
    g1, g2, g3 = gains[0:1], gains[1:2], gains[2:3]

    def first(at, value):
        m = nums[at]
        hidden = (value.astype(F32) * m - mean1) * m * inv1 * g1
        put_shifted(s1, at, hidden * jax.nn.sigmoid(hidden) * m)

    lax.fori_loop(0, rows, lambda r, _: (first(r + 1, image[r]), 0)[1], 0)
    first(0, edge1[0])
    first(rows + 1, edge1[1])
    load1.wait()
    taps(rows, columns, s1, w1v, acc, False)

    def keep(r, _):
        conv_out[r] = acc[r] * mask(r)
        return 0

    lax.fori_loop(0, rows, keep, 0)
    swap.edges_start(1, conv_out.at[0], conv_out.at[rows - 1], edge2)
    swap.sums_start(1, local_moments(rows, lambda r: conv_out[r], mask, held))
    mean2, inv2 = joint_moments(swap.sums_wait(1), counts, count)
    swap.edges_wait(1, conv_out.at[0], conv_out.at[rows - 1], edge2)
    scale, shift = 1.0 + scales[0:1], scales[1:2]

    def second(at, value):
        m = nums[at]
        hidden = (value - mean2) * m * inv2 * g2 * scale + shift
        put_shifted(s2, at, hidden * jax.nn.sigmoid(hidden) * m)

    lax.fori_loop(0, rows, lambda r, _: (second(r + 1, conv_out[r]), 0)[1], 0)
    second(0, edge2[0])
    second(rows + 1, edge2[1])
    load2.wait()
    taps(rows, columns, s2, w2v, acc, False)

    def add(r, _):
        resid[r] = masked(r) + acc[r] * mask(r)
        return 0

    lax.fori_loop(0, rows, add, 0)
    swap.sums_start(2, local_moments(rows, lambda r: resid[r], mask, held))
    mean3, inv3 = joint_moments(swap.sums_wait(2), counts, count)

    def third(r, _):
        normed[r] = ((resid[r] - mean3) * mask(r) * inv3 * g3).astype(BF16)
        return 0

    lax.fori_loop(0, rows, third, 0)
    stats[...] = stack_rows(mean1, inv1, mean2, inv2, mean3, inv3)


def forward(nums, image, gains, scales, w1, w2, sp):
    rows, columns, _ = image.shape
    field = (rows, columns, C)
    shifted = (3, rows + 2, columns, C)
    return pl.pallas_call(
        functools.partial(forward_kernel, sp),
        out_shape=[
            jax.ShapeDtypeStruct(field, F32),
            jax.ShapeDtypeStruct(field, BF16),
            jax.ShapeDtypeStruct(field, F32),
            jax.ShapeDtypeStruct(shifted, BF16),
            jax.ShapeDtypeStruct(shifted, BF16),
            jax.ShapeDtypeStruct((8, C), F32),
        ],
        in_specs=[SMEM, VMEM, VMEM, VMEM, ANY, ANY],
        out_specs=[VMEM] * 6,
        scratch_shapes=[
            pltpu.VMEM(w1.shape, BF16),
            pltpu.VMEM(w2.shape, BF16),
            pltpu.VMEM((2, columns, C), BF16),
            pltpu.VMEM((2, columns, C), F32),
            pltpu.VMEM(field, F32),
            pltpu.VMEM((3, sp, 8, C), F32),
            DMA((2, 3, sp)),
            DMA((2, 2, 2)),
            DMA((2,)),
        ],
        compiler_params=params(1),
        name="forward",
    )(nums, image, gains, scales, w1, w2)


def attention_kernel(
    sp,
    heads,
    nums,
    normed,
    text,
    wq,
    wt,
    wo,
    cot,
    resid,
    output,
    gnorm,
    gq,
    gt,
    go,
    gtext,
    nall,
    gown,
    gall,
    qkv,
    keys,
    values,
    dk,
    dv,
    att,
    attin,
    dqkv,
    gtkv,
    gpart,
    grecv,
    tpart,
    low,
    nsem,
    gsem,
    asem,
    psem,
    tsem,
):
    rows, columns = cot.shape[0], cot.shape[1]
    pixels = rows * columns
    width = heads * HEAD
    total_px = sp * pixels
    me, x = lax.axis_index("fsdp"), lax.axis_index("sp")
    factor = HEAD**-0.5
    greet([(me, (x + d) % sp) for d in range(1, sp)])

    def send(pair, src, dst):
        def copy(d):
            to = (x + d) % sp
            return remote(src(to), dst.at[x], pair.at[0, d], pair.at[1, d], (me, to))

        return [copy(d) for d in range(1, sp)]

    def start(copies):
        for copy in copies:
            copy.start()

    def wait(copies):
        for copy in copies:
            copy.wait()

    moves = send(nsem, lambda to: normed, nall)
    start(moves)

    def lower(r, _):
        low[r] = (cot[r].astype(F32) * nums[r + 1]).astype(BF16)
        return 0

    lax.fori_loop(0, rows, lower, 0)
    low2 = low[...].reshape(pixels, C)
    for k in range(sp):
        gown[k] = lax.dot_general(
            low2,
            wo[k * width : (k + 1) * width, :],
            (((1,), (1,)), ((), ())),
            preferred_element_type=F32,
        ).astype(BF16)
    gmoves = send(gsem, lambda to: gown.at[to], gall)
    start(gmoves)
    gall[x] = gown[x]
    nall[x] = normed[...]
    text_kv = jnp.dot(text[...], wt[...], preferred_element_type=F32).astype(BF16)
    keys[total_px:, :] = text_kv[:, :width]
    values[total_px:, :] = text_kv[:, width:]

    def project(k):
        out = jnp.dot(nall[k], wq[...], preferred_element_type=F32).astype(BF16)
        at = pl.ds(pl.multiple_of(k * pixels, pixels), pixels)
        qkv[at, :] = out
        keys[at, :] = out[:, width : 2 * width]
        values[at, :] = out[:, 2 * width :]

    project(x)
    wait(moves)
    for d in range(1, sp):
        project((x + d) % sp)
    wait(gmoves)

    block = 256
    per = pixels // block
    for h in range(heads):
        lanes = slice(h * HEAD, (h + 1) * HEAD)
        kh, vh = keys[:, lanes], values[:, lanes]
        kt, vt = kh.T, vh.T
        dk[...] = jnp.zeros_like(dk)
        dv[...] = jnp.zeros_like(dv)

        def step(j, _, lanes=lanes, kh=kh, vh=vh, kt=kt, vt=vt):
            at = pl.ds(pl.multiple_of(j * block, block), block)
            inner = pl.ds(pl.multiple_of((j % per) * block, block), block)
            q = qkv[at, lanes]
            g = gall[j // per, inner, lanes]
            s = (
                lax.dot_general(kh, q, (((1,), (1,)), ((), ())), preferred_element_type=F32)
                * factor
            )
            pieces = [
                s[r * columns : (r + 1) * columns] + nums[rows + 4 + sp + r]
                for r in range(sp * rows)
            ]
            s = jnp.concatenate(pieces + [s[total_px:]], axis=0)
            raised = jnp.exp(s - jnp.max(s, axis=0, keepdims=True))
            chances = raised * (1.0 / jnp.sum(raised, axis=0, keepdims=True))
            short = chances.astype(BF16)
            att[j // per, inner, lanes] = jnp.dot(
                vt, short, preferred_element_type=F32
            ).T.astype(BF16)
            slope = lax.dot_general(vh, g, (((1,), (1,)), ((), ())), preferred_element_type=F32)
            mean = jnp.sum(chances * slope, axis=0, keepdims=True)
            grad = (chances * (slope - mean)).astype(BF16)
            dqkv[at, lanes] = (jnp.dot(kt, grad, preferred_element_type=F32) * factor).T.astype(
                BF16
            )
            dk[...] += jnp.dot(grad, q, preferred_element_type=F32)
            dv[...] += jnp.dot(short, g, preferred_element_type=F32)
            return 0

        lax.fori_loop(0, sp * per, step, 0)
        low_k = (dk[...] * factor).astype(BF16)
        low_v = dv[...].astype(BF16)
        dqkv[:, width + h * HEAD : width + (h + 1) * HEAD] = low_k[:total_px]
        dqkv[:, 2 * width + h * HEAD : 2 * width + (h + 1) * HEAD] = low_v[:total_px]
        gtkv[:, h * HEAD : (h + 1) * HEAD] = low_k[total_px:]
        gtkv[:, width + h * HEAD : width + (h + 1) * HEAD] = low_v[total_px:]

    amoves = send(asem, lambda to: att.at[to], attin)
    start(amoves)
    attin[x] = att[x]

    def to_normed(k):
        at = pl.ds(pl.multiple_of(k * pixels, pixels), pixels)
        return lax.dot_general(
            dqkv[at, :], wq[...], (((1,), (1,)), ((), ())), preferred_element_type=F32
        )

    for d in range(1, sp):
        to = (x + d) % sp
        gpart[to] = to_normed(to).astype(BF16)
    pmoves = send(psem, lambda to: gpart.at[to], grecv)
    start(pmoves)
    tpart[x] = lax.dot_general(
        gtkv[...], wt[...], (((1,), (1,)), ((), ())), preferred_element_type=F32
    ).astype(BF16)
    tmoves = send(tsem, lambda to: tpart.at[x], tpart)
    start(tmoves)
    gnorm[...] = to_normed(x)
    wait(amoves)
    joined = jnp.concatenate([attin[k] for k in range(sp)], axis=1)
    branch = jnp.dot(joined, wo[...], preferred_element_type=F32)
    for r in range(rows):
        at = slice(r * columns, (r + 1) * columns)
        output[at, :] = (resid[at, :] + branch[at] * nums[r + 1]).astype(BF16)
    down = (((0,), (0,)), ((), ()))
    go[...] = lax.dot_general(joined, low2, down, preferred_element_type=F32).astype(BF16)
    gq[...] = lax.dot_general(
        nall[...].reshape(total_px, C), dqkv[...], down, preferred_element_type=F32
    ).astype(BF16)
    gt[...] = lax.dot_general(text[...], gtkv[...], down, preferred_element_type=F32).astype(BF16)
    wait(pmoves)
    for d in range(1, sp):
        gnorm[...] += grecv[(x + d) % sp].astype(F32)
    wait(tmoves)
    total = tpart[0].astype(F32)
    for k in range(1, sp):
        total = total + tpart[k].astype(F32)
    gtext[...] = total


def attention(nums, normed, text, wq, wt, wo, cot, resid, sp):
    rows, columns, _ = cot.shape
    pixels = rows * columns
    heads = C // HEAD // sp
    width = heads * HEAD
    tokens, wide = text.shape
    n_keys = sp * pixels + tokens
    return pl.pallas_call(
        functools.partial(attention_kernel, sp, heads),
        out_shape=[
            jax.ShapeDtypeStruct((pixels, C), BF16),
            jax.ShapeDtypeStruct((pixels, C), F32),
            jax.ShapeDtypeStruct(wq.shape, BF16),
            jax.ShapeDtypeStruct(wt.shape, BF16),
            jax.ShapeDtypeStruct(wo.shape, BF16),
            jax.ShapeDtypeStruct(text.shape, F32),
        ],
        in_specs=[SMEM] + [VMEM] * 7,
        out_specs=[VMEM] * 6,
        scratch_shapes=[
            pltpu.VMEM((sp, pixels, C), BF16),
            pltpu.VMEM((sp, pixels, width), BF16),
            pltpu.VMEM((sp, pixels, width), BF16),
            pltpu.VMEM((sp * pixels, 3 * width), BF16),
            pltpu.VMEM((n_keys, width), BF16),
            pltpu.VMEM((n_keys, width), BF16),
            pltpu.VMEM((n_keys, HEAD), F32),
            pltpu.VMEM((n_keys, HEAD), F32),
            pltpu.VMEM((sp, pixels, width), BF16),
            pltpu.VMEM((sp, pixels, width), BF16),
            pltpu.VMEM((sp * pixels, 3 * width), BF16),
            pltpu.VMEM((tokens, 2 * width), BF16),
            pltpu.VMEM((sp, pixels, C), BF16),
            pltpu.VMEM((sp, pixels, C), BF16),
            pltpu.VMEM((sp, tokens, wide), BF16),
            pltpu.VMEM((rows, columns, C), BF16),
        ]
        + [DMA((2, sp))] * 5,
        compiler_params=params(2),
        name="attention",
    )(nums, normed, text, wq, wt, wo, cot, resid)


def backward_kernel(
    fsdp,
    sp,
    nums,
    image,
    gains,
    scales,
    stats,
    resid,
    conv_out,
    s1,
    s2,
    gnorm,
    cot,
    w1,
    w2,
    gw1,
    gw2,
    gimage,
    ggains,
    gscales,
    w1v,
    w2v,
    out1,
    out2,
    p1,
    p2,
    edge1,
    edge2,
    gres,
    acc,
    sums,
    mine,
    every,
    ssem,
    hsem,
    wsem,
    osem,
    tsem,
):
    rows, columns = image.shape[0], image.shape[1]
    pixels = rows * columns
    me, x = lax.axis_index("fsdp"), lax.axis_index("sp")
    swap = Swap(sp, sums, ssem, hsem)
    load1 = pltpu.make_async_copy(w1, w1v, wsem.at[0])
    load2 = pltpu.make_async_copy(w2, w2v, wsem.at[1])
    load2.start()
    load1.start()
    edge1[...] = jnp.zeros_like(edge1)
    edge2[...] = jnp.zeros_like(edge2)
    greet(swap.peers() + [((me + d) % fsdp, x) for d in range(1, fsdp)])
    count = nums[rows + 2]
    g1, g2, g3 = gains[0:1], gains[1:2], gains[2:3]
    mean1, inv1, mean2, inv2, mean3, inv3 = (stats[k : k + 1] for k in range(6))

    def mask(r):
        return nums[r + 1]

    def joint(k):
        members = swap.sums_wait(k)
        total = members[0]
        for m in members[1:]:
            total = total + m
        return total

    def weight_grad(shifted, padded, store, target, sem):
        grad = padded[1, 1 : rows + 1].reshape(pixels, C)

        def body(t, _):
            for dc in range(3):
                lhs = shifted[dc, pl.ds(t, rows)].reshape(pixels, C)
                at = pl.ds(pl.multiple_of((3 * t + dc) * C, C), C)
                store[at, :] = lax.dot_general(
                    lhs, grad, (((0,), (0,)), ((), ())), preferred_element_type=F32
                ).astype(BF16)
            return 0

        lax.fori_loop(0, 3, body, 0)
        pltpu.make_async_copy(store, target, sem).start()

    def hat3(r):
        return (resid[r] - mean3) * mask(r) * inv3

    def from_three(r):
        g = gnorm[r] * mask(r)
        return g, g * hat3(r)

    plain, crossed = column_sums(rows, from_three)
    gain3 = crossed
    swap.sums_start(0, stack_rows(lane_groups(plain * g3), lane_groups(crossed * g3)))
    total = joint(0) / count
    m1, m2 = total[0:1], total[1:2]

    def residual(r, _):
        m = mask(r)
        e = gnorm[r] * m * g3
        value = cot[r].astype(F32) * m + m * inv3 * (e - m1 - hat3(r) * m2)
        gres[r] = value
        put_shifted(p2, r + 1, value * m)
        return 0

    lax.fori_loop(0, rows, residual, 0)
    swap.edges_start(0, p2.at[1, 1], p2.at[1, rows], edge2)
    weight_grad(s2, p2, out2, gw2, osem.at[0])
    swap.edges_wait(0, p2.at[1, 1], p2.at[1, rows], edge2)
    put_shifted(p2, 0, edge2[0].astype(F32))
    put_shifted(p2, rows + 1, edge2[1].astype(F32))
    load2.wait()
    taps(rows, columns, p2, w2v, acc, True)
    scale, shift = 1.0 + scales[0:1], scales[1:2]

    def hat2(r):
        return (conv_out[r] - mean2) * mask(r) * inv2

    def slope(value):
        s = jax.nn.sigmoid(value)
        return s * (1.0 + value * (1.0 - s))

    def from_two(r):
        hat = hat2(r)
        g = acc[r] * mask(r) * slope(hat * g2 * scale + shift)
        acc[r] = g
        return g, g * hat

    plain, crossed = column_sums(rows, from_two)
    gain2 = crossed * scale
    swap.sums_start(
        1,
        stack_rows(
            lane_groups(plain * (scale * g2)),
            lane_groups(crossed * (scale * g2)),
            crossed * g2,
            plain,
        ),
    )
    total = joint(1)
    for k in range(8):
        row = 2 + k // 4
        lanes = slice((k % 4) * 128, (k % 4 + 1) * 128)
        mine[k : k + 1, :] = total[row : row + 1, lanes].astype(BF16).astype(F32)
    copies = tiles_start(fsdp, mine, every, tsem.at[0], tsem.at[1], lambda ref, to: ref)
    every[me] = mine[...]
    m1, m2 = total[0:1] / count, total[1:2] / count

    def middle(r, _):
        m = mask(r)
        value = m * inv2 * (acc[r] * (scale * g2) - m1 - hat2(r) * m2)
        put_shifted(p1, r + 1, value)
        return 0

    lax.fori_loop(0, rows, middle, 0)
    swap.edges_start(1, p1.at[1, 1], p1.at[1, rows], edge1)
    weight_grad(s1, p1, out1, gw1, osem.at[1])
    swap.edges_wait(1, p1.at[1, 1], p1.at[1, rows], edge1)
    put_shifted(p1, 0, edge1[0].astype(F32))
    put_shifted(p1, rows + 1, edge1[1].astype(F32))
    load1.wait()
    taps(rows, columns, p1, w1v, acc, True)

    def hat1(r):
        return (image[r].astype(F32) * mask(r) - mean1) * mask(r) * inv1

    def from_one(r):
        hat = hat1(r)
        g = acc[r] * mask(r) * slope(hat * g1)
        acc[r] = g
        return g, g * hat

    plain, crossed = column_sums(rows, from_one)
    swap.sums_start(2, stack_rows(lane_groups(plain * g1), lane_groups(crossed * g1)))
    ggains[...] = stack_rows(crossed, gain2, gain3)
    total = joint(2) / count
    m1, m2 = total[0:1], total[1:2]

    def final(r, _):
        m = mask(r)
        gimage[r] = (gres[r] + m * inv1 * (acc[r] * g1 - m1 - hat1(r) * m2)) * m
        return 0

    lax.fori_loop(0, rows, final, 0)
    for copy in copies:
        copy.wait()
    gscales[...] = every[...]
    pltpu.make_async_copy(out2, gw2, osem.at[0]).wait()
    pltpu.make_async_copy(out1, gw1, osem.at[1]).wait()


def backward(nums, image, gains, scales, stats, resid, conv_out, s1, s2, gnorm, cot, w1, w2, fsdp, sp):
    rows, columns, _ = image.shape
    field = (rows, columns, C)
    shifted = (3, rows + 2, columns, C)
    return pl.pallas_call(
        functools.partial(backward_kernel, fsdp, sp),
        out_shape=[
            jax.ShapeDtypeStruct(w1.shape, BF16),
            jax.ShapeDtypeStruct(w2.shape, BF16),
            jax.ShapeDtypeStruct(field, F32),
            jax.ShapeDtypeStruct((8, C), F32),
            jax.ShapeDtypeStruct((fsdp, 8, 128), F32),
        ],
        in_specs=[SMEM] + [VMEM] * 10 + [ANY, ANY],
        out_specs=[ANY, ANY, VMEM, VMEM, VMEM],
        scratch_shapes=[
            pltpu.VMEM(w1.shape, BF16),
            pltpu.VMEM(w2.shape, BF16),
            pltpu.VMEM(w1.shape, BF16),
            pltpu.VMEM(w2.shape, BF16),
            pltpu.VMEM(shifted, BF16),
            pltpu.VMEM(shifted, BF16),
            pltpu.VMEM((2, columns, C), BF16),
            pltpu.VMEM((2, columns, C), BF16),
            pltpu.VMEM(field, F32),
            pltpu.VMEM(field, F32),
            pltpu.VMEM((3, sp, 8, C), F32),
            pltpu.VMEM((8, 128), F32),
            pltpu.VMEM((fsdp, 8, 128), F32),
            DMA((2, 3, sp)),
            DMA((2, 2, 2)),
            DMA((2,)),
            DMA((2,)),
            DMA((2, fsdp)),
        ],
        compiler_params=params(3),
        name="backward",
    )(nums, image, gains, scales, stats, resid, conv_out, s1, s2, gnorm, cot, w1, w2)


def per_device(
    image,
    embedding,
    text,
    heights,
    gain_one,
    conv_one,
    emb_proj,
    gain_two,
    conv_two,
    gain_three,
    qkv_proj,
    text_proj,
    out_proj,
    cotangent,
):
    rows, columns = image.shape[1], image.shape[2]
    fsdp, sp = lax.axis_size("fsdp"), lax.axis_size("sp")
    x = lax.axis_index("sp")
    heads = C // HEAD // sp
    width = heads * HEAD
    share = gain_one.shape[0]
    emb_rows = emb_proj.shape[0]
    nums = numbers(heights[0], rows, columns, sp)
    emb_float = embedding.astype(F32)
    emb_act = jax.nn.silu(emb_float).astype(BF16)

    def columns_of(weight, kinds):
        blocks = weight.reshape(weight.shape[0], kinds, sp, width)
        return lax.dynamic_index_in_dim(blocks, x, 2, keepdims=False).reshape(weight.shape[0], -1)

    def lanes(array):
        return jnp.pad(array, [(0, 0)] * (array.ndim - 1) + [(0, 128 - array.shape[-1])])

    gains_row = jnp.concatenate([gain_one, gain_two, gain_three]).astype(F32)
    tiles = jnp.stack(
        [
            lanes(emb_act.astype(F32).reshape(fsdp, emb_rows)),
            jnp.broadcast_to(lanes(gains_row[None]), (fsdp, 128)),
        ],
        axis=1,
    )
    tiles = jnp.pad(tiles, ((0, 0), (0, 6), (0, 0)))
    table = jnp.pad(emb_proj, ((0, 128 - emb_rows), (0, 0)))
    (w1, w2, wq, wt, wo), tiles_in, scales = gather(
        [
            conv_one,
            conv_two,
            columns_of(qkv_proj, 3),
            columns_of(text_proj, 2),
            out_proj,
        ],
        [True, True, False, False, True],
        tiles,
        table,
        fsdp,
        sp,
    )
    scales = scales.reshape(2, C)
    gains = tiles_in[:, 1, : 3 * share].reshape(fsdp, 3, share).transpose(1, 0, 2).reshape(3, C)
    emb_cols = tiles_in[:, 0, :emb_rows].astype(BF16)
    pixels = rows * columns
    resid, normed, conv_out, s1, s2, stats = forward(nums, image[0], gains, scales, w1, w2, sp)
    output, gnorm, gq, gt, go, gtext = attention(
        nums,
        normed.reshape(pixels, C),
        text[0],
        wq,
        wt,
        wo,
        cotangent[0],
        resid.reshape(pixels, C),
        sp,
    )
    gw1, gw2, gimage, ggains, every = backward(
        nums,
        image[0],
        gains,
        scales,
        stats,
        resid,
        conv_out,
        s1,
        s2,
        gnorm.reshape(rows, columns, C),
        cotangent[0],
        w1,
        w2,
        fsdp,
        sp,
    )
    grad_scales = every.reshape(fsdp, 2 * C).astype(BF16)
    grad_emb_proj = lax.dot_general(
        emb_cols, grad_scales, (((0,), (0,)), ((), ())), preferred_element_type=F32
    )
    piece = lax.dot_general(
        grad_scales, emb_proj, (((1,), (1,)), ((), ())), preferred_element_type=F32
    )
    gain_tiles = ggains[:3].reshape(3, fsdp, share).transpose(1, 0, 2).reshape(fsdp, 3 * share)
    tiles = jnp.stack([lanes(piece), lanes(gain_tiles)], axis=1)
    tiles = jnp.pad(tiles, ((0, 0), (0, 6), (0, 0)))
    (r1, r2, rq, rt, ro), tiles_in, small = scatter(
        [gw1, gw2, gq, gt, go], ["add", "add", "join", "join", "add"], tiles, fsdp, sp
    )

    def joined(result, kinds):
        n = result.shape[1]
        return result.reshape(sp, n, kinds, width).transpose(1, 2, 0, 3).reshape(n, kinds * C)

    grad_embedding = tiles_in[:, 0, :emb_rows].reshape(1, -1)
    sigmoid = jax.nn.sigmoid(emb_float)
    grad_embedding = grad_embedding * (sigmoid * (1.0 + emb_float * (1.0 - sigmoid)))
    gain_sums = small[1, : 3 * share].reshape(3, share)
    return (
        output.reshape(1, rows, columns, C),
        gimage[None],
        grad_embedding,
        gtext[None],
        gain_sums[0],
        r1.reshape(-1, C),
        grad_emb_proj,
        gain_sums[1],
        r2.reshape(-1, C),
        gain_sums[2],
        joined(rq, 3),
        joined(rt, 2),
        ro.reshape(-1, C),
    )


def solution(mesh):
    weight = P("fsdp", None)
    gain = P("fsdp")
    field = P("fsdp", "sp", None, None)
    in_specs = (
        field,
        P("fsdp", None),
        P("fsdp", None, None),
        gain,
        gain,
        weight,
        weight,
        gain,
        weight,
        gain,
        weight,
        weight,
        weight,
        field,
    )
    out_specs = (
        field,
        field,
        P("fsdp", None),
        P("fsdp", None, None),
        gain,
        weight,
        weight,
        gain,
        weight,
        gain,
        weight,
        weight,
        weight,
    )
    return jax.shard_map(
        per_device, mesh=mesh, in_specs=in_specs, out_specs=out_specs, check_vma=False
    )
```

```python
import functools

import jax
import jax.numpy as jnp
from jax import lax
from jax.experimental import pallas as pl
from jax.experimental.pallas import tpu as pltpu
from jax.sharding import PartitionSpec as P

C = 512
GROUPS = 32
HEAD = 64
EPSILON = 1e-05
MASKED = -1e30
LIMIT = 60 * 1024 * 1024

F32 = jnp.float32
BF16 = jnp.bfloat16
DMA = pltpu.SemaphoreType.DMA
ANY = pl.BlockSpec(memory_space=pl.ANY)
VMEM = pl.BlockSpec(memory_space=pltpu.VMEM)
SMEM = pl.BlockSpec(memory_space=pltpu.SMEM)


def sizes_of(fsdp, sp):
    lines = sp if fsdp % (2 * sp) == 0 else 1
    return fsdp // (2 * lines), lines, 2


def remote(src, dst, send, recv, device):
    return pltpu.make_async_remote_copy(
        src, dst, send, recv, device_id=device, device_id_type=pl.DeviceIdType.MESH
    )


def greet(peers):
    barrier = pltpu.get_barrier_semaphore()
    for peer in peers:
        pl.semaphore_signal(
            barrier, inc=1, device_id=peer, device_id_type=pl.DeviceIdType.MESH
        )
    pl.semaphore_wait(barrier, len(peers))


def params(cid):
    return pltpu.CompilerParams(
        collective_id=cid, has_side_effects=True, vmem_limit_bytes=LIMIT
    )


def tiles_start(fsdp, source, dest, send, recv, pick):
    me, x = lax.axis_index("fsdp"), lax.axis_index("sp")
    copies = []
    for d in range(1, fsdp):
        to = (me + d) % fsdp
        copy = remote(pick(source, to), dest.at[me], send.at[d], recv.at[d], (to, x))
        copy.start()
        copies.append(copy)
    return copies


def gather_kernel(dims, fsdp, sp, shapes, *refs):
    zs, ys, cs = dims
    count = len(shapes)
    shards, tiles, table = refs[:count], refs[count], refs[count + 1]
    refs = refs[count + 2 :]
    outs, tiles_out, scales_out = refs[:count], refs[count], refs[count + 1]
    refs = refs[count + 2 :]
    bufs, got, part, part_in = refs[:count], refs[count], refs[count + 1], refs[count + 2]
    zsend, zrecv, ysend, yrecv, xsend, xrecv, csend, crecv, local, tsem, psem = refs[count + 3 :]
    me, x = lax.axis_index("fsdp"), lax.axis_index("sp")
    z, y, c = me // (ys * cs), (me // cs) % ys, me % cs

    def dev(zz, yy, cc):
        return ((zz * ys + yy) * cs + cc, x)

    peers = [((me + d) % fsdp, x) for d in range(1, fsdp)]
    peers += [(me, (x + d) % sp) for d in range(1, sp)]
    greet(peers)
    flying = tiles_start(fsdp, tiles, got, tsem.at[0], tsem.at[1], lambda ref, to: ref.at[to])

    def owner(dz, dy):
        return (z - dz + zs) % zs, (y - dy + ys) % ys

    def piece(a):
        return x if shapes[a][0] > 1 else 0

    def zcopy(a, dz):
        h = piece(a)
        return remote(
            shards[a].at[h],
            outs[a].at[z, y, c, h],
            zsend.at[a, dz],
            zrecv.at[a, dz],
            dev((z + dz) % zs, y, c),
        )

    def ycopy(a, dz, dy):
        h = piece(a)
        zz, _ = owner(dz, 0)
        src = shards[a].at[h] if dz == 0 else outs[a].at[zz, y, c, h]
        return remote(
            src,
            outs[a].at[zz, y, c, h],
            ysend.at[a, dz, dy],
            yrecv.at[a, dz, dy],
            dev(z, (y + dy) % ys, c),
        )

    def xcopy(a, dz, dy, dx):
        zz, yy = owner(dz, dy)
        return remote(
            outs[a].at[zz, yy, c, x],
            outs[a].at[zz, yy, c, x],
            xsend.at[a, dz, dy, dx],
            xrecv.at[a, dz, dy, dx],
            (me, (x + dx) % sp),
        )

    def ccopy(a, dz, dy, dx):
        zz, yy = owner(dz, dy)
        if dz == 0 and dy == 0:
            src, dst = shards[a], outs[a].at[zz, yy, c]
        else:
            h = (x - dx + sp) % sp if shapes[a][0] > 1 else 0
            src = dst = outs[a].at[zz, yy, c, h]
        return remote(src, dst, csend.at[a, dz, dy, dx], crecv.at[a, dz, dy, dx], dev(z, y, 1 - c))

    def launch(copy):
        copy.start()
        flying.append(copy)

    def onward(a, dz, dy):
        if shapes[a][0] > 1:
            for dx in range(1, sp):
                launch(xcopy(a, dz, dy, dx))
        launch(ccopy(a, dz, dy, 0))

    for a in range(count):
        for dz in range(1, zs):
            launch(zcopy(a, dz))
        for dy in range(1, ys):
            launch(ycopy(a, 0, dy))
        launch(ccopy(a, 0, 0, 0))
        pltpu.make_async_copy(shards[a], bufs[a], local.at[a]).start()

    got[me] = tiles[me]
    for copy in flying[: fsdp - 1]:
        copy.wait_recv()
    rows = got[:, 0, :].astype(BF16)
    for j in range(8):
        part[:, j, :] = jnp.dot(
            rows, table[:, j * 128 : (j + 1) * 128], preferred_element_type=F32
        )
    part_in[me] = part[me]
    for a in range(count):
        pltpu.make_async_copy(shards[a], bufs[a], local.at[a]).wait()
        pltpu.make_async_copy(bufs[a], outs[a].at[z, y, c], local.at[a]).start()
    second = tiles_start(fsdp, part, part_in, psem.at[0], psem.at[1], lambda ref, to: ref.at[to])
    flying += second

    def over_z(a):
        for dz in range(1, zs):
            zcopy(a, dz).wait_recv()
            for dy in range(1, ys):
                launch(ycopy(a, dz, dy))
            onward(a, dz, 0)

    def over_y(a):
        for dz in range(zs):
            for dy in range(1, ys):
                ycopy(a, dz, dy).wait_recv()
                onward(a, dz, dy)

    def over_x(a):
        if shapes[a][0] > 1:
            for dz in range(zs):
                for dy in range(ys):
                    if dz + dy:
                        for dx in range(1, sp):
                            xcopy(a, dz, dy, dx).wait_recv()
                            launch(ccopy(a, dz, dy, dx))

    for step in range(count + 2):
        if step < count:
            over_z(step)
        if 1 <= step <= count:
            over_y(step - 1)
        if step >= 2:
            over_x(step - 2)
    for copy in second:
        copy.wait_recv()
    total = part_in[0]
    for f in range(1, fsdp):
        total = total + part_in[f]
    scales_out[...] = total
    tiles_out[...] = got[...]
    for a in range(count):
        for dz in range(zs):
            for dy in range(ys):
                many = sp if shapes[a][0] > 1 and dz + dy else 1
                for dx in range(many):
                    ccopy(a, dz, dy, dx).wait_recv()
        pltpu.make_async_copy(bufs[a], outs[a].at[z, y, c], local.at[a]).wait()
    for copy in flying:
        copy.wait_send()


def parts_of(rows, sp):
    return sp if rows % (16 * sp) == 0 else 1


def gather(shards, kinds, tiles, table, fsdp, sp):
    dims = sizes_of(fsdp, sp)
    zs, ys, cs = dims
    count = len(shards)
    split = []
    for shard, kind in zip(shards, kinds, strict=True):
        rows, width = shard.shape
        h = parts_of(rows, sp) if kind else 1
        split.append(shard.reshape(h, rows // h, width))
    shapes = [s.shape for s in split]
    outs = pl.pallas_call(
        functools.partial(gather_kernel, dims, fsdp, sp, shapes),
        out_shape=[jax.ShapeDtypeStruct(dims + s, BF16) for s in shapes]
        + [
            jax.ShapeDtypeStruct((fsdp, 8, 128), F32),
            jax.ShapeDtypeStruct((8, 128), F32),
        ],
        in_specs=[ANY] * count + [VMEM] * 2,
        out_specs=[ANY] * count + [VMEM] * 2,
        scratch_shapes=[pltpu.VMEM(s, BF16) for s in shapes]
        + [pltpu.VMEM((fsdp, 8, 128), F32)] * 3
        + [DMA((count, zs))] * 2
        + [DMA((count, zs, ys))] * 2
        + [DMA((count, zs, ys, sp))] * 4
        + [DMA((count,)), DMA((2, fsdp)), DMA((2, fsdp))],
        compiler_params=params(0),
        name="gather",
    )(*split, tiles, table)
    whole = [
        o.reshape(fsdp * s.shape[0], s.shape[1]) for o, s in zip(outs[:count], shards, strict=True)
    ]
    return whole, outs[count], outs[count + 1]


def add_rows(rows, first, second, put):
    step = 32 if rows % 32 == 0 else (16 if rows % 16 == 0 else 8)

    def body(i, _):
        at = pl.ds(pl.multiple_of(i * step, step), step)
        put(at, first[at, :].astype(F32) + second[at, :].astype(F32))
        return 0

    lax.fori_loop(0, rows // step, body, 0)


class Sums:
    def __init__(self, dims, sp, shapes, modes, grads, own, outs, bufs, sems):
        self.dims, self.sp, self.shapes, self.modes = dims, sp, shapes, modes
        self.grads, self.own, self.outs = grads, own, outs
        self.crecvd, self.xrecvd, self.yrecvd, self.zrecvd, self.last = bufs
        self.csem, self.xsem, self.ysem, self.zsem, self.fsem, self.lsem = sems
        zs, ys, cs = dims
        self.me, self.x = lax.axis_index("fsdp"), lax.axis_index("sp")
        self.z, self.y, self.c = self.me // (ys * cs), (self.me // cs) % ys, self.me % cs
        self.flying = []

    def dev(self, zz, yy, cc):
        return ((zz * self.dims[1] + yy) * self.dims[2] + cc, self.x)

    def launch(self, copy):
        copy.start()
        self.flying.append(copy)

    def order(self):
        zs, ys, _ = self.dims
        return [(dz, dy) for dz in range(zs - 1, -1, -1) for dy in range(ys - 1, -1, -1)]

    def grad(self, a, dz, dy, cc):
        zs, ys, cs = self.dims
        h, rows, _ = self.shapes[a]
        owner = (((self.z + dz) % zs) * ys + (self.y + dy) % ys) * cs + cc
        return self.grads[a].at[pl.ds(pl.multiple_of(owner * (h * rows), 16), h * rows)]

    def part(self, a, dz, dy, k):
        zs, ys, cs = self.dims
        h, rows, _ = self.shapes[a]
        if self.own[a] is not None:
            return self.own[a].at[dz, dy, pl.ds(pl.multiple_of(k * rows, 16), rows)]
        owner = (((self.z + dz) % zs) * ys + (self.y + dy) % ys) * cs + self.c
        return self.grads[a].at[pl.ds(pl.multiple_of((owner * h + k) * rows, 16), rows)]

    def piece(self, a):
        return self.x if self.shapes[a][0] > 1 else 0

    def ccopy(self, a, dz, dy):
        return remote(
            self.grad(a, dz, dy, 1 - self.c),
            self.crecvd[a].at[dz, dy],
            self.csem.at[0, a, dz, dy],
            self.csem.at[1, a, dz, dy],
            self.dev(self.z, self.y, 1 - self.c),
        )

    def mine(self, a, dz, dy):
        return pltpu.make_async_copy(
            self.grad(a, dz, dy, self.c), self.own[a].at[dz, dy], self.lsem.at[a, dz, dy]
        )

    def xcopy(self, a, dz, dy, dx):
        to = (self.x + dx) % self.sp
        return remote(
            self.part(a, dz, dy, to),
            self.xrecvd[a].at[dz, dy, dx - 1],
            self.xsem.at[0, a, dz, dy, dx],
            self.xsem.at[1, a, dz, dy, dx],
            (self.me, to),
        )

    def ycopy(self, a, dz, dy):
        return remote(
            self.part(a, dz, dy, self.piece(a)),
            self.yrecvd[a].at[dz, dy - 1],
            self.ysem.at[0, a, dz, dy],
            self.ysem.at[1, a, dz, dy],
            self.dev(self.z, (self.y + dy) % self.dims[1], self.c),
        )

    def zcopy(self, a, dz):
        return remote(
            self.part(a, dz, 0, self.piece(a)),
            self.zrecvd[a].at[dz - 1],
            self.zsem.at[0, a, dz],
            self.zsem.at[1, a, dz],
            self.dev((self.z + dz) % self.dims[0], self.y, self.c),
        )

    def fcopy(self, a, dx):
        return remote(
            self.last[a].at[self.x],
            self.last[a].at[self.x],
            self.fsem.at[0, a, dx],
            self.fsem.at[1, a, dx],
            (self.me, (self.x + dx) % self.sp),
        )

    def add(self, a, first, second, target):
        def put(at, value):
            target[at, :] = value.astype(BF16)

        add_rows(self.shapes[a][1], first, second, put)

    def start(self, a):
        for dz, dy in self.order():
            self.launch(self.ccopy(a, dz, dy))
            if self.own[a] is not None:
                self.mine(a, dz, dy).start()

    def over_c(self, a):
        h, rows, _ = self.shapes[a]
        for dz, dy in self.order():
            if self.own[a] is not None:
                self.mine(a, dz, dy).wait()
            self.ccopy(a, dz, dy).wait_recv()
            for k in range(h):
                ref = self.part(a, dz, dy, k)
                self.add(a, ref, self.crecvd[a].at[dz, dy, pl.ds(k * rows, rows)], ref)
            if h > 1:
                for dx in range(1, self.sp):
                    self.launch(self.xcopy(a, dz, dy, dx))

    def over_x(self, a, dz):
        for dy in range(self.dims[1] - 1, -1, -1):
            if self.shapes[a][0] > 1:
                ref = self.part(a, dz, dy, self.x)
                for dx in range(1, self.sp):
                    self.xcopy(a, dz, dy, dx).wait_recv()
                    self.add(a, ref, self.xrecvd[a].at[dz, dy, dx - 1], ref)
            if dy:
                self.launch(self.ycopy(a, dz, dy))

    def over_y(self, a, dz):
        ref = self.part(a, dz, 0, self.piece(a))
        for dy in range(1, self.dims[1]):
            self.ycopy(a, dz, dy).wait_recv()
            self.add(a, ref, self.yrecvd[a].at[dz, dy - 1], ref)
        if dz:
            self.launch(self.zcopy(a, dz))

    def over_z(self, a):
        zs = self.dims[0]
        ref = self.part(a, 0, 0, self.piece(a))
        for dz in range(1, zs):
            self.zcopy(a, dz).wait_recv()
            target = self.last[a].at[self.x] if dz == zs - 1 else ref
            self.add(a, ref, self.zrecvd[a].at[dz - 1], target)
        if zs == 1:
            self.last[a][self.x] = ref[...]
        for dx in range(1, self.sp):
            self.launch(self.fcopy(a, dx))

    def all_x(self, a):
        for dz in range(self.dims[0] - 1, -1, -1):
            self.over_x(a, dz)

    def all_y(self, a):
        for dz in range(self.dims[0] - 1, -1, -1):
            self.over_y(a, dz)

    def both(self, a):
        zs = self.dims[0]
        for dz in range(zs - 1, -2, -1):
            if dz >= 0:
                self.over_x(a, dz)
            if dz < zs - 1:
                self.over_y(a, dz + 1)

    def finish(self, a):
        for dx in range(1, self.sp):
            self.fcopy(a, dx).wait_recv()
        if self.modes[a] == "add" and self.shapes[a][0] == 1:
            value = self.last[a][0].astype(F32)
            for k in range(1, self.sp):
                value = value + self.last[a][k].astype(F32)
            self.outs[a][0] = value
        else:
            for k in range(self.sp):
                self.outs[a][k] = self.last[a][k].astype(F32)

    def drain(self):
        for copy in self.flying:
            copy.wait_send()


def lane_groups(values):
    lane = lax.broadcasted_iota(jnp.int32, values.shape, 1)
    step = 1
    while step < C // GROUPS:
        up = pltpu.roll(values, step, 1)
        down = pltpu.roll(values, C - step, 1)
        values = values + jnp.where((lane & step) != 0, up, down)
        step *= 2
    return values


def column_sums(rows, fields):
    probe = jax.eval_shape(lambda: fields(0))

    def body(r, sums):
        return tuple(
            s + jnp.sum(v.reshape(-1, 8, C), axis=0) for s, v in zip(sums, fields(r), strict=True)
        )

    sums = lax.fori_loop(0, rows, body, tuple(jnp.zeros((8, C), F32) for _ in probe))
    return [jnp.broadcast_to(jnp.sum(s, axis=0, keepdims=True), (8, C)) for s in sums]


def stack_rows(*values):
    row = lax.broadcasted_iota(jnp.int32, (8, C), 0)
    out = jnp.zeros((8, C), F32)
    for k, value in enumerate(values):
        out = jnp.where(row == k, value, out)
    return out


class Swap:
    def __init__(self, sp, sums, ssem, hsem):
        self.sp, self.sums, self.ssem, self.hsem = sp, sums, ssem, hsem
        self.me, self.x = lax.axis_index("fsdp"), lax.axis_index("sp")

    def peers(self):
        return [(self.me, (self.x + d) % self.sp) for d in range(1, self.sp)]

    def _sums(self, k, d):
        return remote(
            self.sums.at[k, self.x],
            self.sums.at[k, self.x],
            self.ssem.at[0, k, d],
            self.ssem.at[1, k, d],
            (self.me, (self.x + d) % self.sp),
        )

    def sums_start(self, k, value):
        self.sums[k, self.x] = value
        for d in range(1, self.sp):
            self._sums(k, d).start()

    def sums_wait(self, k):
        for d in range(1, self.sp):
            self._sums(k, d).wait()
        return [self.sums[k, i] for i in range(self.sp)]

    def _up(self, k, src, dst):
        to = (self.x + self.sp - 1) % self.sp
        return remote(src, dst.at[1], self.hsem.at[0, k, 0], self.hsem.at[1, k, 0], (self.me, to))

    def _down(self, k, src, dst):
        to = (self.x + 1) % self.sp
        return remote(src, dst.at[0], self.hsem.at[0, k, 1], self.hsem.at[1, k, 1], (self.me, to))

    def edges_start(self, k, top, bottom, dst):
        @pl.when(self.x > 0)
        def _():
            self._up(k, top, dst).start()

        @pl.when(self.x < self.sp - 1)
        def _():
            self._down(k, bottom, dst).start()

    def edges_wait(self, k, top, bottom, dst):
        @pl.when(self.x > 0)
        def _():
            self._up(k, top, dst).wait_send()
            self._down(k, bottom, dst).wait_recv()

        @pl.when(self.x < self.sp - 1)
        def _():
            self._down(k, bottom, dst).wait_send()
            self._up(k, top, dst).wait_recv()


def put_shifted(dst, at, value):
    columns = value.shape[0]
    col = lax.broadcasted_iota(jnp.int32, value.shape, 0)
    dst[1, at] = value.astype(BF16)
    dst[0, at] = jnp.where(col == 0, 0.0, pltpu.roll(value, 1, 0)).astype(BF16)
    dst[2, at] = jnp.where(col == columns - 1, 0.0, pltpu.roll(value, columns - 1, 0)).astype(BF16)


def taps(rows, columns, shifted, weight, acc, back):
    pixels = rows * columns

    def body(t, _):
        total = None
        for dc in range(3):
            if back:
                lhs = shifted[2 - dc, pl.ds(2 - t, rows)].reshape(pixels, C)
            else:
                lhs = shifted[dc, pl.ds(t, rows)].reshape(pixels, C)
            rhs = weight[pl.ds(pl.multiple_of((3 * t + dc) * C, C), C), :]
            out = lax.dot_general(
                lhs, rhs, (((1,), (1 if back else 0,)), ((), ())), preferred_element_type=F32
            )
            total = out if total is None else total + out
        total = total.reshape(rows, columns, C)

        @pl.when(t == 0)
        def _():
            acc[...] = total

        @pl.when(t > 0)
        def _():
            acc[...] += total

        return 0

    lax.fori_loop(0, 3, body, 0)


def numbers(height, rows, columns, sp):
    x = lax.axis_index("sp")
    ids = x * rows + jnp.arange(-1, rows + 1, dtype=jnp.int32)
    valid = ((ids >= 0) & (ids < height)).astype(F32)
    count = (height * columns * (C // GROUPS)).astype(F32)
    held = jnp.clip(height - rows * jnp.arange(sp, dtype=jnp.int32), 0, rows)
    held = (held * columns * (C // GROUPS)).astype(F32)
    bias = jnp.where(jnp.arange(sp * rows, dtype=jnp.int32) < height, 0.0, MASKED).astype(F32)
    return jnp.concatenate([valid, count[None], held, held[x][None], bias])


def local_moments(rows, field, mask, held):
    (total,) = column_sums(rows, lambda r: (field(r),))
    total = lane_groups(total)
    mean = (total / jnp.maximum(held, 1.0))[:1]

    def centred(r):
        v = (field(r) - mean) * mask(r)
        return (v * v,)

    (square,) = column_sums(rows, centred)
    return stack_rows(total, lane_groups(square))


def joint_moments(members, counts, count):
    mean = members[0][:1]
    for m in members[1:]:
        mean = mean + m[:1]
    mean = mean / count
    square = None
    for m, n in zip(members, counts, strict=True):
        off = m[:1] / jnp.maximum(n, 1.0) - mean
        term = m[1:2] + n * off * off
        square = term if square is None else square + term
    return mean, lax.rsqrt(square / count + EPSILON)


def forward_kernel(
    sp,
    nums,
    image,
    gains,
    scales,
    w1,
    w2,
    resid,
    normed,
    conv_out,
    s1,
    s2,
    stats,
    w1v,
    w2v,
    edge1,
    edge2,
    acc,
    sums,
    ssem,
    hsem,
    wsem,
):
    rows, columns = image.shape[0], image.shape[1]
    swap = Swap(sp, sums, ssem, hsem)
    load1 = pltpu.make_async_copy(w1, w1v, wsem.at[0])
    load2 = pltpu.make_async_copy(w2, w2v, wsem.at[1])
    load1.start()
    load2.start()
    edge1[...] = jnp.zeros_like(edge1)
    edge2[...] = jnp.zeros_like(edge2)
    greet(swap.peers())
    swap.edges_start(0, image.at[0], image.at[rows - 1], edge1)
    count = nums[rows + 2]
    counts = [nums[rows + 3 + i] for i in range(sp)]
    held = nums[rows + 3 + sp]

    def mask(r):
        return nums[r + 1]

    def masked(r):
        return image[r].astype(F32) * mask(r)

    swap.sums_start(0, local_moments(rows, masked, mask, held))
    mean1, inv1 = joint_moments(swap.sums_wait(0), counts, count)
    swap.edges_wait(0, image.at[0], image.at[rows - 1], edge1)
    g1, g2, g3 = gains[0:1], gains[1:2], gains[2:3]

    def first(at, value):
        m = nums[at]
        hidden = (value.astype(F32) * m - mean1) * m * inv1 * g1
        put_shifted(s1, at, hidden * jax.nn.sigmoid(hidden) * m)

    lax.fori_loop(0, rows, lambda r, _: (first(r + 1, image[r]), 0)[1], 0)
    first(0, edge1[0])
    first(rows + 1, edge1[1])
    load1.wait()
    taps(rows, columns, s1, w1v, acc, False)

    def keep(r, _):
        conv_out[r] = acc[r] * mask(r)
        return 0

    lax.fori_loop(0, rows, keep, 0)
    swap.edges_start(1, conv_out.at[0], conv_out.at[rows - 1], edge2)
    swap.sums_start(1, local_moments(rows, lambda r: conv_out[r], mask, held))
    mean2, inv2 = joint_moments(swap.sums_wait(1), counts, count)
    swap.edges_wait(1, conv_out.at[0], conv_out.at[rows - 1], edge2)
    scale, shift = 1.0 + scales[0:1], scales[1:2]

    def second(at, value):
        m = nums[at]
        hidden = (value - mean2) * m * inv2 * g2 * scale + shift
        put_shifted(s2, at, hidden * jax.nn.sigmoid(hidden) * m)

    lax.fori_loop(0, rows, lambda r, _: (second(r + 1, conv_out[r]), 0)[1], 0)
    second(0, edge2[0])
    second(rows + 1, edge2[1])
    load2.wait()
    taps(rows, columns, s2, w2v, acc, False)

    def add(r, _):
        resid[r] = masked(r) + acc[r] * mask(r)
        return 0

    lax.fori_loop(0, rows, add, 0)
    swap.sums_start(2, local_moments(rows, lambda r: resid[r], mask, held))
    mean3, inv3 = joint_moments(swap.sums_wait(2), counts, count)

    def third(r, _):
        normed[r] = ((resid[r] - mean3) * mask(r) * inv3 * g3).astype(BF16)
        return 0

    lax.fori_loop(0, rows, third, 0)
    stats[...] = stack_rows(mean1, inv1, mean2, inv2, mean3, inv3)


def forward(nums, image, gains, scales, w1, w2, sp):
    rows, columns, _ = image.shape
    field = (rows, columns, C)
    shifted = (3, rows + 2, columns, C)
    return pl.pallas_call(
        functools.partial(forward_kernel, sp),
        out_shape=[
            jax.ShapeDtypeStruct(field, F32),
            jax.ShapeDtypeStruct(field, BF16),
            jax.ShapeDtypeStruct(field, F32),
            jax.ShapeDtypeStruct(shifted, BF16),
            jax.ShapeDtypeStruct(shifted, BF16),
            jax.ShapeDtypeStruct((8, C), F32),
        ],
        in_specs=[SMEM, VMEM, VMEM, VMEM, ANY, ANY],
        out_specs=[VMEM] * 6,
        scratch_shapes=[
            pltpu.VMEM(w1.shape, BF16),
            pltpu.VMEM(w2.shape, BF16),
            pltpu.VMEM((2, columns, C), BF16),
            pltpu.VMEM((2, columns, C), F32),
            pltpu.VMEM(field, F32),
            pltpu.VMEM((3, sp, 8, C), F32),
            DMA((2, 3, sp)),
            DMA((2, 2, 2)),
            DMA((2,)),
        ],
        compiler_params=params(1),
        name="forward",
    )(nums, image, gains, scales, w1, w2)


def attention_kernel(
    sp,
    heads,
    nums,
    normed,
    text,
    wq,
    wt,
    wo,
    cot,
    resid,
    output,
    gnorm,
    gq,
    gt,
    go,
    gtext,
    nall,
    gown,
    gall,
    qkv,
    keys,
    values,
    dk,
    dv,
    att,
    attin,
    dqkv,
    gtkv,
    gpart,
    grecv,
    tpart,
    low,
    nsem,
    gsem,
    asem,
    psem,
    tsem,
):
    rows, columns = cot.shape[0], cot.shape[1]
    pixels = rows * columns
    width = heads * HEAD
    total_px = sp * pixels
    me, x = lax.axis_index("fsdp"), lax.axis_index("sp")
    factor = HEAD**-0.5
    greet([(me, (x + d) % sp) for d in range(1, sp)])

    def send(pair, src, dst):
        def copy(d):
            to = (x + d) % sp
            return remote(src(to), dst.at[x], pair.at[0, d], pair.at[1, d], (me, to))

        return [copy(d) for d in range(1, sp)]

    def start(copies):
        for copy in copies:
            copy.start()

    def wait(copies):
        for copy in copies:
            copy.wait()

    moves = send(nsem, lambda to: normed, nall)
    start(moves)

    def lower(r, _):
        low[r] = (cot[r].astype(F32) * nums[r + 1]).astype(BF16)
        return 0

    lax.fori_loop(0, rows, lower, 0)
    low2 = low[...].reshape(pixels, C)
    for k in range(sp):
        gown[k] = lax.dot_general(
            low2,
            wo[k * width : (k + 1) * width, :],
            (((1,), (1,)), ((), ())),
            preferred_element_type=F32,
        ).astype(BF16)
    gmoves = send(gsem, lambda to: gown.at[to], gall)
    start(gmoves)
    gall[x] = gown[x]
    nall[x] = normed[...]
    text_kv = jnp.dot(text[...], wt[...], preferred_element_type=F32).astype(BF16)
    keys[total_px:, :] = text_kv[:, :width]
    values[total_px:, :] = text_kv[:, width:]

    def project(k):
        out = jnp.dot(nall[k], wq[...], preferred_element_type=F32).astype(BF16)
        at = pl.ds(pl.multiple_of(k * pixels, pixels), pixels)
        qkv[at, :] = out
        keys[at, :] = out[:, width : 2 * width]
        values[at, :] = out[:, 2 * width :]

    project(x)
    wait(moves)
    for d in range(1, sp):
        project((x + d) % sp)
    wait(gmoves)

    block = 256
    per = pixels // block
    for h in range(heads):
        lanes = slice(h * HEAD, (h + 1) * HEAD)
        kh, vh = keys[:, lanes], values[:, lanes]
        kt, vt = kh.T, vh.T
        dk[...] = jnp.zeros_like(dk)
        dv[...] = jnp.zeros_like(dv)

        def step(j, _, lanes=lanes, kh=kh, vh=vh, kt=kt, vt=vt):
            at = pl.ds(pl.multiple_of(j * block, block), block)
            inner = pl.ds(pl.multiple_of((j % per) * block, block), block)
            q = qkv[at, lanes]
            g = gall[j // per, inner, lanes]
            s = (
                lax.dot_general(kh, q, (((1,), (1,)), ((), ())), preferred_element_type=F32)
                * factor
            )
            pieces = [
                s[r * columns : (r + 1) * columns] + nums[rows + 4 + sp + r]
                for r in range(sp * rows)
            ]
            s = jnp.concatenate(pieces + [s[total_px:]], axis=0)
            raised = jnp.exp(s - jnp.max(s, axis=0, keepdims=True))
            chances = raised * (1.0 / jnp.sum(raised, axis=0, keepdims=True))
            short = chances.astype(BF16)
            att[j // per, inner, lanes] = jnp.dot(
                vt, short, preferred_element_type=F32
            ).T.astype(BF16)
            slope = lax.dot_general(vh, g, (((1,), (1,)), ((), ())), preferred_element_type=F32)
            mean = jnp.sum(chances * slope, axis=0, keepdims=True)
            grad = (chances * (slope - mean)).astype(BF16)
            dqkv[at, lanes] = (jnp.dot(kt, grad, preferred_element_type=F32) * factor).T.astype(
                BF16
            )
            dk[...] += jnp.dot(grad, q, preferred_element_type=F32)
            dv[...] += jnp.dot(short, g, preferred_element_type=F32)
            return 0

        lax.fori_loop(0, sp * per, step, 0)
        low_k = (dk[...] * factor).astype(BF16)
        low_v = dv[...].astype(BF16)
        dqkv[:, width + h * HEAD : width + (h + 1) * HEAD] = low_k[:total_px]
        dqkv[:, 2 * width + h * HEAD : 2 * width + (h + 1) * HEAD] = low_v[:total_px]
        gtkv[:, h * HEAD : (h + 1) * HEAD] = low_k[total_px:]
        gtkv[:, width + h * HEAD : width + (h + 1) * HEAD] = low_v[total_px:]

    amoves = send(asem, lambda to: att.at[to], attin)
    start(amoves)
    attin[x] = att[x]

    def to_normed(k):
        at = pl.ds(pl.multiple_of(k * pixels, pixels), pixels)
        return lax.dot_general(
            dqkv[at, :], wq[...], (((1,), (1,)), ((), ())), preferred_element_type=F32
        )

    for d in range(1, sp):
        to = (x + d) % sp
        gpart[to] = to_normed(to).astype(BF16)
    pmoves = send(psem, lambda to: gpart.at[to], grecv)
    start(pmoves)
    tpart[x] = lax.dot_general(
        gtkv[...], wt[...], (((1,), (1,)), ((), ())), preferred_element_type=F32
    ).astype(BF16)
    tmoves = send(tsem, lambda to: tpart.at[x], tpart)
    start(tmoves)
    gnorm[...] = to_normed(x)
    wait(amoves)
    joined = jnp.concatenate([attin[k] for k in range(sp)], axis=1)
    branch = jnp.dot(joined, wo[...], preferred_element_type=F32)
    for r in range(rows):
        at = slice(r * columns, (r + 1) * columns)
        output[at, :] = (resid[at, :] + branch[at] * nums[r + 1]).astype(BF16)
    down = (((0,), (0,)), ((), ()))
    go[...] = lax.dot_general(joined, low2, down, preferred_element_type=F32).astype(BF16)
    gq[...] = lax.dot_general(
        nall[...].reshape(total_px, C), dqkv[...], down, preferred_element_type=F32
    ).astype(BF16)
    gt[...] = lax.dot_general(text[...], gtkv[...], down, preferred_element_type=F32).astype(BF16)
    wait(pmoves)
    for d in range(1, sp):
        gnorm[...] += grecv[(x + d) % sp].astype(F32)
    wait(tmoves)
    total = tpart[0].astype(F32)
    for k in range(1, sp):
        total = total + tpart[k].astype(F32)
    gtext[...] = total


def attention(nums, normed, text, wq, wt, wo, cot, resid, sp):
    rows, columns, _ = cot.shape
    pixels = rows * columns
    heads = C // HEAD // sp
    width = heads * HEAD
    tokens, wide = text.shape
    n_keys = sp * pixels + tokens
    return pl.pallas_call(
        functools.partial(attention_kernel, sp, heads),
        out_shape=[
            jax.ShapeDtypeStruct((pixels, C), BF16),
            jax.ShapeDtypeStruct((pixels, C), F32),
            jax.ShapeDtypeStruct(wq.shape, BF16),
            jax.ShapeDtypeStruct(wt.shape, BF16),
            jax.ShapeDtypeStruct(wo.shape, BF16),
            jax.ShapeDtypeStruct(text.shape, F32),
        ],
        in_specs=[SMEM] + [VMEM] * 7,
        out_specs=[VMEM] * 6,
        scratch_shapes=[
            pltpu.VMEM((sp, pixels, C), BF16),
            pltpu.VMEM((sp, pixels, width), BF16),
            pltpu.VMEM((sp, pixels, width), BF16),
            pltpu.VMEM((sp * pixels, 3 * width), BF16),
            pltpu.VMEM((n_keys, width), BF16),
            pltpu.VMEM((n_keys, width), BF16),
            pltpu.VMEM((n_keys, HEAD), F32),
            pltpu.VMEM((n_keys, HEAD), F32),
            pltpu.VMEM((sp, pixels, width), BF16),
            pltpu.VMEM((sp, pixels, width), BF16),
            pltpu.VMEM((sp * pixels, 3 * width), BF16),
            pltpu.VMEM((tokens, 2 * width), BF16),
            pltpu.VMEM((sp, pixels, C), BF16),
            pltpu.VMEM((sp, pixels, C), BF16),
            pltpu.VMEM((sp, tokens, wide), BF16),
            pltpu.VMEM((rows, columns, C), BF16),
        ]
        + [DMA((2, sp))] * 5,
        compiler_params=params(2),
        name="attention",
    )(nums, normed, text, wq, wt, wo, cot, resid)


def backward_kernel(dims, fsdp, sp, shapes, modes, *refs):
    n = len(shapes)
    (nums, image, gains, scales, stats, resid, conv_out, s1, s2, gnorm, cot, table, w1, w2), refs = (
        refs[:14],
        refs[14:],
    )
    attn, refs = refs[: n - 2], refs[n - 2 :]
    outs, gimage, gscales, etiles, gtotal, refs = refs[:n], *refs[n : n + 4], refs[n + 4 :]
    (w1v, w2v, out1, out2, p1, p2, edge1, edge2, gres, acc, sums, mine, every, pieces, got_e), refs = (
        refs[:15],
        refs[15:],
    )
    (ggains, got_g, gsmall), refs = refs[:3], refs[3:]
    own, refs = (None, None) + tuple(refs[: n - 2]), refs[n - 2 :]
    bufs, refs = [refs[i * n : (i + 1) * n] for i in range(5)], refs[5 * n :]
    (ssem, hsem, wsem, tsem, esem, gsem, rsem), sems = refs[:7], refs[7:]
    total_of = Sums(dims, sp, shapes, modes, (out1, out2) + tuple(attn), own, outs, bufs, sems)
    rows, columns = image.shape[0], image.shape[1]
    pixels = rows * columns
    me, x = lax.axis_index("fsdp"), lax.axis_index("sp")
    swap = Swap(sp, sums, ssem, hsem)
    load1 = pltpu.make_async_copy(w1, w1v, wsem.at[0])
    load2 = pltpu.make_async_copy(w2, w2v, wsem.at[1])
    load2.start()
    load1.start()
    edge1[...] = jnp.zeros_like(edge1)
    edge2[...] = jnp.zeros_like(edge2)
    greet(swap.peers() + [((me + d) % fsdp, x) for d in range(1, fsdp)])
    late = list(range(2, n))
    for a in late:
        total_of.start(a)
    count = nums[rows + 2]
    g1, g2, g3 = gains[0:1], gains[1:2], gains[2:3]
    mean1, inv1, mean2, inv2, mean3, inv3 = (stats[k : k + 1] for k in range(6))

    def mask(r):
        return nums[r + 1]

    def joint(k):
        members = swap.sums_wait(k)
        total = members[0]
        for m in members[1:]:
            total = total + m
        return total

    def weight_grad(shifted, padded, store):
        grad = padded[1, 1 : rows + 1].reshape(pixels, C)

        def body(t, _):
            for dc in range(3):
                lhs = shifted[dc, pl.ds(t, rows)].reshape(pixels, C)
                at = pl.ds(pl.multiple_of((3 * t + dc) * C, C), C)
                store[at, :] = lax.dot_general(
                    lhs, grad, (((0,), (0,)), ((), ())), preferred_element_type=F32
                ).astype(BF16)
            return 0

        lax.fori_loop(0, 3, body, 0)

    def hat3(r):
        return (resid[r] - mean3) * mask(r) * inv3

    def from_three(r):
        g = gnorm[r] * mask(r)
        return g, g * hat3(r)

    plain, crossed = column_sums(rows, from_three)
    gain3 = crossed
    swap.sums_start(0, stack_rows(lane_groups(plain * g3), lane_groups(crossed * g3)))
    total = joint(0) / count
    m1, m2 = total[0:1], total[1:2]

    def residual(r, _):
        m = mask(r)
        e = gnorm[r] * m * g3
        value = cot[r].astype(F32) * m + m * inv3 * (e - m1 - hat3(r) * m2)
        gres[r] = value
        put_shifted(p2, r + 1, value * m)
        return 0

    lax.fori_loop(0, rows, residual, 0)
    swap.edges_start(0, p2.at[1, 1], p2.at[1, rows], edge2)
    weight_grad(s2, p2, out2)
    total_of.start(1)
    for a in late:
        total_of.over_c(a)
        if shapes[a][0] == 1:
            total_of.all_x(a)
    swap.edges_wait(0, p2.at[1, 1], p2.at[1, rows], edge2)
    put_shifted(p2, 0, edge2[0].astype(F32))
    put_shifted(p2, rows + 1, edge2[1].astype(F32))
    load2.wait()
    taps(rows, columns, p2, w2v, acc, True)
    total_of.over_c(1)
    for a in late:
        if shapes[a][0] > 1:
            total_of.all_x(a)
    scale, shift = 1.0 + scales[0:1], scales[1:2]

    def hat2(r):
        return (conv_out[r] - mean2) * mask(r) * inv2

    def slope(value):
        s = jax.nn.sigmoid(value)
        return s * (1.0 + value * (1.0 - s))

    def from_two(r):
        hat = hat2(r)
        g = acc[r] * mask(r) * slope(hat * g2 * scale + shift)
        acc[r] = g
        return g, g * hat

    plain, crossed = column_sums(rows, from_two)
    gain2 = crossed * scale
    swap.sums_start(
        1,
        stack_rows(
            lane_groups(plain * (scale * g2)),
            lane_groups(crossed * (scale * g2)),
            crossed * g2,
            plain,
        ),
    )
    total = joint(1)
    for k in range(8):
        row = 2 + k // 4
        lanes = slice((k % 4) * 128, (k % 4 + 1) * 128)
        mine[k : k + 1, :] = total[row : row + 1, lanes].astype(BF16).astype(F32)
    copies = tiles_start(fsdp, mine, every, tsem.at[0], tsem.at[1], lambda ref, to: ref)
    every[me] = mine[...]
    m1, m2 = total[0:1] / count, total[1:2] / count

    def middle(r, _):
        m = mask(r)
        value = m * inv2 * (acc[r] * (scale * g2) - m1 - hat2(r) * m2)
        put_shifted(p1, r + 1, value)
        return 0

    lax.fori_loop(0, rows, middle, 0)
    swap.edges_start(1, p1.at[1, 1], p1.at[1, rows], edge1)
    for a in late:
        total_of.all_y(a)
    weight_grad(s1, p1, out1)
    total_of.start(0)
    swap.edges_wait(1, p1.at[1, 1], p1.at[1, rows], edge1)
    put_shifted(p1, 0, edge1[0].astype(F32))
    put_shifted(p1, rows + 1, edge1[1].astype(F32))
    load1.wait()
    total_of.over_c(0)
    taps(rows, columns, p1, w1v, acc, True)
    total_of.both(1)

    def hat1(r):
        return (image[r].astype(F32) * mask(r) - mean1) * mask(r) * inv1

    def from_one(r):
        hat = hat1(r)
        g = acc[r] * mask(r) * slope(hat * g1)
        acc[r] = g
        return g, g * hat

    plain, crossed = column_sums(rows, from_one)
    swap.sums_start(2, stack_rows(lane_groups(plain * g1), lane_groups(crossed * g1)))
    ggains[...] = stack_rows(crossed, gain2, gain3)
    share = C // fsdp

    def gain_block(ref, to):
        return ref.at[:, pl.ds(pl.multiple_of((to * share) // 128 * 128, 128), 128)]

    gcopies = tiles_start(fsdp, ggains, got_g, gsem.at[0], gsem.at[1], gain_block)
    got_g[me] = ggains[:, pl.ds(pl.multiple_of((me * share) // 128 * 128, 128), 128)]
    for copy in copies:
        copy.wait()
    gscales[...] = every[...]
    piece = None
    for j in range(8):
        term = lax.dot_general(
            every[:, j, :].astype(BF16),
            table[:, j * 128 : (j + 1) * 128],
            (((1,), (1,)), ((), ())),
            preferred_element_type=F32,
        )
        piece = term if piece is None else piece + term
    pieces[...] = jnp.broadcast_to(piece[:, None, :], pieces.shape)
    ecopies = tiles_start(fsdp, pieces, got_e, esem.at[0], esem.at[1], lambda ref, to: ref.at[to])
    got_e[me] = pieces[me]
    total = joint(2) / count
    m1, m2 = total[0:1], total[1:2]

    def final(r, _):
        m = mask(r)
        gimage[r] = (gres[r] + m * inv1 * (acc[r] * g1 - m1 - hat1(r) * m2)) * m
        return 0

    lax.fori_loop(0, rows, final, 0)
    for a in late:
        total_of.over_z(a)
    total_of.over_z(1)
    total_of.both(0)
    for copy in gcopies:
        copy.wait()
    total = got_g[0]
    for f in range(1, fsdp):
        total = total + got_g[f]
    gsmall[x] = total

    def small_copy(d):
        to = (me, (x + d) % sp)
        return remote(gsmall.at[x], gsmall.at[x], rsem.at[0, d], rsem.at[1, d], to)

    for d in range(1, sp):
        small_copy(d).start()
    for a in late:
        total_of.finish(a)
    total_of.finish(1)
    for copy in ecopies:
        copy.wait()
    etiles[...] = got_e[...]
    for d in range(1, sp):
        small_copy(d).wait()
    total = gsmall[0]
    for i in range(1, sp):
        total = total + gsmall[i]
    gtotal[...] = total
    total_of.over_z(0)
    total_of.finish(0)
    total_of.drain()


def backward(
    nums, image, gains, scales, stats, resid, conv_out, s1, s2, gnorm, cot, table, w1, w2, attn, fsdp, sp
):
    rows, columns, _ = image.shape
    field = (rows, columns, C)
    shifted = (3, rows + 2, columns, C)
    dims = sizes_of(fsdp, sp)
    zs, ys, _ = dims
    shapes, outs = [], []
    grads = [w1, w2] + [g for g, _ in attn]
    modes = ["add", "add"] + [m for _, m in attn]
    for grad, mode in zip(grads, modes, strict=True):
        r, width = grad.shape[0] // fsdp, grad.shape[1]
        h = parts_of(r, sp) if mode == "add" else 1
        shapes.append((h, r // h, width))
        copies = 1 if mode == "add" and h == 1 else sp
        outs.append(jax.ShapeDtypeStruct((copies, r // h, width), F32))
    count = len(grads)

    def scratch(*shape):
        return pltpu.VMEM(shape, BF16)

    tile = jax.ShapeDtypeStruct((fsdp, 8, 128), F32)
    tiles = pltpu.VMEM((fsdp, 8, 128), F32)
    return pl.pallas_call(
        functools.partial(backward_kernel, dims, fsdp, sp, shapes, modes),
        out_shape=outs
        + [jax.ShapeDtypeStruct(field, F32), tile, tile, jax.ShapeDtypeStruct((8, 128), F32)],
        in_specs=[SMEM] + [VMEM] * 11 + [ANY] * count,
        out_specs=[VMEM] * (count + 4),
        scratch_shapes=[
            scratch(*w1.shape),
            scratch(*w2.shape),
            scratch(*w1.shape),
            scratch(*w2.shape),
            scratch(*shifted),
            scratch(*shifted),
            scratch(2, columns, C),
            scratch(2, columns, C),
            pltpu.VMEM(field, F32),
            pltpu.VMEM(field, F32),
            pltpu.VMEM((3, sp, 8, C), F32),
            pltpu.VMEM((8, 128), F32),
            tiles,
            tiles,
            tiles,
            pltpu.VMEM((8, C), F32),
            tiles,
            pltpu.VMEM((sp, 8, 128), F32),
        ]
        + [scratch(zs, ys, s[0] * s[1], s[2]) for s in shapes[2:]]
        + [scratch(zs, ys, s[0] * s[1], s[2]) for s in shapes]
        + [
            scratch(zs, ys, sp - 1, *s[1:]) if s[0] > 1 else scratch(1, 1, 1, 16, 128)
            for s in shapes
        ]
        + [scratch(zs, max(ys - 1, 1), *s[1:]) for s in shapes]
        + [scratch(max(zs - 1, 1), *s[1:]) for s in shapes]
        + [scratch(sp, *s[1:]) for s in shapes]
        + [
            DMA((2, 3, sp)),
            DMA((2, 2, 2)),
            DMA((2,)),
            DMA((2, fsdp)),
            DMA((2, fsdp)),
            DMA((2, fsdp)),
            DMA((2, sp)),
            DMA((2, count, zs, ys)),
            DMA((2, count, zs, ys, sp)),
            DMA((2, count, zs, ys)),
            DMA((2, count, zs)),
            DMA((2, count, sp)),
            DMA((count, zs, ys)),
        ],
        compiler_params=params(3),
        name="backward",
    )(
        nums, image, gains, scales, stats, resid, conv_out, s1, s2, gnorm, cot, table, w1, w2,
        *[g for g, _ in attn],
    )


def per_device(
    image,
    embedding,
    text,
    heights,
    gain_one,
    conv_one,
    emb_proj,
    gain_two,
    conv_two,
    gain_three,
    qkv_proj,
    text_proj,
    out_proj,
    cotangent,
):
    rows, columns = image.shape[1], image.shape[2]
    fsdp, sp = lax.axis_size("fsdp"), lax.axis_size("sp")
    x = lax.axis_index("sp")
    heads = C // HEAD // sp
    width = heads * HEAD
    share = gain_one.shape[0]
    emb_rows = emb_proj.shape[0]
    nums = numbers(heights[0], rows, columns, sp)
    emb_float = embedding.astype(F32)
    emb_act = jax.nn.silu(emb_float).astype(BF16)

    def columns_of(weight, kinds):
        blocks = weight.reshape(weight.shape[0], kinds, sp, width)
        return lax.dynamic_index_in_dim(blocks, x, 2, keepdims=False).reshape(weight.shape[0], -1)

    def lanes(array):
        return jnp.pad(array, [(0, 0)] * (array.ndim - 1) + [(0, 128 - array.shape[-1])])

    gains_row = jnp.concatenate([gain_one, gain_two, gain_three]).astype(F32)
    tiles = jnp.stack(
        [
            lanes(emb_act.astype(F32).reshape(fsdp, emb_rows)),
            jnp.broadcast_to(lanes(gains_row[None]), (fsdp, 128)),
        ],
        axis=1,
    )
    tiles = jnp.pad(tiles, ((0, 0), (0, 6), (0, 0)))
    table = jnp.pad(emb_proj, ((0, 128 - emb_rows), (0, 0)))
    (w1, w2, wq, wt, wo), tiles_in, scales = gather(
        [
            conv_one,
            conv_two,
            columns_of(qkv_proj, 3),
            columns_of(text_proj, 2),
            out_proj,
        ],
        [True, True, False, False, True],
        tiles,
        table,
        fsdp,
        sp,
    )
    scales = scales.reshape(2, C)
    gains = tiles_in[:, 1, : 3 * share].reshape(fsdp, 3, share).transpose(1, 0, 2).reshape(3, C)
    emb_cols = tiles_in[:, 0, :emb_rows].astype(BF16)
    pixels = rows * columns
    resid, normed, conv_out, s1, s2, stats = forward(nums, image[0], gains, scales, w1, w2, sp)
    output, gnorm, gq, gt, go, gtext = attention(
        nums,
        normed.reshape(pixels, C),
        text[0],
        wq,
        wt,
        wo,
        cotangent[0],
        resid.reshape(pixels, C),
        sp,
    )
    (r1, r2, rt, rq, ro, gimage, every, tiles_in, small) = backward(
        nums,
        image[0],
        gains,
        scales,
        stats,
        resid,
        conv_out,
        s1,
        s2,
        gnorm.reshape(rows, columns, C),
        cotangent[0],
        table,
        w1,
        w2,
        [(gt, "join"), (gq, "join"), (go, "add")],
        fsdp,
        sp,
    )
    grad_scales = every.reshape(fsdp, 2 * C).astype(BF16)
    grad_emb_proj = lax.dot_general(
        emb_cols, grad_scales, (((0,), (0,)), ((), ())), preferred_element_type=F32
    )

    def joined(result, kinds):
        n = result.shape[1]
        return result.reshape(sp, n, kinds, width).transpose(1, 2, 0, 3).reshape(n, kinds * C)

    grad_embedding = tiles_in[:, 0, :emb_rows].reshape(1, -1)
    sigmoid = jax.nn.sigmoid(emb_float)
    grad_embedding = grad_embedding * (sigmoid * (1.0 + emb_float * (1.0 - sigmoid)))
    lane = (lax.axis_index("fsdp") * share) % 128
    gain_sums = lax.dynamic_slice(small, (0, lane), (3, share))
    return (
        output.reshape(1, rows, columns, C),
        gimage[None],
        grad_embedding,
        gtext[None],
        gain_sums[0],
        r1.reshape(-1, C),
        grad_emb_proj,
        gain_sums[1],
        r2.reshape(-1, C),
        gain_sums[2],
        joined(rq, 3),
        joined(rt, 2),
        ro.reshape(-1, C),
    )


def solution(mesh):
    weight = P("fsdp", None)
    gain = P("fsdp")
    field = P("fsdp", "sp", None, None)
    in_specs = (
        field,
        P("fsdp", None),
        P("fsdp", None, None),
        gain,
        gain,
        weight,
        weight,
        gain,
        weight,
        gain,
        weight,
        weight,
        weight,
        field,
    )
    out_specs = (
        field,
        field,
        P("fsdp", None),
        P("fsdp", None, None),
        gain,
        weight,
        weight,
        gain,
        weight,
        gain,
        weight,
        weight,
        weight,
    )
    return jax.shard_map(
        per_device, mesh=mesh, in_specs=in_specs, out_specs=out_specs, check_vma=False
    )
```

```python
import functools

import jax
import jax.numpy as jnp
from jax import lax
from jax.experimental import pallas as pl
from jax.experimental.pallas import tpu as pltpu
from jax.sharding import PartitionSpec as P

C = 512
GROUPS = 32
HEAD = 64
EPSILON = 1e-05
MASKED = -1e30
LIMIT = 60 * 1024 * 1024

F32 = jnp.float32
BF16 = jnp.bfloat16
DMA = pltpu.SemaphoreType.DMA
ANY = pl.BlockSpec(memory_space=pl.ANY)
VMEM = pl.BlockSpec(memory_space=pltpu.VMEM)
SMEM = pl.BlockSpec(memory_space=pltpu.SMEM)


def sizes_of(fsdp, sp):
    lines = sp if fsdp % (2 * sp) == 0 else 1
    return fsdp // (2 * lines), lines, 2


def remote(src, dst, send, recv, device):
    return pltpu.make_async_remote_copy(
        src, dst, send, recv, device_id=device, device_id_type=pl.DeviceIdType.MESH
    )


def greet(peers):
    barrier = pltpu.get_barrier_semaphore()
    for peer in peers:
        pl.semaphore_signal(
            barrier, inc=1, device_id=peer, device_id_type=pl.DeviceIdType.MESH
        )
    pl.semaphore_wait(barrier, len(peers))


def params(cid):
    return pltpu.CompilerParams(
        collective_id=cid, has_side_effects=True, vmem_limit_bytes=LIMIT
    )


def tiles_start(fsdp, source, dest, send, recv, pick):
    me, x = lax.axis_index("fsdp"), lax.axis_index("sp")
    copies = []
    for d in range(1, fsdp):
        to = (me + d) % fsdp
        copy = remote(pick(source, to), dest.at[me], send.at[d], recv.at[d], (to, x))
        copy.start()
        copies.append(copy)
    return copies


def span(index, rows, size):
    return pl.ds(pl.multiple_of(index * rows, 16 if rows % 16 == 0 else 8), size)


class Gather:
    def __init__(self, dims, sp, shapes, shards, homes, sems):
        self.dims, self.sp, self.shapes, self.shards, self.homes = dims, sp, shapes, shards, homes
        self.zsem, self.ysem, self.xsem, self.csem = sems
        zs, ys, cs = dims
        self.me, self.x = lax.axis_index("fsdp"), lax.axis_index("sp")
        self.z, self.y, self.c = self.me // (ys * cs), (self.me // cs) % ys, self.me % cs
        self.flying = []

    def dev(self, zz, yy, cc):
        return ((zz * self.dims[1] + yy) * self.dims[2] + cc, self.x)

    def launch(self, copy):
        copy.start()
        self.flying.append(copy)

    def owner(self, dz, dy):
        zs, ys, _ = self.dims
        return (self.z - dz + zs) % zs, (self.y - dy + ys) % ys

    def piece(self, a):
        return self.x if self.shapes[a][0] > 1 else 0

    def home(self, a, zz, yy, cc, k=None):
        h, rows, _ = self.shapes[a]
        index = (zz * self.dims[1] + yy) * self.dims[2] + cc
        if k is None:
            return self.homes[a].at[span(index, h * rows, h * rows)]
        return self.homes[a].at[span(index * h + k, rows, rows)]

    def mine(self, a):
        h, rows, _ = self.shapes[a]
        return self.shards[a].at[span(self.piece(a), rows, rows)] if h > 1 else self.shards[a]

    def zcopy(self, a, dz):
        return remote(
            self.mine(a),
            self.home(a, self.z, self.y, self.c, self.piece(a)),
            self.zsem.at[0, a, dz],
            self.zsem.at[1, a, dz],
            self.dev((self.z + dz) % self.dims[0], self.y, self.c),
        )

    def ycopy(self, a, dz, dy):
        zz, _ = self.owner(dz, 0)
        place = self.home(a, zz, self.y, self.c, self.piece(a))
        return remote(
            self.mine(a) if dz == 0 else place,
            place,
            self.ysem.at[0, a, dz, dy],
            self.ysem.at[1, a, dz, dy],
            self.dev(self.z, (self.y + dy) % self.dims[1], self.c),
        )

    def xcopy(self, a, dz, dy, dx):
        zz, yy = self.owner(dz, dy)
        place = self.home(a, zz, yy, self.c, self.x)
        return remote(
            place,
            place,
            self.xsem.at[0, a, dz, dy, dx],
            self.xsem.at[1, a, dz, dy, dx],
            (self.me, (self.x + dx) % self.sp),
        )

    def ccopy(self, a, dz, dy, dx):
        zz, yy = self.owner(dz, dy)
        if dz == 0 and dy == 0:
            src, dst = self.shards[a], self.home(a, zz, yy, self.c)
        else:
            k = (self.x - dx + self.sp) % self.sp if self.shapes[a][0] > 1 else 0
            src = dst = self.home(a, zz, yy, self.c, k)
        return remote(
            src,
            dst,
            self.csem.at[0, a, dz, dy, dx],
            self.csem.at[1, a, dz, dy, dx],
            self.dev(self.z, self.y, 1 - self.c),
        )

    def onward(self, a, dz, dy):
        if self.shapes[a][0] > 1:
            for dx in range(1, self.sp):
                self.launch(self.xcopy(a, dz, dy, dx))
        self.launch(self.ccopy(a, dz, dy, 0))

    def start(self, a):
        for dz in range(1, self.dims[0]):
            self.launch(self.zcopy(a, dz))
        for dy in range(1, self.dims[1]):
            self.launch(self.ycopy(a, 0, dy))
        self.launch(self.ccopy(a, 0, 0, 0))

    def over_z(self, a):
        for dz in range(1, self.dims[0]):
            self.zcopy(a, dz).wait_recv()
            for dy in range(1, self.dims[1]):
                self.launch(self.ycopy(a, dz, dy))
            self.onward(a, dz, 0)

    def over_y(self, a):
        for dz in range(self.dims[0]):
            for dy in range(1, self.dims[1]):
                self.ycopy(a, dz, dy).wait_recv()
                self.onward(a, dz, dy)

    def over_x(self, a):
        if self.shapes[a][0] > 1:
            for dz in range(self.dims[0]):
                for dy in range(self.dims[1]):
                    if dz + dy:
                        for dx in range(1, self.sp):
                            self.xcopy(a, dz, dy, dx).wait_recv()
                            self.launch(self.ccopy(a, dz, dy, dx))

    def finish(self, a):
        for dz in range(self.dims[0]):
            for dy in range(self.dims[1]):
                many = self.sp if self.shapes[a][0] > 1 and dz + dy else 1
                for dx in range(many):
                    self.ccopy(a, dz, dy, dx).wait_recv()

    def drain(self):
        for copy in self.flying:
            copy.wait_send()


def parts_of(rows, sp):
    return sp if rows % (16 * sp) == 0 else 1


def add_rows(rows, first, second, put):
    step = 32 if rows % 32 == 0 else (16 if rows % 16 == 0 else 8)

    def body(i, _):
        at = pl.ds(pl.multiple_of(i * step, step), step)
        put(at, first[at, :].astype(F32) + second[at, :].astype(F32))
        return 0

    lax.fori_loop(0, rows // step, body, 0)


class Sums:
    def __init__(self, dims, sp, shapes, modes, grads, own, outs, bufs, sems):
        self.dims, self.sp, self.shapes, self.modes = dims, sp, shapes, modes
        self.grads, self.own, self.outs = grads, own, outs
        self.crecvd, self.xrecvd, self.yrecvd, self.zrecvd, self.last = bufs
        self.csem, self.xsem, self.ysem, self.zsem, self.fsem, self.lsem = sems
        zs, ys, cs = dims
        self.me, self.x = lax.axis_index("fsdp"), lax.axis_index("sp")
        self.z, self.y, self.c = self.me // (ys * cs), (self.me // cs) % ys, self.me % cs
        self.flying = []

    def dev(self, zz, yy, cc):
        return ((zz * self.dims[1] + yy) * self.dims[2] + cc, self.x)

    def launch(self, copy):
        copy.start()
        self.flying.append(copy)

    def order(self):
        zs, ys, _ = self.dims
        return [(dz, dy) for dz in range(zs - 1, -1, -1) for dy in range(ys - 1, -1, -1)]

    def grad(self, a, dz, dy, cc):
        zs, ys, cs = self.dims
        h, rows, _ = self.shapes[a]
        owner = (((self.z + dz) % zs) * ys + (self.y + dy) % ys) * cs + cc
        return self.grads[a].at[span(owner, h * rows, h * rows)]

    def part(self, a, dz, dy, k):
        zs, ys, cs = self.dims
        h, rows, _ = self.shapes[a]
        if self.own[a] is not None:
            return self.own[a].at[dz, dy, span(k, rows, rows)]
        owner = (((self.z + dz) % zs) * ys + (self.y + dy) % ys) * cs + self.c
        return self.grads[a].at[span(owner * h + k, rows, rows)]

    def piece(self, a):
        return self.x if self.shapes[a][0] > 1 else 0

    def ccopy(self, a, dz, dy):
        return remote(
            self.grad(a, dz, dy, 1 - self.c),
            self.crecvd[a].at[dz, dy],
            self.csem.at[0, a, dz, dy],
            self.csem.at[1, a, dz, dy],
            self.dev(self.z, self.y, 1 - self.c),
        )

    def mine(self, a, dz, dy):
        return pltpu.make_async_copy(
            self.grad(a, dz, dy, self.c), self.own[a].at[dz, dy], self.lsem.at[a, dz, dy]
        )

    def xcopy(self, a, dz, dy, dx):
        to = (self.x + dx) % self.sp
        return remote(
            self.part(a, dz, dy, to),
            self.xrecvd[a].at[dz, dy, dx - 1],
            self.xsem.at[0, a, dz, dy, dx],
            self.xsem.at[1, a, dz, dy, dx],
            (self.me, to),
        )

    def ycopy(self, a, dz, dy):
        return remote(
            self.part(a, dz, dy, self.piece(a)),
            self.yrecvd[a].at[dz, dy - 1],
            self.ysem.at[0, a, dz, dy],
            self.ysem.at[1, a, dz, dy],
            self.dev(self.z, (self.y + dy) % self.dims[1], self.c),
        )

    def zcopy(self, a, dz):
        return remote(
            self.part(a, dz, 0, self.piece(a)),
            self.zrecvd[a].at[dz - 1],
            self.zsem.at[0, a, dz],
            self.zsem.at[1, a, dz],
            self.dev((self.z + dz) % self.dims[0], self.y, self.c),
        )

    def fcopy(self, a, dx):
        return remote(
            self.last[a].at[self.x],
            self.last[a].at[self.x],
            self.fsem.at[0, a, dx],
            self.fsem.at[1, a, dx],
            (self.me, (self.x + dx) % self.sp),
        )

    def add(self, a, first, second, target):
        def put(at, value):
            target[at, :] = value.astype(BF16)

        add_rows(self.shapes[a][1], first, second, put)

    def start(self, a):
        for dz, dy in self.order():
            self.launch(self.ccopy(a, dz, dy))
            if self.own[a] is not None:
                self.mine(a, dz, dy).start()

    def over_c(self, a):
        h, rows, _ = self.shapes[a]
        for dz, dy in self.order():
            if self.own[a] is not None:
                self.mine(a, dz, dy).wait()
            self.ccopy(a, dz, dy).wait_recv()
            for k in range(h):
                ref = self.part(a, dz, dy, k)
                self.add(a, ref, self.crecvd[a].at[dz, dy, pl.ds(k * rows, rows)], ref)
            if h > 1:
                for dx in range(1, self.sp):
                    self.launch(self.xcopy(a, dz, dy, dx))

    def over_x(self, a, dz):
        for dy in range(self.dims[1] - 1, -1, -1):
            if self.shapes[a][0] > 1:
                ref = self.part(a, dz, dy, self.x)
                for dx in range(1, self.sp):
                    self.xcopy(a, dz, dy, dx).wait_recv()
                    self.add(a, ref, self.xrecvd[a].at[dz, dy, dx - 1], ref)
            if dy:
                self.launch(self.ycopy(a, dz, dy))

    def over_y(self, a, dz):
        ref = self.part(a, dz, 0, self.piece(a))
        for dy in range(1, self.dims[1]):
            self.ycopy(a, dz, dy).wait_recv()
            self.add(a, ref, self.yrecvd[a].at[dz, dy - 1], ref)
        if dz:
            self.launch(self.zcopy(a, dz))

    def over_z(self, a):
        zs = self.dims[0]
        ref = self.part(a, 0, 0, self.piece(a))
        for dz in range(1, zs):
            self.zcopy(a, dz).wait_recv()
            target = self.last[a].at[self.x] if dz == zs - 1 else ref
            self.add(a, ref, self.zrecvd[a].at[dz - 1], target)
        if zs == 1:
            self.last[a][self.x] = ref[...]
        for dx in range(1, self.sp):
            self.launch(self.fcopy(a, dx))

    def all_x(self, a):
        for dz in range(self.dims[0] - 1, -1, -1):
            self.over_x(a, dz)

    def all_y(self, a):
        for dz in range(self.dims[0] - 1, -1, -1):
            self.over_y(a, dz)

    def both(self, a):
        zs = self.dims[0]
        for dz in range(zs - 1, -2, -1):
            if dz >= 0:
                self.over_x(a, dz)
            if dz < zs - 1:
                self.over_y(a, dz + 1)

    def finish(self, a):
        for dx in range(1, self.sp):
            self.fcopy(a, dx).wait_recv()
        if self.modes[a] == "add" and self.shapes[a][0] == 1:
            value = self.last[a][0].astype(F32)
            for k in range(1, self.sp):
                value = value + self.last[a][k].astype(F32)
            self.outs[a][0] = value
        else:
            for k in range(self.sp):
                self.outs[a][k] = self.last[a][k].astype(F32)

    def drain(self):
        for copy in self.flying:
            copy.wait_send()


def lane_groups(values):
    lane = lax.broadcasted_iota(jnp.int32, values.shape, 1)
    step = 1
    while step < C // GROUPS:
        up = pltpu.roll(values, step, 1)
        down = pltpu.roll(values, C - step, 1)
        values = values + jnp.where((lane & step) != 0, up, down)
        step *= 2
    return values


def column_sums(rows, fields):
    probe = jax.eval_shape(lambda: fields(0))

    def body(r, sums):
        return tuple(
            s + jnp.sum(v.reshape(-1, 8, C), axis=0) for s, v in zip(sums, fields(r), strict=True)
        )

    sums = lax.fori_loop(0, rows, body, tuple(jnp.zeros((8, C), F32) for _ in probe))
    return [jnp.broadcast_to(jnp.sum(s, axis=0, keepdims=True), (8, C)) for s in sums]


def stack_rows(*values):
    row = lax.broadcasted_iota(jnp.int32, (8, C), 0)
    out = jnp.zeros((8, C), F32)
    for k, value in enumerate(values):
        out = jnp.where(row == k, value, out)
    return out


class Swap:
    def __init__(self, sp, sums, ssem, hsem):
        self.sp, self.sums, self.ssem, self.hsem = sp, sums, ssem, hsem
        self.me, self.x = lax.axis_index("fsdp"), lax.axis_index("sp")

    def peers(self):
        return [(self.me, (self.x + d) % self.sp) for d in range(1, self.sp)]

    def _sums(self, k, d):
        return remote(
            self.sums.at[k, self.x],
            self.sums.at[k, self.x],
            self.ssem.at[0, k, d],
            self.ssem.at[1, k, d],
            (self.me, (self.x + d) % self.sp),
        )

    def sums_start(self, k, value):
        self.sums[k, self.x] = value
        for d in range(1, self.sp):
            self._sums(k, d).start()

    def sums_wait(self, k):
        for d in range(1, self.sp):
            self._sums(k, d).wait()
        return [self.sums[k, i] for i in range(self.sp)]

    def _up(self, k, src, dst):
        to = (self.x + self.sp - 1) % self.sp
        return remote(src, dst.at[1], self.hsem.at[0, k, 0], self.hsem.at[1, k, 0], (self.me, to))

    def _down(self, k, src, dst):
        to = (self.x + 1) % self.sp
        return remote(src, dst.at[0], self.hsem.at[0, k, 1], self.hsem.at[1, k, 1], (self.me, to))

    def edges_start(self, k, top, bottom, dst):
        @pl.when(self.x > 0)
        def _():
            self._up(k, top, dst).start()

        @pl.when(self.x < self.sp - 1)
        def _():
            self._down(k, bottom, dst).start()

    def edges_wait(self, k, top, bottom, dst):
        @pl.when(self.x > 0)
        def _():
            self._up(k, top, dst).wait_send()
            self._down(k, bottom, dst).wait_recv()

        @pl.when(self.x < self.sp - 1)
        def _():
            self._down(k, bottom, dst).wait_send()
            self._up(k, top, dst).wait_recv()


def put_shifted(dst, at, value):
    columns = value.shape[0]
    col = lax.broadcasted_iota(jnp.int32, value.shape, 0)
    dst[1, at] = value.astype(BF16)
    dst[0, at] = jnp.where(col == 0, 0.0, pltpu.roll(value, 1, 0)).astype(BF16)
    dst[2, at] = jnp.where(col == columns - 1, 0.0, pltpu.roll(value, columns - 1, 0)).astype(BF16)


def taps(rows, columns, shifted, weight, acc, back):
    pixels = rows * columns

    def body(t, _):
        total = None
        for dc in range(3):
            if back:
                lhs = shifted[2 - dc, pl.ds(2 - t, rows)].reshape(pixels, C)
            else:
                lhs = shifted[dc, pl.ds(t, rows)].reshape(pixels, C)
            rhs = weight[pl.ds(pl.multiple_of((3 * t + dc) * C, C), C), :]
            out = lax.dot_general(
                lhs, rhs, (((1,), (1 if back else 0,)), ((), ())), preferred_element_type=F32
            )
            total = out if total is None else total + out
        total = total.reshape(rows, columns, C)

        @pl.when(t == 0)
        def _():
            acc[...] = total

        @pl.when(t > 0)
        def _():
            acc[...] += total

        return 0

    lax.fori_loop(0, 3, body, 0)


def numbers(height, rows, columns, sp):
    x = lax.axis_index("sp")
    ids = x * rows + jnp.arange(-1, rows + 1, dtype=jnp.int32)
    valid = ((ids >= 0) & (ids < height)).astype(F32)
    count = (height * columns * (C // GROUPS)).astype(F32)
    held = jnp.clip(height - rows * jnp.arange(sp, dtype=jnp.int32), 0, rows)
    held = (held * columns * (C // GROUPS)).astype(F32)
    bias = jnp.where(jnp.arange(sp * rows, dtype=jnp.int32) < height, 0.0, MASKED).astype(F32)
    return jnp.concatenate([valid, count[None], held, held[x][None], bias])


def local_moments(rows, field, mask, held):
    (total,) = column_sums(rows, lambda r: (field(r),))
    total = lane_groups(total)
    mean = (total / jnp.maximum(held, 1.0))[:1]

    def centred(r):
        v = (field(r) - mean) * mask(r)
        return (v * v,)

    (square,) = column_sums(rows, centred)
    return stack_rows(total, lane_groups(square))


def joint_moments(members, counts, count):
    mean = members[0][:1]
    for m in members[1:]:
        mean = mean + m[:1]
    mean = mean / count
    square = None
    for m, n in zip(members, counts, strict=True):
        off = m[:1] / jnp.maximum(n, 1.0) - mean
        term = m[1:2] + n * off * off
        square = term if square is None else square + term
    return mean, lax.rsqrt(square / count + EPSILON)


def forward_kernel(dims, fsdp, sp, shapes, kinds, *refs):
    n = len(shapes)
    (nums, image, tiles, table), shards, refs = refs[:4], refs[4 : 4 + n], refs[4 + n :]
    (resid, normed, conv_out, s1, s2, stats, gains, scales, got), refs = refs[:9], refs[9:]
    outs, refs = refs[:n], refs[n:]
    (w1v, w2v), bufs, refs = refs[:2], refs[2:n], refs[n:]
    (edge1, edge2, acc, sums, part, part_in), refs = refs[:6], refs[6:]
    (ssem, hsem, wsem, lsem, tsem, psem), sems = refs[:6], refs[6:]
    move = Gather(dims, sp, shapes, shards[:2] + bufs, (w1v, w2v) + outs[2:], sems)
    me, x = move.me, move.x
    late = list(range(2, n))
    rows, columns = image.shape[0], image.shape[1]
    swap = Swap(sp, sums, ssem, hsem)
    homes = [move.home(a, move.z, move.y, move.c) for a in range(n)]
    loads = [pltpu.make_async_copy(shards[a], homes[a], wsem.at[a]) for a in range(2)]
    staged = []
    for a in late:
        width = shapes[a][2] // kinds[a]
        for j in range(kinds[a]):
            if shards[a].shape[1] == shapes[a][2]:
                src = shards[a]
            else:
                start = pl.multiple_of((j * sp + x) * width, 128)
                src = shards[a].at[:, pl.ds(start, width)]
            dst = bufs[a - 2].at[:, j * width : (j + 1) * width]
            staged.append((a, pltpu.make_async_copy(src, dst, lsem.at[a, j])))
    for load in loads + [copy for _, copy in staged]:
        load.start()
    edge1[...] = jnp.zeros_like(edge1)
    edge2[...] = jnp.zeros_like(edge2)
    greet(swap.peers() + [((me + d) % fsdp, x) for d in range(1, fsdp)])
    first_tiles = tiles_start(
        fsdp, tiles, got, tsem.at[0], tsem.at[1], lambda ref, to: ref.at[to]
    )
    got[me] = tiles[me]
    move.start(0)
    swap.edges_start(0, image.at[0], image.at[rows - 1], edge1)
    count = nums[rows + 2]
    counts = [nums[rows + 3 + i] for i in range(sp)]
    held = nums[rows + 3 + sp]

    def mask(r):
        return nums[r + 1]

    def masked(r):
        return image[r].astype(F32) * mask(r)

    swap.sums_start(0, local_moments(rows, masked, mask, held))
    move.start(1)
    for _, copy in staged:
        copy.wait()
    for a in late:
        move.start(a)
    stores = [pltpu.make_async_copy(bufs[a - 2], homes[a], wsem.at[a]) for a in late]
    for copy in stores:
        copy.start()
    for copy in first_tiles:
        copy.wait_recv()
    share = C // fsdp
    many = 128 // share
    for b in range(C // 128):
        block = got[b * many]
        for f in range(b * many + 1, (b + 1) * many):
            block = block + got[f]
        gains[:, b * 128 : (b + 1) * 128] = block
    act = got[:, 0, :].astype(BF16)
    for j in range(8):
        part[:, j, :] = jnp.dot(
            act, table[:, j * 128 : (j + 1) * 128], preferred_element_type=F32
        )
    part_in[me] = part[me]
    second_tiles = tiles_start(
        fsdp, part, part_in, psem.at[0], psem.at[1], lambda ref, to: ref.at[to]
    )
    mean1, inv1 = joint_moments(swap.sums_wait(0), counts, count)
    swap.edges_wait(0, image.at[0], image.at[rows - 1], edge1)
    g1, g2, g3 = gains[1:2], gains[2:3], gains[3:4]

    def first(at, value):
        m = nums[at]
        hidden = (value.astype(F32) * m - mean1) * m * inv1 * g1
        put_shifted(s1, at, hidden * jax.nn.sigmoid(hidden) * m)

    lax.fori_loop(0, rows, lambda r, _: (first(r + 1, image[r]), 0)[1], 0)
    first(0, edge1[0])
    first(rows + 1, edge1[1])
    move.over_z(0)
    move.over_y(0)
    move.over_z(1)
    move.over_x(0)
    loads[0].wait()
    move.finish(0)
    pltpu.make_async_copy(w1v, outs[0], wsem.at[0]).start()
    move.over_y(1)
    taps(rows, columns, s1, w1v, acc, False)

    def keep(r, _):
        conv_out[r] = acc[r] * mask(r)
        return 0

    lax.fori_loop(0, rows, keep, 0)
    swap.edges_start(1, conv_out.at[0], conv_out.at[rows - 1], edge2)
    swap.sums_start(1, local_moments(rows, lambda r: conv_out[r], mask, held))
    mean2, inv2 = joint_moments(swap.sums_wait(1), counts, count)
    swap.edges_wait(1, conv_out.at[0], conv_out.at[rows - 1], edge2)
    for copy in second_tiles:
        copy.wait_recv()
    total = part_in[0]
    for f in range(1, fsdp):
        total = total + part_in[f]
    scales[...] = jnp.zeros_like(scales)
    for j in range(8):
        lanes = slice(j % 4 * 128, (j % 4 + 1) * 128)
        scales[j // 4 : j // 4 + 1, lanes] = total[j : j + 1]
    scale, shift = 1.0 + scales[0:1], scales[1:2]

    def second(at, value):
        m = nums[at]
        hidden = (value - mean2) * m * inv2 * g2 * scale + shift
        put_shifted(s2, at, hidden * jax.nn.sigmoid(hidden) * m)

    lax.fori_loop(0, rows, lambda r, _: (second(r + 1, conv_out[r]), 0)[1], 0)
    second(0, edge2[0])
    second(rows + 1, edge2[1])
    for a in late:
        move.over_z(a)
    move.over_x(1)
    loads[1].wait()
    move.finish(1)
    pltpu.make_async_copy(w2v, outs[1], wsem.at[1]).start()
    taps(rows, columns, s2, w2v, acc, False)
    for a in late:
        move.over_y(a)

    def add(r, _):
        resid[r] = masked(r) + acc[r] * mask(r)
        return 0

    lax.fori_loop(0, rows, add, 0)
    swap.sums_start(2, local_moments(rows, lambda r: resid[r], mask, held))
    mean3, inv3 = joint_moments(swap.sums_wait(2), counts, count)

    def third(r, _):
        normed[r] = ((resid[r] - mean3) * mask(r) * inv3 * g3).astype(BF16)
        return 0

    lax.fori_loop(0, rows, third, 0)
    stats[...] = stack_rows(mean1, inv1, mean2, inv2, mean3, inv3)
    for a in late:
        move.over_x(a)
    for a in late:
        move.finish(a)
        stores[a - 2].wait()
    for copy in first_tiles + second_tiles:
        copy.wait_send()
    move.drain()
    pltpu.make_async_copy(w1v, outs[0], wsem.at[0]).wait()
    pltpu.make_async_copy(w2v, outs[1], wsem.at[1]).wait()


def forward(nums, image, tiles, table, shards, kinds, fsdp, sp):
    rows, columns, _ = image.shape
    field = (rows, columns, C)
    shifted = (3, rows + 2, columns, C)
    dims = sizes_of(fsdp, sp)
    zs, ys, _ = dims
    n = len(shards)
    shapes = []
    for shard, kind in zip(shards, kinds, strict=True):
        r, width = shard.shape
        h = 1 if kind else parts_of(r, sp)
        shapes.append((h, r // h, width // sp if kind else width))
    wholes = [jax.ShapeDtypeStruct((fsdp * h * r, w), BF16) for h, r, w in shapes]
    staged = [pltpu.VMEM((h * r, w), BF16) for h, r, w in shapes[2:]]
    tile = pltpu.VMEM((fsdp, 8, 128), F32)
    return pl.pallas_call(
        functools.partial(forward_kernel, dims, fsdp, sp, shapes, [max(k, 1) for k in kinds]),
        out_shape=[
            jax.ShapeDtypeStruct(field, F32),
            jax.ShapeDtypeStruct(field, BF16),
            jax.ShapeDtypeStruct(field, F32),
            jax.ShapeDtypeStruct(shifted, BF16),
            jax.ShapeDtypeStruct(shifted, BF16),
            jax.ShapeDtypeStruct((8, C), F32),
            jax.ShapeDtypeStruct((8, C), F32),
            jax.ShapeDtypeStruct((8, C), F32),
            jax.ShapeDtypeStruct((fsdp, 8, 128), F32),
        ]
        + wholes,
        in_specs=[SMEM] + [VMEM] * 3 + [ANY] * n,
        out_specs=[VMEM] * 9 + [ANY] * n,
        scratch_shapes=[
            pltpu.VMEM(wholes[0].shape, BF16),
            pltpu.VMEM(wholes[1].shape, BF16),
        ]
        + staged
        + [
            pltpu.VMEM((2, columns, C), BF16),
            pltpu.VMEM((2, columns, C), F32),
            pltpu.VMEM(field, F32),
            pltpu.VMEM((3, sp, 8, C), F32),
            tile,
            tile,
            DMA((2, 3, sp)),
            DMA((2, 2, 2)),
            DMA((n,)),
            DMA((n, 3)),
            DMA((2, fsdp)),
            DMA((2, fsdp)),
            DMA((2, n, zs)),
            DMA((2, n, zs, ys)),
            DMA((2, n, zs, ys, sp)),
            DMA((2, n, zs, ys, sp)),
        ],
        compiler_params=params(1),
        name="forward",
    )(nums, image, tiles, table, *shards)


def attention_kernel(
    sp,
    heads,
    nums,
    normed,
    text,
    wq,
    wt,
    wo,
    cot,
    resid,
    output,
    gnorm,
    gq,
    gt,
    go,
    gtext,
    nall,
    gown,
    gall,
    qkv,
    keys,
    values,
    dk,
    dv,
    att,
    attin,
    dqkv,
    gtkv,
    gpart,
    grecv,
    tpart,
    low,
    nsem,
    gsem,
    asem,
    psem,
    tsem,
):
    rows, columns = cot.shape[0], cot.shape[1]
    pixels = rows * columns
    width = heads * HEAD
    total_px = sp * pixels
    me, x = lax.axis_index("fsdp"), lax.axis_index("sp")
    factor = HEAD**-0.5
    greet([(me, (x + d) % sp) for d in range(1, sp)])

    def send(pair, src, dst):
        def copy(d):
            to = (x + d) % sp
            return remote(src(to), dst.at[x], pair.at[0, d], pair.at[1, d], (me, to))

        return [copy(d) for d in range(1, sp)]

    def start(copies):
        for copy in copies:
            copy.start()

    def wait(copies):
        for copy in copies:
            copy.wait()

    moves = send(nsem, lambda to: normed, nall)
    start(moves)

    def lower(r, _):
        low[r] = (cot[r].astype(F32) * nums[r + 1]).astype(BF16)
        return 0

    lax.fori_loop(0, rows, lower, 0)
    low2 = low[...].reshape(pixels, C)
    for k in range(sp):
        gown[k] = lax.dot_general(
            low2,
            wo[k * width : (k + 1) * width, :],
            (((1,), (1,)), ((), ())),
            preferred_element_type=F32,
        ).astype(BF16)
    gmoves = send(gsem, lambda to: gown.at[to], gall)
    start(gmoves)
    gall[x] = gown[x]
    nall[x] = normed[...]
    text_kv = jnp.dot(text[...], wt[...], preferred_element_type=F32).astype(BF16)
    keys[total_px:, :] = text_kv[:, :width]
    values[total_px:, :] = text_kv[:, width:]

    def project(k):
        out = jnp.dot(nall[k], wq[...], preferred_element_type=F32).astype(BF16)
        at = pl.ds(pl.multiple_of(k * pixels, pixels), pixels)
        qkv[at, :] = out
        keys[at, :] = out[:, width : 2 * width]
        values[at, :] = out[:, 2 * width :]

    project(x)
    wait(moves)
    for d in range(1, sp):
        project((x + d) % sp)
    wait(gmoves)

    block = 256
    per = pixels // block
    for h in range(heads):
        lanes = slice(h * HEAD, (h + 1) * HEAD)
        kh, vh = keys[:, lanes], values[:, lanes]
        kt, vt = kh.T, vh.T
        dk[...] = jnp.zeros_like(dk)
        dv[...] = jnp.zeros_like(dv)

        def step(j, _, lanes=lanes, kh=kh, vh=vh, kt=kt, vt=vt):
            at = pl.ds(pl.multiple_of(j * block, block), block)
            inner = pl.ds(pl.multiple_of((j % per) * block, block), block)
            q = qkv[at, lanes]
            g = gall[j // per, inner, lanes]
            s = (
                lax.dot_general(kh, q, (((1,), (1,)), ((), ())), preferred_element_type=F32)
                * factor
            )
            pieces = [
                s[r * columns : (r + 1) * columns] + nums[rows + 4 + sp + r]
                for r in range(sp * rows)
            ]
            s = jnp.concatenate(pieces + [s[total_px:]], axis=0)
            raised = jnp.exp(s - jnp.max(s, axis=0, keepdims=True))
            chances = raised * (1.0 / jnp.sum(raised, axis=0, keepdims=True))
            short = chances.astype(BF16)
            att[j // per, inner, lanes] = jnp.dot(
                vt, short, preferred_element_type=F32
            ).T.astype(BF16)
            slope = lax.dot_general(vh, g, (((1,), (1,)), ((), ())), preferred_element_type=F32)
            mean = jnp.sum(chances * slope, axis=0, keepdims=True)
            grad = (chances * (slope - mean)).astype(BF16)
            dqkv[at, lanes] = (jnp.dot(kt, grad, preferred_element_type=F32) * factor).T.astype(
                BF16
            )
            dk[...] += jnp.dot(grad, q, preferred_element_type=F32)
            dv[...] += jnp.dot(short, g, preferred_element_type=F32)
            return 0

        lax.fori_loop(0, sp * per, step, 0)
        low_k = (dk[...] * factor).astype(BF16)
        low_v = dv[...].astype(BF16)
        dqkv[:, width + h * HEAD : width + (h + 1) * HEAD] = low_k[:total_px]
        dqkv[:, 2 * width + h * HEAD : 2 * width + (h + 1) * HEAD] = low_v[:total_px]
        gtkv[:, h * HEAD : (h + 1) * HEAD] = low_k[total_px:]
        gtkv[:, width + h * HEAD : width + (h + 1) * HEAD] = low_v[total_px:]

    amoves = send(asem, lambda to: att.at[to], attin)
    start(amoves)
    attin[x] = att[x]

    def to_normed(k):
        at = pl.ds(pl.multiple_of(k * pixels, pixels), pixels)
        return lax.dot_general(
            dqkv[at, :], wq[...], (((1,), (1,)), ((), ())), preferred_element_type=F32
        )

    for d in range(1, sp):
        to = (x + d) % sp
        gpart[to] = to_normed(to).astype(BF16)
    pmoves = send(psem, lambda to: gpart.at[to], grecv)
    start(pmoves)
    tpart[x] = lax.dot_general(
        gtkv[...], wt[...], (((1,), (1,)), ((), ())), preferred_element_type=F32
    ).astype(BF16)
    tmoves = send(tsem, lambda to: tpart.at[x], tpart)
    start(tmoves)
    gnorm[...] = to_normed(x)
    wait(amoves)
    joined = jnp.concatenate([attin[k] for k in range(sp)], axis=1)
    branch = jnp.dot(joined, wo[...], preferred_element_type=F32)
    for r in range(rows):
        at = slice(r * columns, (r + 1) * columns)
        output[at, :] = (resid[at, :] + branch[at] * nums[r + 1]).astype(BF16)
    down = (((0,), (0,)), ((), ()))
    go[...] = lax.dot_general(joined, low2, down, preferred_element_type=F32).astype(BF16)
    gq[...] = lax.dot_general(
        nall[...].reshape(total_px, C), dqkv[...], down, preferred_element_type=F32
    ).astype(BF16)
    gt[...] = lax.dot_general(text[...], gtkv[...], down, preferred_element_type=F32).astype(BF16)
    wait(pmoves)
    for d in range(1, sp):
        gnorm[...] += grecv[(x + d) % sp].astype(F32)
    wait(tmoves)
    total = tpart[0].astype(F32)
    for k in range(1, sp):
        total = total + tpart[k].astype(F32)
    gtext[...] = total


def attention(nums, normed, text, wq, wt, wo, cot, resid, sp):
    rows, columns, _ = cot.shape
    pixels = rows * columns
    heads = C // HEAD // sp
    width = heads * HEAD
    tokens, wide = text.shape
    n_keys = sp * pixels + tokens
    return pl.pallas_call(
        functools.partial(attention_kernel, sp, heads),
        out_shape=[
            jax.ShapeDtypeStruct((pixels, C), BF16),
            jax.ShapeDtypeStruct((pixels, C), F32),
            jax.ShapeDtypeStruct(wq.shape, BF16),
            jax.ShapeDtypeStruct(wt.shape, BF16),
            jax.ShapeDtypeStruct(wo.shape, BF16),
            jax.ShapeDtypeStruct(text.shape, F32),
        ],
        in_specs=[SMEM] + [VMEM] * 7,
        out_specs=[VMEM] * 6,
        scratch_shapes=[
            pltpu.VMEM((sp, pixels, C), BF16),
            pltpu.VMEM((sp, pixels, width), BF16),
            pltpu.VMEM((sp, pixels, width), BF16),
            pltpu.VMEM((sp * pixels, 3 * width), BF16),
            pltpu.VMEM((n_keys, width), BF16),
            pltpu.VMEM((n_keys, width), BF16),
            pltpu.VMEM((n_keys, HEAD), F32),
            pltpu.VMEM((n_keys, HEAD), F32),
            pltpu.VMEM((sp, pixels, width), BF16),
            pltpu.VMEM((sp, pixels, width), BF16),
            pltpu.VMEM((sp * pixels, 3 * width), BF16),
            pltpu.VMEM((tokens, 2 * width), BF16),
            pltpu.VMEM((sp, pixels, C), BF16),
            pltpu.VMEM((sp, pixels, C), BF16),
            pltpu.VMEM((sp, tokens, wide), BF16),
            pltpu.VMEM((rows, columns, C), BF16),
        ]
        + [DMA((2, sp))] * 5,
        compiler_params=params(2),
        name="attention",
    )(nums, normed, text, wq, wt, wo, cot, resid)


def backward_kernel(dims, fsdp, sp, shapes, modes, *refs):
    n = len(shapes)
    (nums, image, gains, scales, stats, resid, conv_out, s1, s2, gnorm, cot, table, w1, w2), refs = (
        refs[:14],
        refs[14:],
    )
    attn, refs = refs[: n - 2], refs[n - 2 :]
    outs, gimage, gscales, etiles, gtotal, refs = refs[:n], *refs[n : n + 4], refs[n + 4 :]
    (w1v, w2v, out1, out2, p1, p2, edge1, edge2, gres, acc, sums, mine, every, pieces, got_e), refs = (
        refs[:15],
        refs[15:],
    )
    (ggains, got_g, gsmall), refs = refs[:3], refs[3:]
    own, refs = (None, None) + tuple(refs[: n - 2]), refs[n - 2 :]
    bufs, refs = [refs[i * n : (i + 1) * n] for i in range(5)], refs[5 * n :]
    (ssem, hsem, wsem, tsem, esem, gsem, rsem), sems = refs[:7], refs[7:]
    total_of = Sums(dims, sp, shapes, modes, (out1, out2) + tuple(attn), own, outs, bufs, sems)
    rows, columns = image.shape[0], image.shape[1]
    pixels = rows * columns
    me, x = lax.axis_index("fsdp"), lax.axis_index("sp")
    swap = Swap(sp, sums, ssem, hsem)
    load1 = pltpu.make_async_copy(w1, w1v, wsem.at[0])
    load2 = pltpu.make_async_copy(w2, w2v, wsem.at[1])
    load2.start()
    load1.start()
    edge1[...] = jnp.zeros_like(edge1)
    edge2[...] = jnp.zeros_like(edge2)
    greet(swap.peers() + [((me + d) % fsdp, x) for d in range(1, fsdp)])
    late = list(range(2, n))
    for a in late:
        total_of.start(a)
    count = nums[rows + 2]
    g1, g2, g3 = gains[1:2], gains[2:3], gains[3:4]
    mean1, inv1, mean2, inv2, mean3, inv3 = (stats[k : k + 1] for k in range(6))

    def mask(r):
        return nums[r + 1]

    def joint(k):
        members = swap.sums_wait(k)
        total = members[0]
        for m in members[1:]:
            total = total + m
        return total

    def weight_grad(shifted, padded, store):
        grad = padded[1, 1 : rows + 1].reshape(pixels, C)

        def body(t, _):
            for dc in range(3):
                lhs = shifted[dc, pl.ds(t, rows)].reshape(pixels, C)
                at = pl.ds(pl.multiple_of((3 * t + dc) * C, C), C)
                store[at, :] = lax.dot_general(
                    lhs, grad, (((0,), (0,)), ((), ())), preferred_element_type=F32
                ).astype(BF16)
            return 0

        lax.fori_loop(0, 3, body, 0)

    def hat3(r):
        return (resid[r] - mean3) * mask(r) * inv3

    def from_three(r):
        g = gnorm[r] * mask(r)
        return g, g * hat3(r)

    plain, crossed = column_sums(rows, from_three)
    gain3 = crossed
    swap.sums_start(0, stack_rows(lane_groups(plain * g3), lane_groups(crossed * g3)))
    total = joint(0) / count
    m1, m2 = total[0:1], total[1:2]

    def residual(r, _):
        m = mask(r)
        e = gnorm[r] * m * g3
        value = cot[r].astype(F32) * m + m * inv3 * (e - m1 - hat3(r) * m2)
        gres[r] = value
        put_shifted(p2, r + 1, value * m)
        return 0

    lax.fori_loop(0, rows, residual, 0)
    swap.edges_start(0, p2.at[1, 1], p2.at[1, rows], edge2)
    weight_grad(s2, p2, out2)
    total_of.start(1)
    for a in late:
        total_of.over_c(a)
        if shapes[a][0] == 1:
            total_of.all_x(a)
    swap.edges_wait(0, p2.at[1, 1], p2.at[1, rows], edge2)
    put_shifted(p2, 0, edge2[0].astype(F32))
    put_shifted(p2, rows + 1, edge2[1].astype(F32))
    load2.wait()
    taps(rows, columns, p2, w2v, acc, True)
    total_of.over_c(1)
    for a in late:
        if shapes[a][0] > 1:
            total_of.all_x(a)
    scale, shift = 1.0 + scales[0:1], scales[1:2]

    def hat2(r):
        return (conv_out[r] - mean2) * mask(r) * inv2

    def slope(value):
        s = jax.nn.sigmoid(value)
        return s * (1.0 + value * (1.0 - s))

    def from_two(r):
        hat = hat2(r)
        g = acc[r] * mask(r) * slope(hat * g2 * scale + shift)
        acc[r] = g
        return g, g * hat

    plain, crossed = column_sums(rows, from_two)
    gain2 = crossed * scale
    swap.sums_start(
        1,
        stack_rows(
            lane_groups(plain * (scale * g2)),
            lane_groups(crossed * (scale * g2)),
            crossed * g2,
            plain,
        ),
    )
    total = joint(1)
    for k in range(8):
        row = 2 + k // 4
        lanes = slice((k % 4) * 128, (k % 4 + 1) * 128)
        mine[k : k + 1, :] = total[row : row + 1, lanes].astype(BF16).astype(F32)
    copies = tiles_start(fsdp, mine, every, tsem.at[0], tsem.at[1], lambda ref, to: ref)
    every[me] = mine[...]
    m1, m2 = total[0:1] / count, total[1:2] / count

    def middle(r, _):
        m = mask(r)
        value = m * inv2 * (acc[r] * (scale * g2) - m1 - hat2(r) * m2)
        put_shifted(p1, r + 1, value)
        return 0

    lax.fori_loop(0, rows, middle, 0)
    swap.edges_start(1, p1.at[1, 1], p1.at[1, rows], edge1)
    for a in late:
        total_of.all_y(a)
    weight_grad(s1, p1, out1)
    total_of.start(0)
    swap.edges_wait(1, p1.at[1, 1], p1.at[1, rows], edge1)
    put_shifted(p1, 0, edge1[0].astype(F32))
    put_shifted(p1, rows + 1, edge1[1].astype(F32))
    load1.wait()
    total_of.over_c(0)
    taps(rows, columns, p1, w1v, acc, True)
    total_of.both(1)

    def hat1(r):
        return (image[r].astype(F32) * mask(r) - mean1) * mask(r) * inv1

    def from_one(r):
        hat = hat1(r)
        g = acc[r] * mask(r) * slope(hat * g1)
        acc[r] = g
        return g, g * hat

    plain, crossed = column_sums(rows, from_one)
    swap.sums_start(2, stack_rows(lane_groups(plain * g1), lane_groups(crossed * g1)))
    ggains[...] = stack_rows(crossed, gain2, gain3)
    share = C // fsdp

    def gain_block(ref, to):
        return ref.at[:, pl.ds(pl.multiple_of((to * share) // 128 * 128, 128), 128)]

    gcopies = tiles_start(fsdp, ggains, got_g, gsem.at[0], gsem.at[1], gain_block)
    got_g[me] = ggains[:, pl.ds(pl.multiple_of((me * share) // 128 * 128, 128), 128)]
    for copy in copies:
        copy.wait()
    gscales[...] = every[...]
    piece = None
    for j in range(8):
        term = lax.dot_general(
            every[:, j, :].astype(BF16),
            table[:, j * 128 : (j + 1) * 128],
            (((1,), (1,)), ((), ())),
            preferred_element_type=F32,
        )
        piece = term if piece is None else piece + term
    pieces[...] = jnp.broadcast_to(piece[:, None, :], pieces.shape)
    ecopies = tiles_start(fsdp, pieces, got_e, esem.at[0], esem.at[1], lambda ref, to: ref.at[to])
    got_e[me] = pieces[me]
    total = joint(2) / count
    m1, m2 = total[0:1], total[1:2]

    def final(r, _):
        m = mask(r)
        gimage[r] = (gres[r] + m * inv1 * (acc[r] * g1 - m1 - hat1(r) * m2)) * m
        return 0

    lax.fori_loop(0, rows, final, 0)
    for a in late:
        total_of.over_z(a)
    total_of.over_z(1)
    total_of.both(0)
    for copy in gcopies:
        copy.wait()
    total = got_g[0]
    for f in range(1, fsdp):
        total = total + got_g[f]
    gsmall[x] = total

    def small_copy(d):
        to = (me, (x + d) % sp)
        return remote(gsmall.at[x], gsmall.at[x], rsem.at[0, d], rsem.at[1, d], to)

    for d in range(1, sp):
        small_copy(d).start()
    for a in late:
        total_of.finish(a)
    total_of.finish(1)
    for copy in ecopies:
        copy.wait()
    etiles[...] = got_e[...]
    for d in range(1, sp):
        small_copy(d).wait()
    total = gsmall[0]
    for i in range(1, sp):
        total = total + gsmall[i]
    gtotal[...] = total
    total_of.over_z(0)
    total_of.finish(0)
    total_of.drain()


def backward(
    nums, image, gains, scales, stats, resid, conv_out, s1, s2, gnorm, cot, table, w1, w2, attn, fsdp, sp
):
    rows, columns, _ = image.shape
    field = (rows, columns, C)
    shifted = (3, rows + 2, columns, C)
    dims = sizes_of(fsdp, sp)
    zs, ys, _ = dims
    shapes, outs = [], []
    grads = [w1, w2] + [g for g, _ in attn]
    modes = ["add", "add"] + [m for _, m in attn]
    for grad, mode in zip(grads, modes, strict=True):
        r, width = grad.shape[0] // fsdp, grad.shape[1]
        h = parts_of(r, sp) if mode == "add" else 1
        shapes.append((h, r // h, width))
        copies = 1 if mode == "add" and h == 1 else sp
        outs.append(jax.ShapeDtypeStruct((copies, r // h, width), F32))
    count = len(grads)

    def scratch(*shape):
        return pltpu.VMEM(shape, BF16)

    tile = jax.ShapeDtypeStruct((fsdp, 8, 128), F32)
    tiles = pltpu.VMEM((fsdp, 8, 128), F32)
    return pl.pallas_call(
        functools.partial(backward_kernel, dims, fsdp, sp, shapes, modes),
        out_shape=outs
        + [jax.ShapeDtypeStruct(field, F32), tile, tile, jax.ShapeDtypeStruct((8, 128), F32)],
        in_specs=[SMEM] + [VMEM] * 11 + [ANY] * count,
        out_specs=[VMEM] * (count + 4),
        scratch_shapes=[
            scratch(*w1.shape),
            scratch(*w2.shape),
            scratch(*w1.shape),
            scratch(*w2.shape),
            scratch(*shifted),
            scratch(*shifted),
            scratch(2, columns, C),
            scratch(2, columns, C),
            pltpu.VMEM(field, F32),
            pltpu.VMEM(field, F32),
            pltpu.VMEM((3, sp, 8, C), F32),
            pltpu.VMEM((8, 128), F32),
            tiles,
            tiles,
            tiles,
            pltpu.VMEM((8, C), F32),
            tiles,
            pltpu.VMEM((sp, 8, 128), F32),
        ]
        + [scratch(zs, ys, s[0] * s[1], s[2]) for s in shapes[2:]]
        + [scratch(zs, ys, s[0] * s[1], s[2]) for s in shapes]
        + [
            scratch(zs, ys, sp - 1, *s[1:]) if s[0] > 1 else scratch(1, 1, 1, 16, 128)
            for s in shapes
        ]
        + [scratch(zs, max(ys - 1, 1), *s[1:]) for s in shapes]
        + [scratch(max(zs - 1, 1), *s[1:]) for s in shapes]
        + [scratch(sp, *s[1:]) for s in shapes]
        + [
            DMA((2, 3, sp)),
            DMA((2, 2, 2)),
            DMA((2,)),
            DMA((2, fsdp)),
            DMA((2, fsdp)),
            DMA((2, fsdp)),
            DMA((2, sp)),
            DMA((2, count, zs, ys)),
            DMA((2, count, zs, ys, sp)),
            DMA((2, count, zs, ys)),
            DMA((2, count, zs)),
            DMA((2, count, sp)),
            DMA((count, zs, ys)),
        ],
        compiler_params=params(3),
        name="backward",
    )(
        nums, image, gains, scales, stats, resid, conv_out, s1, s2, gnorm, cot, table, w1, w2,
        *[g for g, _ in attn],
    )


def per_device(
    image,
    embedding,
    text,
    heights,
    gain_one,
    conv_one,
    emb_proj,
    gain_two,
    conv_two,
    gain_three,
    qkv_proj,
    text_proj,
    out_proj,
    cotangent,
):
    rows, columns = image.shape[1], image.shape[2]
    fsdp, sp = lax.axis_size("fsdp"), lax.axis_size("sp")
    heads = C // HEAD // sp
    width = heads * HEAD
    share = gain_one.shape[0]
    emb_rows = emb_proj.shape[0]
    nums = numbers(heights[0], rows, columns, sp)
    emb_float = embedding.astype(F32)
    emb_act = jax.nn.silu(emb_float).astype(BF16)

    def lanes(array):
        return jnp.pad(array, [(0, 0)] * (array.ndim - 1) + [(0, 128 - array.shape[-1])])

    many = 128 // share
    place = lax.broadcasted_iota(jnp.int32, (3, 128), 1) // share == lax.axis_index("fsdp") % many
    gain_rows = jnp.stack([gain_one, gain_two, gain_three]).astype(F32)
    gain_rows = jnp.where(place, jnp.tile(gain_rows, (1, many)), 0.0)
    tiles = jnp.concatenate(
        [
            lanes(emb_act.astype(F32).reshape(fsdp, 1, emb_rows)),
            jnp.broadcast_to(gain_rows[None], (fsdp, 3, 128)),
            jnp.zeros((fsdp, 4, 128), F32),
        ],
        axis=1,
    )
    table = jnp.pad(emb_proj, ((0, 128 - emb_rows), (0, 0)))
    resid, normed, conv_out, s1, s2, stats, gains, scales, tiles_in, w1, w2, wt, wq, wo = forward(
        nums,
        image[0],
        tiles,
        table,
        [conv_one, conv_two, text_proj, qkv_proj, out_proj],
        [0, 0, 2, 3, 0],
        fsdp,
        sp,
    )
    emb_cols = tiles_in[:, 0, :emb_rows].astype(BF16)
    pixels = rows * columns
    output, gnorm, gq, gt, go, gtext = attention(
        nums,
        normed.reshape(pixels, C),
        text[0],
        wq,
        wt,
        wo,
        cotangent[0],
        resid.reshape(pixels, C),
        sp,
    )
    (r1, r2, rt, rq, ro, gimage, every, tiles_in, small) = backward(
        nums,
        image[0],
        gains,
        scales,
        stats,
        resid,
        conv_out,
        s1,
        s2,
        gnorm.reshape(rows, columns, C),
        cotangent[0],
        table,
        w1,
        w2,
        [(gt, "join"), (gq, "join"), (go, "add")],
        fsdp,
        sp,
    )
    grad_scales = every.reshape(fsdp, 2 * C).astype(BF16)
    grad_emb_proj = lax.dot_general(
        emb_cols, grad_scales, (((0,), (0,)), ((), ())), preferred_element_type=F32
    )

    def joined(result, kinds):
        n = result.shape[1]
        return result.reshape(sp, n, kinds, width).transpose(1, 2, 0, 3).reshape(n, kinds * C)

    grad_embedding = tiles_in[:, 0, :emb_rows].reshape(1, -1)
    sigmoid = jax.nn.sigmoid(emb_float)
    grad_embedding = grad_embedding * (sigmoid * (1.0 + emb_float * (1.0 - sigmoid)))
    lane = (lax.axis_index("fsdp") * share) % 128
    gain_sums = lax.dynamic_slice(small, (0, lane), (3, share))
    return (
        output.reshape(1, rows, columns, C),
        gimage[None],
        grad_embedding,
        gtext[None],
        gain_sums[0],
        r1.reshape(-1, C),
        grad_emb_proj,
        gain_sums[1],
        r2.reshape(-1, C),
        gain_sums[2],
        joined(rq, 3),
        joined(rt, 2),
        ro.reshape(-1, C),
    )


def solution(mesh):
    weight = P("fsdp", None)
    gain = P("fsdp")
    field = P("fsdp", "sp", None, None)
    in_specs = (
        field,
        P("fsdp", None),
        P("fsdp", None, None),
        gain,
        gain,
        weight,
        weight,
        gain,
        weight,
        gain,
        weight,
        weight,
        weight,
        field,
    )
    out_specs = (
        field,
        field,
        P("fsdp", None),
        P("fsdp", None, None),
        gain,
        weight,
        weight,
        gain,
        weight,
        gain,
        weight,
        weight,
        weight,
    )
    return jax.shard_map(
        per_device, mesh=mesh, in_specs=in_specs, out_specs=out_specs, check_vma=False
    )
```

```python
import functools

import jax
import jax.numpy as jnp
from jax import lax
from jax.experimental import pallas as pl
from jax.experimental.pallas import tpu as pltpu
from jax.sharding import PartitionSpec as P

C = 512
GROUPS = 32
HEAD = 64
EPSILON = 1e-05
MASKED = -1e30
LIMIT = 60 * 1024 * 1024

F32 = jnp.float32
BF16 = jnp.bfloat16
DMA = pltpu.SemaphoreType.DMA
ANY = pl.BlockSpec(memory_space=pl.ANY)
VMEM = pl.BlockSpec(memory_space=pltpu.VMEM)
SMEM = pl.BlockSpec(memory_space=pltpu.SMEM)


def sizes_of(fsdp, sp):
    lines = sp if fsdp % (2 * sp) == 0 else 1
    return fsdp // (2 * lines), lines, 2


def remote(src, dst, send, recv, device):
    return pltpu.make_async_remote_copy(
        src, dst, send, recv, device_id=device, device_id_type=pl.DeviceIdType.MESH
    )


def greet(peers):
    barrier = pltpu.get_barrier_semaphore()
    for peer in peers:
        pl.semaphore_signal(
            barrier, inc=1, device_id=peer, device_id_type=pl.DeviceIdType.MESH
        )
    pl.semaphore_wait(barrier, len(peers))


def params(cid):
    return pltpu.CompilerParams(
        collective_id=cid, has_side_effects=True, vmem_limit_bytes=LIMIT
    )


def tiles_start(fsdp, source, dest, send, recv, pick):
    me, x = lax.axis_index("fsdp"), lax.axis_index("sp")
    copies = []
    for d in range(1, fsdp):
        to = (me + d) % fsdp
        copy = remote(pick(source, to), dest.at[me], send.at[d], recv.at[d], (to, x))
        copy.start()
        copies.append(copy)
    return copies


def span(index, rows, size):
    return pl.ds(pl.multiple_of(index * rows, 16 if rows % 16 == 0 else 8), size)


def aligned(index, *steps):
    if isinstance(index, int):
        return index
    return pl.multiple_of(index, 16 if all(step % 16 == 0 for step in steps) else 8)


class Gather:
    def __init__(self, dims, sp, entries, sems):
        self.dims, self.sp, self.entries = dims, sp, entries
        self.zsem, self.ysem, self.xsem, self.csem = sems
        zs, ys, cs = dims
        self.me, self.x = lax.axis_index("fsdp"), lax.axis_index("sp")
        self.z, self.y, self.c = self.me // (ys * cs), (self.me // cs) % ys, self.me % cs
        self.flying = []

    def dev(self, zz, yy, cc):
        return ((zz * self.dims[1] + yy) * self.dims[2] + cc, self.x)

    def launch(self, make, *args):
        make(*args).start()
        self.flying.append((make, args))

    def owner(self, dz, dy):
        zs, ys, _ = self.dims
        return (self.z - dz + zs) % zs, (self.y - dy + ys) % ys

    def split(self, a):
        return self.entries[a][2] > 1

    def piece(self, a):
        return self.x if self.split(a) else 0

    def home(self, a, zz, yy, cc, k=None):
        _, whole, h, rows, offset, stride = self.entries[a]
        index = ((zz * self.dims[1] + yy) * self.dims[2] + cc) * stride + offset
        if k is None:
            return whole.at[pl.ds(aligned(index, stride, offset), h * rows)]
        return whole.at[pl.ds(aligned(index + k * rows, stride, offset, rows), rows)]

    def mine(self, a):
        shard, _, h, rows, offset, stride = self.entries[a]
        if h * rows == stride and h == 1:
            return shard
        return shard.at[pl.ds(aligned(offset + self.piece(a) * rows, offset, rows), rows)]

    def own(self, a):
        shard, _, h, rows, offset, stride = self.entries[a]
        return shard if h * rows == stride else shard.at[offset : offset + h * rows]

    def zcopy(self, a, dz):
        return remote(
            self.mine(a),
            self.home(a, self.z, self.y, self.c, self.piece(a)),
            self.zsem.at[0, a, dz],
            self.zsem.at[1, a, dz],
            self.dev((self.z + dz) % self.dims[0], self.y, self.c),
        )

    def ycopy(self, a, dz, dy):
        zz, _ = self.owner(dz, 0)
        place = self.home(a, zz, self.y, self.c, self.piece(a))
        return remote(
            self.mine(a) if dz == 0 else place,
            place,
            self.ysem.at[0, a, dz, dy],
            self.ysem.at[1, a, dz, dy],
            self.dev(self.z, (self.y + dy) % self.dims[1], self.c),
        )

    def xcopy(self, a, dz, dy, dx):
        zz, yy = self.owner(dz, dy)
        place = self.home(a, zz, yy, self.c, self.x)
        return remote(
            place,
            place,
            self.xsem.at[0, a, dz, dy, dx],
            self.xsem.at[1, a, dz, dy, dx],
            (self.me, (self.x + dx) % self.sp),
        )

    def ccopy(self, a, dz, dy, dx):
        zz, yy = self.owner(dz, dy)
        if dz == 0 and dy == 0:
            src, dst = self.own(a), self.home(a, zz, yy, self.c)
        else:
            k = (self.x - dx + self.sp) % self.sp if self.split(a) else 0
            src = dst = self.home(a, zz, yy, self.c, k)
        return remote(
            src,
            dst,
            self.csem.at[0, a, dz, dy, dx],
            self.csem.at[1, a, dz, dy, dx],
            self.dev(self.z, self.y, 1 - self.c),
        )

    def onward(self, a, dz, dy):
        if self.split(a):
            for dx in range(1, self.sp):
                self.launch(self.xcopy, a, dz, dy, dx)
        self.launch(self.ccopy, a, dz, dy, 0)

    def start_z(self, a):
        for dz in range(1, self.dims[0]):
            self.launch(self.zcopy, a, dz)

    def start_y(self, a):
        for dy in range(1, self.dims[1]):
            self.launch(self.ycopy, a, 0, dy)
        self.launch(self.ccopy, a, 0, 0, 0)

    def from_z(self, a, dz):
        self.zcopy(a, dz).wait_recv()
        for dy in range(1, self.dims[1]):
            self.launch(self.ycopy, a, dz, dy)
        self.onward(a, dz, 0)

    def from_y(self, a, dz):
        for dy in range(1, self.dims[1]):
            self.ycopy(a, dz, dy).wait_recv()
            self.onward(a, dz, dy)

    def relay(self, a, dz):
        if 0 < dz < self.dims[0]:
            self.from_z(a, dz)
        if 0 < dz <= self.dims[0]:
            self.from_y(a, dz - 1)

    def over_x(self, a):
        if self.split(a):
            for dz in range(self.dims[0]):
                for dy in range(self.dims[1]):
                    if dz + dy:
                        for dx in range(1, self.sp):
                            self.xcopy(a, dz, dy, dx).wait_recv()
                            self.launch(self.ccopy, a, dz, dy, dx)

    def finish(self, a):
        for dz in range(self.dims[0]):
            for dy in range(self.dims[1]):
                many = self.sp if self.split(a) and dz + dy else 1
                for dx in range(many):
                    self.ccopy(a, dz, dy, dx).wait_recv()

    def drain(self):
        for make, args in self.flying:
            make(*args).wait_send()


def parts_of(rows, sp):
    return sp if rows % (16 * sp) == 0 else 1


def add_rows(rows, first, second, put):
    step = 32 if rows % 32 == 0 else (16 if rows % 16 == 0 else 8)

    def body(i, _):
        at = pl.ds(pl.multiple_of(i * step, step), step)
        put(at, first[at, :].astype(F32) + second[at, :].astype(F32))
        return 0

    lax.fori_loop(0, rows // step, body, 0)


class Sums:
    def __init__(self, dims, sp, shapes, modes, grads, own, outs, bufs, sems):
        self.dims, self.sp, self.shapes, self.modes = dims, sp, shapes, modes
        self.grads, self.own, self.outs = grads, own, outs
        self.crecvd, self.xrecvd, self.yrecvd, self.zrecvd, self.last = bufs
        self.csem, self.xsem, self.ysem, self.zsem, self.fsem, self.lsem = sems
        zs, ys, cs = dims
        self.me, self.x = lax.axis_index("fsdp"), lax.axis_index("sp")
        self.z, self.y, self.c = self.me // (ys * cs), (self.me // cs) % ys, self.me % cs
        self.flying = []

    def dev(self, zz, yy, cc):
        return ((zz * self.dims[1] + yy) * self.dims[2] + cc, self.x)

    def launch(self, copy):
        copy.start()
        self.flying.append(copy)

    def order(self):
        zs, ys, _ = self.dims
        return [(dz, dy) for dz in range(zs - 1, -1, -1) for dy in range(ys - 1, -1, -1)]

    def grad(self, a, dz, dy, cc):
        zs, ys, cs = self.dims
        h, rows, _ = self.shapes[a]
        owner = (((self.z + dz) % zs) * ys + (self.y + dy) % ys) * cs + cc
        return self.grads[a].at[span(owner, h * rows, h * rows)]

    def part(self, a, dz, dy, k):
        zs, ys, cs = self.dims
        h, rows, _ = self.shapes[a]
        if self.own[a] is not None:
            return self.own[a].at[dz, dy, span(k, rows, rows)]
        owner = (((self.z + dz) % zs) * ys + (self.y + dy) % ys) * cs + self.c
        return self.grads[a].at[span(owner * h + k, rows, rows)]

    def piece(self, a):
        return self.x if self.shapes[a][0] > 1 else 0

    def ccopy(self, a, dz, dy):
        return remote(
            self.grad(a, dz, dy, 1 - self.c),
            self.crecvd[a].at[dz, dy],
            self.csem.at[0, a, dz, dy],
            self.csem.at[1, a, dz, dy],
            self.dev(self.z, self.y, 1 - self.c),
        )

    def mine(self, a, dz, dy):
        return pltpu.make_async_copy(
            self.grad(a, dz, dy, self.c), self.own[a].at[dz, dy], self.lsem.at[a, dz, dy]
        )

    def xcopy(self, a, dz, dy, dx):
        to = (self.x + dx) % self.sp
        return remote(
            self.part(a, dz, dy, to),
            self.xrecvd[a].at[dz, dy, dx - 1],
            self.xsem.at[0, a, dz, dy, dx],
            self.xsem.at[1, a, dz, dy, dx],
            (self.me, to),
        )

    def ycopy(self, a, dz, dy):
        return remote(
            self.part(a, dz, dy, self.piece(a)),
            self.yrecvd[a].at[dz, dy - 1],
            self.ysem.at[0, a, dz, dy],
            self.ysem.at[1, a, dz, dy],
            self.dev(self.z, (self.y + dy) % self.dims[1], self.c),
        )

    def zcopy(self, a, dz):
        return remote(
            self.part(a, dz, 0, self.piece(a)),
            self.zrecvd[a].at[dz - 1],
            self.zsem.at[0, a, dz],
            self.zsem.at[1, a, dz],
            self.dev((self.z + dz) % self.dims[0], self.y, self.c),
        )

    def fcopy(self, a, dx):
        return remote(
            self.last[a].at[self.x],
            self.last[a].at[self.x],
            self.fsem.at[0, a, dx],
            self.fsem.at[1, a, dx],
            (self.me, (self.x + dx) % self.sp),
        )

    def add(self, a, first, second, target):
        def put(at, value):
            target[at, :] = value.astype(BF16)

        add_rows(self.shapes[a][1], first, second, put)

    def start(self, a):
        for dz, dy in self.order():
            self.launch(self.ccopy(a, dz, dy))
            if self.own[a] is not None:
                self.mine(a, dz, dy).start()

    def over_c(self, a):
        h, rows, _ = self.shapes[a]
        for dz, dy in self.order():
            if self.own[a] is not None:
                self.mine(a, dz, dy).wait()
            self.ccopy(a, dz, dy).wait_recv()
            for k in range(h):
                ref = self.part(a, dz, dy, k)
                self.add(a, ref, self.crecvd[a].at[dz, dy, pl.ds(k * rows, rows)], ref)
            if h > 1:
                for dx in range(1, self.sp):
                    self.launch(self.xcopy(a, dz, dy, dx))

    def over_x(self, a, dz):
        for dy in range(self.dims[1] - 1, -1, -1):
            if self.shapes[a][0] > 1:
                ref = self.part(a, dz, dy, self.x)
                for dx in range(1, self.sp):
                    self.xcopy(a, dz, dy, dx).wait_recv()
                    self.add(a, ref, self.xrecvd[a].at[dz, dy, dx - 1], ref)
            if dy:
                self.launch(self.ycopy(a, dz, dy))

    def over_y(self, a, dz):
        ref = self.part(a, dz, 0, self.piece(a))
        for dy in range(1, self.dims[1]):
            self.ycopy(a, dz, dy).wait_recv()
            self.add(a, ref, self.yrecvd[a].at[dz, dy - 1], ref)
        if dz:
            self.launch(self.zcopy(a, dz))

    def over_z(self, a):
        zs = self.dims[0]
        ref = self.part(a, 0, 0, self.piece(a))
        for dz in range(1, zs):
            self.zcopy(a, dz).wait_recv()
            target = self.last[a].at[self.x] if dz == zs - 1 else ref
            self.add(a, ref, self.zrecvd[a].at[dz - 1], target)
        if zs == 1:
            self.last[a][self.x] = ref[...]
        for dx in range(1, self.sp):
            self.launch(self.fcopy(a, dx))

    def all_x(self, a):
        for dz in range(self.dims[0] - 1, -1, -1):
            self.over_x(a, dz)

    def all_y(self, a):
        for dz in range(self.dims[0] - 1, -1, -1):
            self.over_y(a, dz)

    def both(self, a):
        zs = self.dims[0]
        for dz in range(zs - 1, -2, -1):
            if dz >= 0:
                self.over_x(a, dz)
            if dz < zs - 1:
                self.over_y(a, dz + 1)

    def finish(self, a):
        for dx in range(1, self.sp):
            self.fcopy(a, dx).wait_recv()
        if self.modes[a] == "add" and self.shapes[a][0] == 1:
            value = self.last[a][0].astype(F32)
            for k in range(1, self.sp):
                value = value + self.last[a][k].astype(F32)
            self.outs[a][0] = value
        else:
            for k in range(self.sp):
                self.outs[a][k] = self.last[a][k].astype(F32)

    def drain(self):
        for copy in self.flying:
            copy.wait_send()


def lane_groups(values):
    lane = lax.broadcasted_iota(jnp.int32, values.shape, 1)
    step = 1
    while step < C // GROUPS:
        up = pltpu.roll(values, step, 1)
        down = pltpu.roll(values, C - step, 1)
        values = values + jnp.where((lane & step) != 0, up, down)
        step *= 2
    return values


def column_sums(rows, fields):
    probe = jax.eval_shape(lambda: fields(0))

    def body(r, sums):
        return tuple(
            s + jnp.sum(v.reshape(-1, 8, C), axis=0) for s, v in zip(sums, fields(r), strict=True)
        )

    sums = lax.fori_loop(0, rows, body, tuple(jnp.zeros((8, C), F32) for _ in probe))
    return [jnp.broadcast_to(jnp.sum(s, axis=0, keepdims=True), (8, C)) for s in sums]


def stack_rows(*values):
    row = lax.broadcasted_iota(jnp.int32, (8, C), 0)
    out = jnp.zeros((8, C), F32)
    for k, value in enumerate(values):
        out = jnp.where(row == k, value, out)
    return out


class Swap:
    def __init__(self, sp, sums, ssem, hsem):
        self.sp, self.sums, self.ssem, self.hsem = sp, sums, ssem, hsem
        self.me, self.x = lax.axis_index("fsdp"), lax.axis_index("sp")

    def peers(self):
        return [(self.me, (self.x + d) % self.sp) for d in range(1, self.sp)]

    def _sums(self, k, d):
        return remote(
            self.sums.at[k, self.x],
            self.sums.at[k, self.x],
            self.ssem.at[0, k, d],
            self.ssem.at[1, k, d],
            (self.me, (self.x + d) % self.sp),
        )

    def sums_start(self, k, value):
        self.sums[k, self.x] = value
        for d in range(1, self.sp):
            self._sums(k, d).start()

    def sums_wait(self, k):
        for d in range(1, self.sp):
            self._sums(k, d).wait()
        return [self.sums[k, i] for i in range(self.sp)]

    def _up(self, k, src, dst):
        to = (self.x + self.sp - 1) % self.sp
        return remote(src, dst.at[1], self.hsem.at[0, k, 0], self.hsem.at[1, k, 0], (self.me, to))

    def _down(self, k, src, dst):
        to = (self.x + 1) % self.sp
        return remote(src, dst.at[0], self.hsem.at[0, k, 1], self.hsem.at[1, k, 1], (self.me, to))

    def edges_start(self, k, top, bottom, dst):
        @pl.when(self.x > 0)
        def _():
            self._up(k, top, dst).start()

        @pl.when(self.x < self.sp - 1)
        def _():
            self._down(k, bottom, dst).start()

    def edges_wait(self, k, top, bottom, dst):
        @pl.when(self.x > 0)
        def _():
            self._up(k, top, dst).wait_send()
            self._down(k, bottom, dst).wait_recv()

        @pl.when(self.x < self.sp - 1)
        def _():
            self._down(k, bottom, dst).wait_send()
            self._up(k, top, dst).wait_recv()


def put_shifted(dst, at, value):
    columns = value.shape[0]
    col = lax.broadcasted_iota(jnp.int32, value.shape, 0)
    dst[1, at] = value.astype(BF16)
    dst[0, at] = jnp.where(col == 0, 0.0, pltpu.roll(value, 1, 0)).astype(BF16)
    dst[2, at] = jnp.where(col == columns - 1, 0.0, pltpu.roll(value, columns - 1, 0)).astype(BF16)


def taps(rows, columns, shifted, weight, acc, back, hooks=()):
    pixels = rows * columns

    def body(t, _):
        for k, hook in enumerate(hooks):
            pl.when(t == k)(hook)
        total = None
        for dc in range(3):
            if back:
                lhs = shifted[2 - dc, pl.ds(2 - t, rows)].reshape(pixels, C)
            else:
                lhs = shifted[dc, pl.ds(t, rows)].reshape(pixels, C)
            rhs = weight[pl.ds(pl.multiple_of((3 * t + dc) * C, C), C), :]
            out = lax.dot_general(
                lhs, rhs, (((1,), (1 if back else 0,)), ((), ())), preferred_element_type=F32
            )
            total = out if total is None else total + out
        total = total.reshape(rows, columns, C)

        @pl.when(t == 0)
        def _():
            acc[...] = total

        @pl.when(t > 0)
        def _():
            acc[...] += total

        return 0

    lax.fori_loop(0, 3, body, 0)


def numbers(height, rows, columns, sp):
    x = lax.axis_index("sp")
    ids = x * rows + jnp.arange(-1, rows + 1, dtype=jnp.int32)
    valid = ((ids >= 0) & (ids < height)).astype(F32)
    count = (height * columns * (C // GROUPS)).astype(F32)
    held = jnp.clip(height - rows * jnp.arange(sp, dtype=jnp.int32), 0, rows)
    held = (held * columns * (C // GROUPS)).astype(F32)
    bias = jnp.where(jnp.arange(sp * rows, dtype=jnp.int32) < height, 0.0, MASKED).astype(F32)
    return jnp.concatenate([valid, count[None], held, held[x][None], bias])


def local_moments(rows, field, mask, held):
    (total,) = column_sums(rows, lambda r: (field(r),))
    total = lane_groups(total)
    mean = (total / jnp.maximum(held, 1.0))[:1]

    def centred(r):
        v = (field(r) - mean) * mask(r)
        return (v * v,)

    (square,) = column_sums(rows, centred)
    return stack_rows(total, lane_groups(square))


def joint_moments(members, counts, count):
    mean = members[0][:1]
    for m in members[1:]:
        mean = mean + m[:1]
    mean = mean / count
    square = None
    for m, n in zip(members, counts, strict=True):
        off = m[:1] / jnp.maximum(n, 1.0) - mean
        term = m[1:2] + n * off * off
        square = term if square is None else square + term
    return mean, lax.rsqrt(square / count + EPSILON)


def forward_kernel(dims, fsdp, sp, shapes, kinds, plan, *refs):
    n = len(shapes)
    (nums, image, tiles, table), shards, refs = refs[:4], refs[4 : 4 + n], refs[4 + n :]
    (resid, normed, conv_out, s1, s2, stats, gains, scales, got), refs = refs[:9], refs[9:]
    outs, refs = refs[:n], refs[n:]
    (w1v, w2v), bufs, refs = refs[:2], refs[2:n], refs[n:]
    (edge1, edge2, acc, sums, part, part_in), refs = refs[:6], refs[6:]
    (ssem, hsem, wsem, lsem, tsem, psem), sems = refs[:6], refs[6:]
    sources, wholes = shards[:2] + bufs, (w1v, w2v) + outs[2:]
    entries = [(sources[a], wholes[a], h, r, at, shapes[a][0]) for a, h, r, at in plan]
    move = Gather(dims, sp, entries, sems)
    me, x = move.me, move.x
    first_of, second_of, late = (
        [e for e, p in enumerate(plan) if min(p[0], 2) == a] for a in range(3)
    )
    rows, columns = image.shape[0], image.shape[1]
    swap = Swap(sp, sums, ssem, hsem)
    homes = [wholes[a].at[span(me, shapes[a][0], shapes[a][0])] for a in range(n)]
    loads = [pltpu.make_async_copy(shards[a], homes[a], wsem.at[a]) for a in range(2)]
    staged = []
    for a in range(2, n):
        width = shapes[a][1] // kinds[a]
        for j in range(kinds[a]):
            if shards[a].shape[1] == shapes[a][1]:
                src = shards[a]
            else:
                start = pl.multiple_of((j * sp + x) * width, 128)
                src = shards[a].at[:, pl.ds(start, width)]
            dst = bufs[a - 2].at[:, j * width : (j + 1) * width]
            staged.append(pltpu.make_async_copy(src, dst, lsem.at[a, j]))
    for load in loads + staged:
        load.start()
    edge1[...] = jnp.zeros_like(edge1)
    edge2[...] = jnp.zeros_like(edge2)
    greet(swap.peers() + [((me + d) % fsdp, x) for d in range(1, fsdp)])
    first_tiles = tiles_start(
        fsdp, tiles, got, tsem.at[0], tsem.at[1], lambda ref, to: ref.at[to]
    )
    got[me] = tiles[me]
    for e in first_of:
        move.start_y(e)
        move.start_z(e)
    swap.edges_start(0, image.at[0], image.at[rows - 1], edge1)
    count = nums[rows + 2]
    counts = [nums[rows + 3 + i] for i in range(sp)]
    held = nums[rows + 3 + sp]

    def mask(r):
        return nums[r + 1]

    def masked(r):
        return image[r].astype(F32) * mask(r)

    swap.sums_start(0, local_moments(rows, masked, mask, held))
    for copy in staged:
        copy.wait()
    for e in first_of:
        move.relay(e, 1)
    stores = [pltpu.make_async_copy(bufs[a - 2], homes[a], wsem.at[a]) for a in range(2, n)]
    for copy in stores:
        copy.start()
    for copy in first_tiles:
        copy.wait_recv()
    share = C // fsdp
    many = 128 // share
    for b in range(C // 128):
        block = got[b * many]
        for f in range(b * many + 1, (b + 1) * many):
            block = block + got[f]
        gains[:, b * 128 : (b + 1) * 128] = block
    act = got[:, 0, :].astype(BF16)
    for j in range(8):
        part[:, j, :] = jnp.dot(
            act, table[:, j * 128 : (j + 1) * 128], preferred_element_type=F32
        )
    part_in[me] = part[me]
    second_tiles = tiles_start(
        fsdp, part, part_in, psem.at[0], psem.at[1], lambda ref, to: ref.at[to]
    )
    for e in second_of + late:
        move.start_z(e)
    mean1, inv1 = joint_moments(swap.sums_wait(0), counts, count)
    swap.edges_wait(0, image.at[0], image.at[rows - 1], edge1)
    g1, g2, g3 = gains[1:2], gains[2:3], gains[3:4]

    def first(at, value):
        m = nums[at]
        hidden = (value.astype(F32) * m - mean1) * m * inv1 * g1
        put_shifted(s1, at, hidden * jax.nn.sigmoid(hidden) * m)

    lax.fori_loop(0, rows, lambda r, _: (first(r + 1, image[r]), 0)[1], 0)
    first(0, edge1[0])
    first(rows + 1, edge1[1])
    for dz in range(2, dims[0] + 1):
        for e in first_of:
            move.relay(e, dz)
    for e in second_of:
        move.start_y(e)
        move.relay(e, 1)
    for e in first_of:
        move.over_x(e)
    loads[0].wait()
    for e in first_of:
        move.finish(e)
    pltpu.make_async_copy(w1v, outs[0], wsem.at[0]).start()

    def along(group, dz):
        for e in group:
            move.relay(e, dz)

    zs = dims[0]
    hooks = [functools.partial(along, second_of, dz) for dz in range(2, min(4, zs + 1))]
    taps(rows, columns, s1, w1v, acc, False, hooks)
    for dz in range(len(hooks) + 2, zs + 1):
        along(second_of, dz)
    for e in late:
        move.start_y(e)

    def keep(r, _):
        conv_out[r] = acc[r] * mask(r)
        return 0

    lax.fori_loop(0, rows, keep, 0)
    swap.edges_start(1, conv_out.at[0], conv_out.at[rows - 1], edge2)
    swap.sums_start(1, local_moments(rows, lambda r: conv_out[r], mask, held))
    along(late, 1)
    along(late, 2)
    mean2, inv2 = joint_moments(swap.sums_wait(1), counts, count)
    swap.edges_wait(1, conv_out.at[0], conv_out.at[rows - 1], edge2)
    for copy in second_tiles:
        copy.wait_recv()
    total = part_in[0]
    for f in range(1, fsdp):
        total = total + part_in[f]
    scales[...] = jnp.zeros_like(scales)
    for j in range(8):
        lanes = slice(j % 4 * 128, (j % 4 + 1) * 128)
        scales[j // 4 : j // 4 + 1, lanes] = total[j : j + 1]
    scale, shift = 1.0 + scales[0:1], scales[1:2]

    def second(at, value):
        m = nums[at]
        hidden = (value - mean2) * m * inv2 * g2 * scale + shift
        put_shifted(s2, at, hidden * jax.nn.sigmoid(hidden) * m)

    lax.fori_loop(0, rows, lambda r, _: (second(r + 1, conv_out[r]), 0)[1], 0)
    second(0, edge2[0])
    second(rows + 1, edge2[1])
    along(late, 3)
    for e in second_of:
        move.over_x(e)
    loads[1].wait()
    for e in second_of:
        move.finish(e)
    pltpu.make_async_copy(w2v, outs[1], wsem.at[1]).start()
    taps(rows, columns, s2, w2v, acc, False)
    for dz in range(4, zs + 1):
        along(late, dz)

    def add(r, _):
        resid[r] = masked(r) + acc[r] * mask(r)
        return 0

    lax.fori_loop(0, rows, add, 0)
    swap.sums_start(2, local_moments(rows, lambda r: resid[r], mask, held))
    mean3, inv3 = joint_moments(swap.sums_wait(2), counts, count)

    def third(r, _):
        normed[r] = ((resid[r] - mean3) * mask(r) * inv3 * g3).astype(BF16)
        return 0

    lax.fori_loop(0, rows, third, 0)
    stats[...] = stack_rows(mean1, inv1, mean2, inv2, mean3, inv3)
    for e in late:
        move.over_x(e)
    for e in late:
        move.finish(e)
    for copy in stores:
        copy.wait()
    for copy in first_tiles + second_tiles:
        copy.wait_send()
    move.drain()
    pltpu.make_async_copy(w1v, outs[0], wsem.at[0]).wait()
    pltpu.make_async_copy(w2v, outs[1], wsem.at[1]).wait()


def forward(nums, image, tiles, table, shards, kinds, fsdp, sp):
    rows, columns, _ = image.shape
    field = (rows, columns, C)
    shifted = (3, rows + 2, columns, C)
    dims = sizes_of(fsdp, sp)
    zs, ys, _ = dims
    n = len(shards)
    shapes, plan = [], []
    for a, (shard, kind) in enumerate(zip(shards, kinds, strict=True)):
        r, width = shard.shape
        shapes.append((r, width // sp if kind else width))
        h = 1 if kind else parts_of(r, sp)
        plan.append((a, h, r // h, 0))
    m = len(plan)
    wholes = [jax.ShapeDtypeStruct((fsdp * r, w), BF16) for r, w in shapes]
    staged = [pltpu.VMEM(shape, BF16) for shape in shapes[2:]]
    tile = pltpu.VMEM((fsdp, 8, 128), F32)
    return pl.pallas_call(
        functools.partial(
            forward_kernel, dims, fsdp, sp, shapes, [max(k, 1) for k in kinds], plan
        ),
        out_shape=[
            jax.ShapeDtypeStruct(field, F32),
            jax.ShapeDtypeStruct(field, BF16),
            jax.ShapeDtypeStruct(field, F32),
            jax.ShapeDtypeStruct(shifted, BF16),
            jax.ShapeDtypeStruct(shifted, BF16),
            jax.ShapeDtypeStruct((8, C), F32),
            jax.ShapeDtypeStruct((8, C), F32),
            jax.ShapeDtypeStruct((8, C), F32),
            jax.ShapeDtypeStruct((fsdp, 8, 128), F32),
        ]
        + wholes,
        in_specs=[SMEM] + [VMEM] * 3 + [ANY] * n,
        out_specs=[VMEM] * 9 + [ANY] * n,
        scratch_shapes=[
            pltpu.VMEM(wholes[0].shape, BF16),
            pltpu.VMEM(wholes[1].shape, BF16),
        ]
        + staged
        + [
            pltpu.VMEM((2, columns, C), BF16),
            pltpu.VMEM((2, columns, C), F32),
            pltpu.VMEM(field, F32),
            pltpu.VMEM((3, sp, 8, C), F32),
            tile,
            tile,
            DMA((2, 3, sp)),
            DMA((2, 2, 2)),
            DMA((n,)),
            DMA((n, 3)),
            DMA((2, fsdp)),
            DMA((2, fsdp)),
            DMA((2, m, zs)),
            DMA((2, m, zs, ys)),
            DMA((2, m, zs, ys, sp)),
            DMA((2, m, zs, ys, sp)),
        ],
        compiler_params=params(1),
        name="forward",
    )(nums, image, tiles, table, *shards)


def attention_kernel(
    sp,
    heads,
    nums,
    normed,
    text,
    wq,
    wt,
    wo,
    cot,
    resid,
    output,
    gnorm,
    gq,
    gt,
    go,
    gtext,
    nall,
    gown,
    gall,
    qkv,
    keys,
    values,
    dk,
    dv,
    att,
    attin,
    dqkv,
    gtkv,
    gpart,
    grecv,
    low,
    nsem,
    gsem,
    asem,
    psem,
):
    rows, columns = cot.shape[0], cot.shape[1]
    pixels = rows * columns
    width = heads * HEAD
    total_px = sp * pixels
    me, x = lax.axis_index("fsdp"), lax.axis_index("sp")
    factor = HEAD**-0.5
    greet([(me, (x + d) % sp) for d in range(1, sp)])

    def send(pair, src, dst):
        def copy(d):
            to = (x + d) % sp
            return remote(src(to), dst.at[x], pair.at[0, d], pair.at[1, d], (me, to))

        return [copy(d) for d in range(1, sp)]

    def start(copies):
        for copy in copies:
            copy.start()

    def wait(copies):
        for copy in copies:
            copy.wait()

    moves = send(nsem, lambda to: normed, nall)
    start(moves)

    def lower(r, _):
        low[r] = (cot[r].astype(F32) * nums[r + 1]).astype(BF16)
        return 0

    lax.fori_loop(0, rows, lower, 0)
    low2 = low[...].reshape(pixels, C)
    for k in range(sp):
        gown[k] = lax.dot_general(
            low2,
            wo[k * width : (k + 1) * width, :],
            (((1,), (1,)), ((), ())),
            preferred_element_type=F32,
        ).astype(BF16)
    gmoves = send(gsem, lambda to: gown.at[to], gall)
    start(gmoves)
    gall[x] = gown[x]
    nall[x] = normed[...]
    text_kv = jnp.dot(text[...], wt[...], preferred_element_type=F32).astype(BF16)
    keys[total_px:, :] = text_kv[:, :width]
    values[total_px:, :] = text_kv[:, width:]

    def project(k):
        out = jnp.dot(nall[k], wq[...], preferred_element_type=F32).astype(BF16)
        at = pl.ds(pl.multiple_of(k * pixels, pixels), pixels)
        qkv[at, :] = out
        keys[at, :] = out[:, width : 2 * width]
        values[at, :] = out[:, 2 * width :]

    project(x)
    wait(moves)
    for d in range(1, sp):
        project((x + d) % sp)
    wait(gmoves)

    block = 256
    per = pixels // block
    for h in range(heads):
        lanes = slice(h * HEAD, (h + 1) * HEAD)
        kh, vh = keys[:, lanes], values[:, lanes]
        kt, vt = kh.T, vh.T
        dk[...] = jnp.zeros_like(dk)
        dv[...] = jnp.zeros_like(dv)

        def step(j, _, lanes=lanes, kh=kh, vh=vh, kt=kt, vt=vt):
            at = pl.ds(pl.multiple_of(j * block, block), block)
            inner = pl.ds(pl.multiple_of((j % per) * block, block), block)
            q = qkv[at, lanes]
            g = gall[j // per, inner, lanes]
            s = (
                lax.dot_general(kh, q, (((1,), (1,)), ((), ())), preferred_element_type=F32)
                * factor
            )
            pieces = [
                s[r * columns : (r + 1) * columns] + nums[rows + 4 + sp + r]
                for r in range(sp * rows)
            ]
            s = jnp.concatenate(pieces + [s[total_px:]], axis=0)
            raised = jnp.exp(s - jnp.max(s, axis=0, keepdims=True))
            chances = raised * (1.0 / jnp.sum(raised, axis=0, keepdims=True))
            short = chances.astype(BF16)
            att[j // per, inner, lanes] = jnp.dot(
                vt, short, preferred_element_type=F32
            ).T.astype(BF16)
            slope = lax.dot_general(vh, g, (((1,), (1,)), ((), ())), preferred_element_type=F32)
            mean = jnp.sum(chances * slope, axis=0, keepdims=True)
            grad = (chances * (slope - mean)).astype(BF16)
            dqkv[at, lanes] = (jnp.dot(kt, grad, preferred_element_type=F32) * factor).T.astype(
                BF16
            )
            dk[...] += jnp.dot(grad, q, preferred_element_type=F32)
            dv[...] += jnp.dot(short, g, preferred_element_type=F32)
            return 0

        lax.fori_loop(0, sp * per, step, 0)
        low_k = (dk[...] * factor).astype(BF16)
        low_v = dv[...].astype(BF16)
        dqkv[:, width + h * HEAD : width + (h + 1) * HEAD] = low_k[:total_px]
        dqkv[:, 2 * width + h * HEAD : 2 * width + (h + 1) * HEAD] = low_v[:total_px]
        gtkv[:, h * HEAD : (h + 1) * HEAD] = low_k[total_px:]
        gtkv[:, width + h * HEAD : width + (h + 1) * HEAD] = low_v[total_px:]

    amoves = send(asem, lambda to: att.at[to], attin)
    start(amoves)
    attin[x] = att[x]

    def to_normed(k):
        at = pl.ds(pl.multiple_of(k * pixels, pixels), pixels)
        return lax.dot_general(
            dqkv[at, :], wq[...], (((1,), (1,)), ((), ())), preferred_element_type=F32
        )

    for d in range(1, sp):
        to = (x + d) % sp
        gpart[to] = to_normed(to).astype(BF16)
    pmoves = send(psem, lambda to: gpart.at[to], grecv)
    start(pmoves)
    gtext[...] = lax.dot_general(
        gtkv[...], wt[...], (((1,), (1,)), ((), ())), preferred_element_type=F32
    ).astype(BF16)
    gnorm[...] = to_normed(x)
    wait(amoves)
    joined = jnp.concatenate([attin[k] for k in range(sp)], axis=1)
    branch = jnp.dot(joined, wo[...], preferred_element_type=F32)
    for r in range(rows):
        at = slice(r * columns, (r + 1) * columns)
        output[at, :] = (resid[at, :] + branch[at] * nums[r + 1]).astype(BF16)
    down = (((0,), (0,)), ((), ()))
    go[...] = lax.dot_general(joined, low2, down, preferred_element_type=F32).astype(BF16)
    gq[...] = lax.dot_general(
        nall[...].reshape(total_px, C), dqkv[...], down, preferred_element_type=F32
    ).astype(BF16)
    gt[...] = lax.dot_general(text[...], gtkv[...], down, preferred_element_type=F32).astype(BF16)
    wait(pmoves)
    for d in range(1, sp):
        gnorm[...] += grecv[(x + d) % sp].astype(F32)


def attention(nums, normed, text, wq, wt, wo, cot, resid, sp):
    rows, columns, _ = cot.shape
    pixels = rows * columns
    heads = C // HEAD // sp
    width = heads * HEAD
    tokens = text.shape[0]
    n_keys = sp * pixels + tokens
    return pl.pallas_call(
        functools.partial(attention_kernel, sp, heads),
        out_shape=[
            jax.ShapeDtypeStruct((pixels, C), BF16),
            jax.ShapeDtypeStruct((pixels, C), F32),
            jax.ShapeDtypeStruct(wq.shape, BF16),
            jax.ShapeDtypeStruct(wt.shape, BF16),
            jax.ShapeDtypeStruct(wo.shape, BF16),
            jax.ShapeDtypeStruct(text.shape, BF16),
        ],
        in_specs=[SMEM] + [VMEM] * 7,
        out_specs=[VMEM] * 6,
        scratch_shapes=[
            pltpu.VMEM((sp, pixels, C), BF16),
            pltpu.VMEM((sp, pixels, width), BF16),
            pltpu.VMEM((sp, pixels, width), BF16),
            pltpu.VMEM((sp * pixels, 3 * width), BF16),
            pltpu.VMEM((n_keys, width), BF16),
            pltpu.VMEM((n_keys, width), BF16),
            pltpu.VMEM((n_keys, HEAD), F32),
            pltpu.VMEM((n_keys, HEAD), F32),
            pltpu.VMEM((sp, pixels, width), BF16),
            pltpu.VMEM((sp, pixels, width), BF16),
            pltpu.VMEM((sp * pixels, 3 * width), BF16),
            pltpu.VMEM((tokens, 2 * width), BF16),
            pltpu.VMEM((sp, pixels, C), BF16),
            pltpu.VMEM((sp, pixels, C), BF16),
            pltpu.VMEM((rows, columns, C), BF16),
        ]
        + [DMA((2, sp))] * 4,
        compiler_params=params(2),
        name="attention",
    )(nums, normed, text, wq, wt, wo, cot, resid)


def backward_kernel(dims, fsdp, sp, shapes, modes, *refs):
    n = len(shapes)
    (nums, image, gains, scales, stats, resid, conv_out, s1, s2, gnorm, cot, table, tpart, w1, w2), refs = (
        refs[:15],
        refs[15:],
    )
    attn, refs = refs[: n - 2], refs[n - 2 :]
    outs, gimage, gscales, etiles, gtotal, gtext, refs = refs[:n], *refs[n : n + 5], refs[n + 5 :]
    (w1v, w2v, out1, out2, p1, p2, edge1, edge2, gres, acc, sums, mine, every, pieces, got_e), refs = (
        refs[:15],
        refs[15:],
    )
    (ggains, got_g, gsmall, trecv), refs = refs[:4], refs[4:]
    own, refs = (None, None) + tuple(refs[: n - 2]), refs[n - 2 :]
    bufs, refs = [refs[i * n : (i + 1) * n] for i in range(5)], refs[5 * n :]
    (ssem, hsem, wsem, tsem, esem, gsem, rsem, xsem), sems = refs[:8], refs[8:]
    total_of = Sums(dims, sp, shapes, modes, (out1, out2) + tuple(attn), own, outs, bufs, sems)
    rows, columns = image.shape[0], image.shape[1]
    pixels = rows * columns
    me, x = lax.axis_index("fsdp"), lax.axis_index("sp")
    swap = Swap(sp, sums, ssem, hsem)
    load1 = pltpu.make_async_copy(w1, w1v, wsem.at[0])
    load2 = pltpu.make_async_copy(w2, w2v, wsem.at[1])
    load2.start()
    load1.start()
    edge1[...] = jnp.zeros_like(edge1)
    edge2[...] = jnp.zeros_like(edge2)
    greet(swap.peers() + [((me + d) % fsdp, x) for d in range(1, fsdp)])
    late = list(range(2, n))
    for a in late:
        total_of.start(a)
    count = nums[rows + 2]
    g1, g2, g3 = gains[1:2], gains[2:3], gains[3:4]
    mean1, inv1, mean2, inv2, mean3, inv3 = (stats[k : k + 1] for k in range(6))

    def mask(r):
        return nums[r + 1]

    def joint(k):
        members = swap.sums_wait(k)
        total = members[0]
        for m in members[1:]:
            total = total + m
        return total

    def weight_grad(shifted, padded, store):
        grad = padded[1, 1 : rows + 1].reshape(pixels, C)

        def body(t, _):
            for dc in range(3):
                lhs = shifted[dc, pl.ds(t, rows)].reshape(pixels, C)
                at = pl.ds(pl.multiple_of((3 * t + dc) * C, C), C)
                store[at, :] = lax.dot_general(
                    lhs, grad, (((0,), (0,)), ((), ())), preferred_element_type=F32
                ).astype(BF16)
            return 0

        lax.fori_loop(0, 3, body, 0)

    def hat3(r):
        return (resid[r] - mean3) * mask(r) * inv3

    def from_three(r):
        g = gnorm[r] * mask(r)
        return g, g * hat3(r)

    plain, crossed = column_sums(rows, from_three)
    gain3 = crossed
    swap.sums_start(0, stack_rows(lane_groups(plain * g3), lane_groups(crossed * g3)))
    total = joint(0) / count
    m1, m2 = total[0:1], total[1:2]

    def residual(r, _):
        m = mask(r)
        e = gnorm[r] * m * g3
        value = cot[r].astype(F32) * m + m * inv3 * (e - m1 - hat3(r) * m2)
        gres[r] = value
        put_shifted(p2, r + 1, value * m)
        return 0

    lax.fori_loop(0, rows, residual, 0)
    swap.edges_start(0, p2.at[1, 1], p2.at[1, rows], edge2)
    tmoves = []
    for d in range(1, sp):
        to = (me, (x + d) % sp)
        tmoves.append(remote(tpart, trecv.at[d - 1], xsem.at[0, d], xsem.at[1, d], to))
        tmoves[-1].start()
    weight_grad(s2, p2, out2)
    total_of.start(1)
    for a in late:
        total_of.over_c(a)
        if shapes[a][0] == 1:
            total_of.all_x(a)
    swap.edges_wait(0, p2.at[1, 1], p2.at[1, rows], edge2)
    put_shifted(p2, 0, edge2[0].astype(F32))
    put_shifted(p2, rows + 1, edge2[1].astype(F32))
    load2.wait()
    taps(rows, columns, p2, w2v, acc, True)
    total_of.over_c(1)
    total_of.all_x(1)
    scale, shift = 1.0 + scales[0:1], scales[1:2]

    def hat2(r):
        return (conv_out[r] - mean2) * mask(r) * inv2

    def slope(value):
        s = jax.nn.sigmoid(value)
        return s * (1.0 + value * (1.0 - s))

    def from_two(r):
        hat = hat2(r)
        g = acc[r] * mask(r) * slope(hat * g2 * scale + shift)
        acc[r] = g
        return g, g * hat

    plain, crossed = column_sums(rows, from_two)
    gain2 = crossed * scale
    swap.sums_start(
        1,
        stack_rows(
            lane_groups(plain * (scale * g2)),
            lane_groups(crossed * (scale * g2)),
            crossed * g2,
            plain,
        ),
    )
    total = joint(1)
    for k in range(8):
        row = 2 + k // 4
        lanes = slice((k % 4) * 128, (k % 4 + 1) * 128)
        mine[k : k + 1, :] = total[row : row + 1, lanes].astype(BF16).astype(F32)
    copies = tiles_start(fsdp, mine, every, tsem.at[0], tsem.at[1], lambda ref, to: ref)
    every[me] = mine[...]
    m1, m2 = total[0:1] / count, total[1:2] / count

    def middle(r, _):
        m = mask(r)
        value = m * inv2 * (acc[r] * (scale * g2) - m1 - hat2(r) * m2)
        put_shifted(p1, r + 1, value)
        return 0

    lax.fori_loop(0, rows, middle, 0)
    swap.edges_start(1, p1.at[1, 1], p1.at[1, rows], edge1)
    for a in late:
        if shapes[a][0] > 1:
            total_of.all_x(a)
    weight_grad(s1, p1, out1)
    total_of.start(0)
    for a in late:
        if shapes[a][0] == 1:
            total_of.all_y(a)
    swap.edges_wait(1, p1.at[1, 1], p1.at[1, rows], edge1)
    put_shifted(p1, 0, edge1[0].astype(F32))
    put_shifted(p1, rows + 1, edge1[1].astype(F32))
    load1.wait()
    total_of.over_c(0)
    taps(rows, columns, p1, w1v, acc, True)

    def hat1(r):
        return (image[r].astype(F32) * mask(r) - mean1) * mask(r) * inv1

    def from_one(r):
        hat = hat1(r)
        g = acc[r] * mask(r) * slope(hat * g1)
        acc[r] = g
        return g, g * hat

    plain, crossed = column_sums(rows, from_one)
    swap.sums_start(2, stack_rows(lane_groups(plain * g1), lane_groups(crossed * g1)))
    ggains[...] = stack_rows(crossed, gain2, gain3)
    share = C // fsdp

    def gain_block(ref, to):
        return ref.at[:, pl.ds(pl.multiple_of((to * share) // 128 * 128, 128), 128)]

    gcopies = tiles_start(fsdp, ggains, got_g, gsem.at[0], gsem.at[1], gain_block)
    got_g[me] = ggains[:, pl.ds(pl.multiple_of((me * share) // 128 * 128, 128), 128)]
    total_of.all_y(1)
    for a in late:
        if shapes[a][0] > 1:
            total_of.all_y(a)
    for copy in copies:
        copy.wait()
    gscales[...] = every[...]
    piece = None
    for j in range(8):
        term = lax.dot_general(
            every[:, j, :].astype(BF16),
            table[:, j * 128 : (j + 1) * 128],
            (((1,), (1,)), ((), ())),
            preferred_element_type=F32,
        )
        piece = term if piece is None else piece + term
    pieces[...] = jnp.broadcast_to(piece[:, None, :], pieces.shape)
    ecopies = tiles_start(fsdp, pieces, got_e, esem.at[0], esem.at[1], lambda ref, to: ref.at[to])
    got_e[me] = pieces[me]
    total_of.both(0)
    for a in late:
        total_of.over_z(a)
    total = joint(2) / count
    m1, m2 = total[0:1], total[1:2]

    def final(r, _):
        m = mask(r)
        gimage[r] = (gres[r] + m * inv1 * (acc[r] * g1 - m1 - hat1(r) * m2)) * m
        return 0

    lax.fori_loop(0, rows, final, 0)
    total_of.over_z(1)
    for copy in tmoves:
        copy.wait()
    text_rows = 32

    def text_sum(r, _):
        at = span(r, text_rows, text_rows)
        value = tpart[at, :].astype(F32)
        for i in range(sp - 1):
            value = value + trecv[i, at, :].astype(F32)
        gtext[at, :] = value
        return 0

    lax.fori_loop(0, tpart.shape[0] // text_rows, text_sum, 0)
    for copy in gcopies:
        copy.wait()
    total = got_g[0]
    for f in range(1, fsdp):
        total = total + got_g[f]
    gsmall[x] = total

    def small_copy(d):
        to = (me, (x + d) % sp)
        return remote(gsmall.at[x], gsmall.at[x], rsem.at[0, d], rsem.at[1, d], to)

    for d in range(1, sp):
        small_copy(d).start()
    for a in late:
        total_of.finish(a)
    for copy in ecopies:
        copy.wait()
    etiles[...] = got_e[...]
    for d in range(1, sp):
        small_copy(d).wait()
    total = gsmall[0]
    for i in range(1, sp):
        total = total + gsmall[i]
    gtotal[...] = total
    total_of.over_z(0)
    total_of.finish(1)
    total_of.finish(0)
    total_of.drain()


def backward(
    nums, image, gains, scales, stats, resid, conv_out, s1, s2, gnorm, cot, table, tpart, w1, w2, attn, fsdp, sp
):
    rows, columns, _ = image.shape
    field = (rows, columns, C)
    shifted = (3, rows + 2, columns, C)
    dims = sizes_of(fsdp, sp)
    zs, ys, _ = dims
    shapes, outs = [], []
    grads = [w1, w2] + [g for g, _ in attn]
    modes = ["add", "add"] + [m for _, m in attn]
    for a, (grad, mode) in enumerate(zip(grads, modes, strict=True)):
        r, width = grad.shape[0] // fsdp, grad.shape[1]
        h = parts_of(r, sp) if mode == "add" and a != 1 else 1
        shapes.append((h, r // h, width))
        copies = 1 if mode == "add" and h == 1 else sp
        outs.append(jax.ShapeDtypeStruct((copies, r // h, width), F32))
    count = len(grads)

    def scratch(*shape):
        return pltpu.VMEM(shape, BF16)

    tile = jax.ShapeDtypeStruct((fsdp, 8, 128), F32)
    tiles = pltpu.VMEM((fsdp, 8, 128), F32)
    return pl.pallas_call(
        functools.partial(backward_kernel, dims, fsdp, sp, shapes, modes),
        out_shape=outs
        + [jax.ShapeDtypeStruct(field, F32), tile, tile, jax.ShapeDtypeStruct((8, 128), F32)]
        + [jax.ShapeDtypeStruct(tpart.shape, F32)],
        in_specs=[SMEM] + [VMEM] * 12 + [ANY] * count,
        out_specs=[VMEM] * (count + 5),
        scratch_shapes=[
            scratch(*w1.shape),
            scratch(*w2.shape),
            scratch(*w1.shape),
            scratch(*w2.shape),
            scratch(*shifted),
            scratch(*shifted),
            scratch(2, columns, C),
            scratch(2, columns, C),
            pltpu.VMEM(field, F32),
            pltpu.VMEM(field, F32),
            pltpu.VMEM((3, sp, 8, C), F32),
            pltpu.VMEM((8, 128), F32),
            tiles,
            tiles,
            tiles,
            pltpu.VMEM((8, C), F32),
            tiles,
            pltpu.VMEM((sp, 8, 128), F32),
            scratch(max(sp - 1, 1), *tpart.shape),
        ]
        + [scratch(zs, ys, s[0] * s[1], s[2]) for s in shapes[2:]]
        + [scratch(zs, ys, s[0] * s[1], s[2]) for s in shapes]
        + [
            scratch(zs, ys, sp - 1, *s[1:]) if s[0] > 1 else scratch(1, 1, 1, 16, 128)
            for s in shapes
        ]
        + [scratch(zs, max(ys - 1, 1), *s[1:]) for s in shapes]
        + [scratch(max(zs - 1, 1), *s[1:]) for s in shapes]
        + [scratch(sp, *s[1:]) for s in shapes]
        + [
            DMA((2, 3, sp)),
            DMA((2, 2, 2)),
            DMA((2,)),
            DMA((2, fsdp)),
            DMA((2, fsdp)),
            DMA((2, fsdp)),
            DMA((2, sp)),
            DMA((2, sp)),
            DMA((2, count, zs, ys)),
            DMA((2, count, zs, ys, sp)),
            DMA((2, count, zs, ys)),
            DMA((2, count, zs)),
            DMA((2, count, sp)),
            DMA((count, zs, ys)),
        ],
        compiler_params=params(3),
        name="backward",
    )(
        nums, image, gains, scales, stats, resid, conv_out, s1, s2, gnorm, cot, table, tpart, w1, w2,
        *[g for g, _ in attn],
    )


def per_device(
    image,
    embedding,
    text,
    heights,
    gain_one,
    conv_one,
    emb_proj,
    gain_two,
    conv_two,
    gain_three,
    qkv_proj,
    text_proj,
    out_proj,
    cotangent,
):
    rows, columns = image.shape[1], image.shape[2]
    fsdp, sp = lax.axis_size("fsdp"), lax.axis_size("sp")
    heads = C // HEAD // sp
    width = heads * HEAD
    share = gain_one.shape[0]
    emb_rows = emb_proj.shape[0]
    nums = numbers(heights[0], rows, columns, sp)
    emb_float = embedding.astype(F32)
    emb_act = jax.nn.silu(emb_float).astype(BF16)

    def lanes(array):
        return jnp.pad(array, [(0, 0)] * (array.ndim - 1) + [(0, 128 - array.shape[-1])])

    many = 128 // share
    place = lax.broadcasted_iota(jnp.int32, (3, 128), 1) // share == lax.axis_index("fsdp") % many
    gain_rows = jnp.stack([gain_one, gain_two, gain_three]).astype(F32)
    gain_rows = jnp.where(place, jnp.tile(gain_rows, (1, many)), 0.0)
    tiles = jnp.concatenate(
        [
            lanes(emb_act.astype(F32).reshape(fsdp, 1, emb_rows)),
            jnp.broadcast_to(gain_rows[None], (fsdp, 3, 128)),
            jnp.zeros((fsdp, 4, 128), F32),
        ],
        axis=1,
    )
    table = jnp.pad(emb_proj, ((0, 128 - emb_rows), (0, 0)))
    resid, normed, conv_out, s1, s2, stats, gains, scales, tiles_in, w1, w2, wt, wq, wo = forward(
        nums,
        image[0],
        tiles,
        table,
        [conv_one, conv_two, text_proj, qkv_proj, out_proj],
        [0, 0, 2, 3, 0],
        fsdp,
        sp,
    )
    emb_cols = tiles_in[:, 0, :emb_rows].astype(BF16)
    pixels = rows * columns
    output, gnorm, gq, gt, go, tpart = attention(
        nums,
        normed.reshape(pixels, C),
        text[0],
        wq,
        wt,
        wo,
        cotangent[0],
        resid.reshape(pixels, C),
        sp,
    )
    (r1, r2, rt, rq, ro, gimage, every, tiles_in, small, gtext) = backward(
        nums,
        image[0],
        gains,
        scales,
        stats,
        resid,
        conv_out,
        s1,
        s2,
        gnorm.reshape(rows, columns, C),
        cotangent[0],
        table,
        tpart,
        w1,
        w2,
        [(gt, "join"), (gq, "join"), (go, "add")],
        fsdp,
        sp,
    )
    grad_scales = every.reshape(fsdp, 2 * C).astype(BF16)
    grad_emb_proj = lax.dot_general(
        emb_cols, grad_scales, (((0,), (0,)), ((), ())), preferred_element_type=F32
    )

    def joined(result, kinds):
        n = result.shape[1]
        return result.reshape(sp, n, kinds, width).transpose(1, 2, 0, 3).reshape(n, kinds * C)

    grad_embedding = tiles_in[:, 0, :emb_rows].reshape(1, -1)
    sigmoid = jax.nn.sigmoid(emb_float)
    grad_embedding = grad_embedding * (sigmoid * (1.0 + emb_float * (1.0 - sigmoid)))
    lane = (lax.axis_index("fsdp") * share) % 128
    gain_sums = lax.dynamic_slice(small, (0, lane), (3, share))
    return (
        output.reshape(1, rows, columns, C),
        gimage[None],
        grad_embedding,
        gtext[None],
        gain_sums[0],
        r1.reshape(-1, C),
        grad_emb_proj,
        gain_sums[1],
        r2.reshape(-1, C),
        gain_sums[2],
        joined(rq, 3),
        joined(rt, 2),
        ro.reshape(-1, C),
    )


def solution(mesh):
    weight = P("fsdp", None)
    gain = P("fsdp")
    field = P("fsdp", "sp", None, None)
    in_specs = (
        field,
        P("fsdp", None),
        P("fsdp", None, None),
        gain,
        gain,
        weight,
        weight,
        gain,
        weight,
        gain,
        weight,
        weight,
        weight,
        field,
    )
    out_specs = (
        field,
        field,
        P("fsdp", None),
        P("fsdp", None, None),
        gain,
        weight,
        weight,
        gain,
        weight,
        gain,
        weight,
        weight,
        weight,
    )
    return jax.shard_map(
        per_device, mesh=mesh, in_specs=in_specs, out_specs=out_specs, check_vma=False
    )
```

```python
import functools

import jax
import jax.numpy as jnp
from jax import lax
from jax.experimental import pallas as pl
from jax.experimental.pallas import tpu as pltpu
from jax.sharding import PartitionSpec as P

C = 512
GROUPS = 32
HEAD = 64
EPSILON = 1e-05
MASKED = -1e30
LIMIT = 60 * 1024 * 1024

F32 = jnp.float32
BF16 = jnp.bfloat16
DMA = pltpu.SemaphoreType.DMA
ANY = pl.BlockSpec(memory_space=pl.ANY)
VMEM = pl.BlockSpec(memory_space=pltpu.VMEM)
SMEM = pl.BlockSpec(memory_space=pltpu.SMEM)


def sizes_of(fsdp, sp):
    lines = sp if fsdp % (2 * sp) == 0 else 1
    return fsdp // (2 * lines), lines, 2


def remote(src, dst, send, recv, device):
    return pltpu.make_async_remote_copy(
        src, dst, send, recv, device_id=device, device_id_type=pl.DeviceIdType.MESH
    )


def greet(peers):
    barrier = pltpu.get_barrier_semaphore()
    for peer in peers:
        pl.semaphore_signal(
            barrier, inc=1, device_id=peer, device_id_type=pl.DeviceIdType.MESH
        )
    pl.semaphore_wait(barrier, len(peers))


def params(cid):
    return pltpu.CompilerParams(
        collective_id=cid, has_side_effects=True, vmem_limit_bytes=LIMIT
    )


def tiles_start(fsdp, source, dest, send, recv, pick):
    me, x = lax.axis_index("fsdp"), lax.axis_index("sp")
    copies = []
    for d in range(1, fsdp):
        to = (me + d) % fsdp
        copy = remote(pick(source, to), dest.at[me], send.at[d], recv.at[d], (to, x))
        copy.start()
        copies.append(copy)
    return copies


def span(index, rows, size):
    return pl.ds(pl.multiple_of(index * rows, 16 if rows % 16 == 0 else 8), size)


def aligned(index, *steps):
    if isinstance(index, int):
        return index
    return pl.multiple_of(index, 16 if all(step % 16 == 0 for step in steps) else 8)


class Gather:
    def __init__(self, dims, sp, entries, sems):
        self.dims, self.sp, self.entries = dims, sp, entries
        self.zsem, self.ysem, self.xsem, self.csem = sems
        zs, ys, cs = dims
        self.me, self.x = lax.axis_index("fsdp"), lax.axis_index("sp")
        self.z, self.y, self.c = self.me // (ys * cs), (self.me // cs) % ys, self.me % cs
        self.flying = []

    def dev(self, zz, yy, cc):
        return ((zz * self.dims[1] + yy) * self.dims[2] + cc, self.x)

    def launch(self, make, *args):
        make(*args).start()
        self.flying.append((make, args))

    def owner(self, dz, dy):
        zs, ys, _ = self.dims
        return (self.z - dz + zs) % zs, (self.y - dy + ys) % ys

    def split(self, a):
        return self.entries[a][2] > 1

    def piece(self, a):
        return self.x if self.split(a) else 0

    def home(self, a, zz, yy, cc, k=None):
        _, whole, h, rows, offset, stride = self.entries[a]
        index = ((zz * self.dims[1] + yy) * self.dims[2] + cc) * stride + offset
        if k is None:
            return whole.at[pl.ds(aligned(index, stride, offset), h * rows)]
        return whole.at[pl.ds(aligned(index + k * rows, stride, offset, rows), rows)]

    def mine(self, a):
        shard, _, h, rows, offset, stride = self.entries[a]
        if h * rows == stride and h == 1:
            return shard
        return shard.at[pl.ds(aligned(offset + self.piece(a) * rows, offset, rows), rows)]

    def own(self, a):
        shard, _, h, rows, offset, stride = self.entries[a]
        return shard if h * rows == stride else shard.at[offset : offset + h * rows]

    def zcopy(self, a, dz):
        return remote(
            self.mine(a),
            self.home(a, self.z, self.y, self.c, self.piece(a)),
            self.zsem.at[0, a, dz],
            self.zsem.at[1, a, dz],
            self.dev((self.z + dz) % self.dims[0], self.y, self.c),
        )

    def ycopy(self, a, dz, dy):
        zz, _ = self.owner(dz, 0)
        place = self.home(a, zz, self.y, self.c, self.piece(a))
        return remote(
            self.mine(a) if dz == 0 else place,
            place,
            self.ysem.at[0, a, dz, dy],
            self.ysem.at[1, a, dz, dy],
            self.dev(self.z, (self.y + dy) % self.dims[1], self.c),
        )

    def xcopy(self, a, dz, dy, dx):
        zz, yy = self.owner(dz, dy)
        place = self.home(a, zz, yy, self.c, self.x)
        return remote(
            place,
            place,
            self.xsem.at[0, a, dz, dy, dx],
            self.xsem.at[1, a, dz, dy, dx],
            (self.me, (self.x + dx) % self.sp),
        )

    def ccopy(self, a, dz, dy, dx):
        zz, yy = self.owner(dz, dy)
        if dz == 0 and dy == 0:
            src, dst = self.own(a), self.home(a, zz, yy, self.c)
        else:
            k = (self.x - dx + self.sp) % self.sp if self.split(a) else 0
            src = dst = self.home(a, zz, yy, self.c, k)
        return remote(
            src,
            dst,
            self.csem.at[0, a, dz, dy, dx],
            self.csem.at[1, a, dz, dy, dx],
            self.dev(self.z, self.y, 1 - self.c),
        )

    def onward(self, a, dz, dy):
        if self.split(a):
            for dx in range(1, self.sp):
                self.launch(self.xcopy, a, dz, dy, dx)
        self.launch(self.ccopy, a, dz, dy, 0)

    def start_z(self, a):
        for dz in range(1, self.dims[0]):
            self.launch(self.zcopy, a, dz)

    def start_y(self, a):
        for dy in range(1, self.dims[1]):
            self.launch(self.ycopy, a, 0, dy)
        self.launch(self.ccopy, a, 0, 0, 0)

    def from_z(self, a, dz):
        self.zcopy(a, dz).wait_recv()
        for dy in range(1, self.dims[1]):
            self.launch(self.ycopy, a, dz, dy)
        self.onward(a, dz, 0)

    def from_y(self, a, dz):
        for dy in range(1, self.dims[1]):
            self.ycopy(a, dz, dy).wait_recv()
            self.onward(a, dz, dy)

    def relay(self, a, dz):
        if 0 < dz < self.dims[0]:
            self.from_z(a, dz)
        if 0 < dz <= self.dims[0]:
            self.from_y(a, dz - 1)

    def over_x(self, a):
        if self.split(a):
            for dz in range(self.dims[0]):
                for dy in range(self.dims[1]):
                    if dz + dy:
                        for dx in range(1, self.sp):
                            self.xcopy(a, dz, dy, dx).wait_recv()
                            self.launch(self.ccopy, a, dz, dy, dx)

    def finish(self, a):
        for dz in range(self.dims[0]):
            for dy in range(self.dims[1]):
                many = self.sp if self.split(a) and dz + dy else 1
                for dx in range(many):
                    self.ccopy(a, dz, dy, dx).wait_recv()

    def drain(self):
        for make, args in self.flying:
            make(*args).wait_send()


def parts_of(rows, sp):
    return sp if rows % (16 * sp) == 0 else 1


def add_rows(rows, first, second, put):
    step = 32 if rows % 32 == 0 else (16 if rows % 16 == 0 else 8)

    def body(i, _):
        at = pl.ds(pl.multiple_of(i * step, step), step)
        put(at, first[at, :].astype(F32) + second[at, :].astype(F32))
        return 0

    lax.fori_loop(0, rows // step, body, 0)


class Sums:
    def __init__(self, dims, sp, shapes, modes, grads, own, outs, bufs, sems):
        self.dims, self.sp, self.shapes, self.modes = dims, sp, shapes, modes
        self.grads, self.own, self.outs = grads, own, outs
        self.crecvd, self.xrecvd, self.yrecvd, self.zrecvd, self.last = bufs
        self.csem, self.xsem, self.ysem, self.zsem, self.fsem, self.lsem = sems
        zs, ys, cs = dims
        self.me, self.x = lax.axis_index("fsdp"), lax.axis_index("sp")
        self.z, self.y, self.c = self.me // (ys * cs), (self.me // cs) % ys, self.me % cs
        self.flying = []

    def dev(self, zz, yy, cc):
        return ((zz * self.dims[1] + yy) * self.dims[2] + cc, self.x)

    def launch(self, copy):
        copy.start()
        self.flying.append(copy)

    def order(self):
        zs, ys, _ = self.dims
        return [(dz, dy) for dz in range(zs - 1, -1, -1) for dy in range(ys - 1, -1, -1)]

    def grad(self, a, dz, dy, cc):
        zs, ys, cs = self.dims
        h, rows, _ = self.shapes[a]
        owner = (((self.z + dz) % zs) * ys + (self.y + dy) % ys) * cs + cc
        return self.grads[a].at[span(owner, h * rows, h * rows)]

    def part(self, a, dz, dy, k):
        zs, ys, cs = self.dims
        h, rows, _ = self.shapes[a]
        if self.own[a] is not None:
            return self.own[a].at[dz, dy, span(k, rows, rows)]
        owner = (((self.z + dz) % zs) * ys + (self.y + dy) % ys) * cs + self.c
        return self.grads[a].at[span(owner * h + k, rows, rows)]

    def piece(self, a):
        return self.x if self.shapes[a][0] > 1 else 0

    def ccopy(self, a, dz, dy):
        return remote(
            self.grad(a, dz, dy, 1 - self.c),
            self.crecvd[a].at[dz, dy],
            self.csem.at[0, a, dz, dy],
            self.csem.at[1, a, dz, dy],
            self.dev(self.z, self.y, 1 - self.c),
        )

    def mine(self, a, dz, dy):
        return pltpu.make_async_copy(
            self.grad(a, dz, dy, self.c), self.own[a].at[dz, dy], self.lsem.at[a, dz, dy]
        )

    def xcopy(self, a, dz, dy, dx):
        to = (self.x + dx) % self.sp
        return remote(
            self.part(a, dz, dy, to),
            self.xrecvd[a].at[dz, dy, dx - 1],
            self.xsem.at[0, a, dz, dy, dx],
            self.xsem.at[1, a, dz, dy, dx],
            (self.me, to),
        )

    def ycopy(self, a, dz, dy):
        return remote(
            self.part(a, dz, dy, self.piece(a)),
            self.yrecvd[a].at[dz, dy - 1],
            self.ysem.at[0, a, dz, dy],
            self.ysem.at[1, a, dz, dy],
            self.dev(self.z, (self.y + dy) % self.dims[1], self.c),
        )

    def zcopy(self, a, dz):
        return remote(
            self.part(a, dz, 0, self.piece(a)),
            self.zrecvd[a].at[dz - 1],
            self.zsem.at[0, a, dz],
            self.zsem.at[1, a, dz],
            self.dev((self.z + dz) % self.dims[0], self.y, self.c),
        )

    def fcopy(self, a, dx):
        return remote(
            self.last[a].at[self.x],
            self.last[a].at[self.x],
            self.fsem.at[0, a, dx],
            self.fsem.at[1, a, dx],
            (self.me, (self.x + dx) % self.sp),
        )

    def add(self, a, first, second, target):
        def put(at, value):
            target[at, :] = value.astype(BF16)

        add_rows(self.shapes[a][1], first, second, put)

    def start(self, a):
        for dz, dy in self.order():
            self.launch(self.ccopy(a, dz, dy))
            if self.own[a] is not None:
                self.mine(a, dz, dy).start()

    def over_c(self, a):
        h, rows, _ = self.shapes[a]
        for dz, dy in self.order():
            if self.own[a] is not None:
                self.mine(a, dz, dy).wait()
            self.ccopy(a, dz, dy).wait_recv()
            for k in range(h):
                ref = self.part(a, dz, dy, k)
                self.add(a, ref, self.crecvd[a].at[dz, dy, pl.ds(k * rows, rows)], ref)
            if h > 1:
                for dx in range(1, self.sp):
                    self.launch(self.xcopy(a, dz, dy, dx))

    def over_x(self, a, dz):
        for dy in range(self.dims[1] - 1, -1, -1):
            if self.shapes[a][0] > 1:
                ref = self.part(a, dz, dy, self.x)
                for dx in range(1, self.sp):
                    self.xcopy(a, dz, dy, dx).wait_recv()
                    self.add(a, ref, self.xrecvd[a].at[dz, dy, dx - 1], ref)
            if dy:
                self.launch(self.ycopy(a, dz, dy))

    def over_y(self, a, dz):
        ref = self.part(a, dz, 0, self.piece(a))
        for dy in range(1, self.dims[1]):
            self.ycopy(a, dz, dy).wait_recv()
            self.add(a, ref, self.yrecvd[a].at[dz, dy - 1], ref)
        if dz:
            self.launch(self.zcopy(a, dz))

    def over_z(self, a):
        zs = self.dims[0]
        ref = self.part(a, 0, 0, self.piece(a))
        for dz in range(1, zs):
            self.zcopy(a, dz).wait_recv()
            target = self.last[a].at[self.x] if dz == zs - 1 else ref
            self.add(a, ref, self.zrecvd[a].at[dz - 1], target)
        if zs == 1:
            self.last[a][self.x] = ref[...]
        for dx in range(1, self.sp):
            self.launch(self.fcopy(a, dx))

    def all_x(self, a):
        for dz in range(self.dims[0] - 1, -1, -1):
            self.over_x(a, dz)

    def all_y(self, a):
        for dz in range(self.dims[0] - 1, -1, -1):
            self.over_y(a, dz)

    def both(self, a):
        zs = self.dims[0]
        for dz in range(zs - 1, -2, -1):
            if dz >= 0:
                self.over_x(a, dz)
            if dz < zs - 1:
                self.over_y(a, dz + 1)

    def finish(self, a):
        for dx in range(1, self.sp):
            self.fcopy(a, dx).wait_recv()
        if self.modes[a] == "add" and self.shapes[a][0] == 1:
            value = self.last[a][0].astype(F32)
            for k in range(1, self.sp):
                value = value + self.last[a][k].astype(F32)
            self.outs[a][0] = value
        else:
            for k in range(self.sp):
                self.outs[a][k] = self.last[a][k].astype(F32)

    def drain(self):
        for copy in self.flying:
            copy.wait_send()


def lane_groups(values):
    lane = lax.broadcasted_iota(jnp.int32, values.shape, 1)
    step = 1
    while step < C // GROUPS:
        up = pltpu.roll(values, step, 1)
        down = pltpu.roll(values, C - step, 1)
        values = values + jnp.where((lane & step) != 0, up, down)
        step *= 2
    return values


def column_sums(rows, fields):
    probe = jax.eval_shape(lambda: fields(0))

    def body(r, sums):
        return tuple(
            s + jnp.sum(v.reshape(-1, 8, C), axis=0) for s, v in zip(sums, fields(r), strict=True)
        )

    sums = lax.fori_loop(0, rows, body, tuple(jnp.zeros((8, C), F32) for _ in probe))
    return [jnp.broadcast_to(jnp.sum(s, axis=0, keepdims=True), (8, C)) for s in sums]


def stack_rows(*values):
    row = lax.broadcasted_iota(jnp.int32, (8, C), 0)
    out = jnp.zeros((8, C), F32)
    for k, value in enumerate(values):
        out = jnp.where(row == k, value, out)
    return out


class Swap:
    def __init__(self, sp, sums, ssem, hsem):
        self.sp, self.sums, self.ssem, self.hsem = sp, sums, ssem, hsem
        self.me, self.x = lax.axis_index("fsdp"), lax.axis_index("sp")

    def peers(self):
        return [(self.me, (self.x + d) % self.sp) for d in range(1, self.sp)]

    def _sums(self, k, d):
        return remote(
            self.sums.at[k, self.x],
            self.sums.at[k, self.x],
            self.ssem.at[0, k, d],
            self.ssem.at[1, k, d],
            (self.me, (self.x + d) % self.sp),
        )

    def sums_start(self, k, value):
        self.sums[k, self.x] = value
        for d in range(1, self.sp):
            self._sums(k, d).start()

    def sums_wait(self, k):
        for d in range(1, self.sp):
            self._sums(k, d).wait()
        return [self.sums[k, i] for i in range(self.sp)]

    def _up(self, k, src, dst):
        to = (self.x + self.sp - 1) % self.sp
        return remote(src, dst.at[1], self.hsem.at[0, k, 0], self.hsem.at[1, k, 0], (self.me, to))

    def _down(self, k, src, dst):
        to = (self.x + 1) % self.sp
        return remote(src, dst.at[0], self.hsem.at[0, k, 1], self.hsem.at[1, k, 1], (self.me, to))

    def edges_start(self, k, top, bottom, dst):
        @pl.when(self.x > 0)
        def _():
            self._up(k, top, dst).start()

        @pl.when(self.x < self.sp - 1)
        def _():
            self._down(k, bottom, dst).start()

    def edges_wait(self, k, top, bottom, dst):
        @pl.when(self.x > 0)
        def _():
            self._up(k, top, dst).wait_send()
            self._down(k, bottom, dst).wait_recv()

        @pl.when(self.x < self.sp - 1)
        def _():
            self._down(k, bottom, dst).wait_send()
            self._up(k, top, dst).wait_recv()


def put_shifted(dst, at, value):
    columns = value.shape[0]
    col = lax.broadcasted_iota(jnp.int32, value.shape, 0)
    dst[1, at] = value.astype(BF16)
    dst[0, at] = jnp.where(col == 0, 0.0, pltpu.roll(value, 1, 0)).astype(BF16)
    dst[2, at] = jnp.where(col == columns - 1, 0.0, pltpu.roll(value, columns - 1, 0)).astype(BF16)


def taps(rows, columns, shifted, weight, acc, back, hooks=()):
    pixels = rows * columns

    def body(t, _):
        for k, hook in enumerate(hooks):
            pl.when(t == k)(hook)
        total = None
        for dc in range(3):
            if back:
                lhs = shifted[2 - dc, pl.ds(2 - t, rows)].reshape(pixels, C)
            else:
                lhs = shifted[dc, pl.ds(t, rows)].reshape(pixels, C)
            rhs = weight[pl.ds(pl.multiple_of((3 * t + dc) * C, C), C), :]
            out = lax.dot_general(
                lhs, rhs, (((1,), (1 if back else 0,)), ((), ())), preferred_element_type=F32
            )
            total = out if total is None else total + out
        total = total.reshape(rows, columns, C)

        @pl.when(t == 0)
        def _():
            acc[...] = total

        @pl.when(t > 0)
        def _():
            acc[...] += total

        return 0

    lax.fori_loop(0, 3, body, 0)


def numbers(height, rows, columns, sp):
    x = lax.axis_index("sp")
    ids = x * rows + jnp.arange(-1, rows + 1, dtype=jnp.int32)
    valid = ((ids >= 0) & (ids < height)).astype(F32)
    count = (height * columns * (C // GROUPS)).astype(F32)
    held = jnp.clip(height - rows * jnp.arange(sp, dtype=jnp.int32), 0, rows)
    held = (held * columns * (C // GROUPS)).astype(F32)
    bias = jnp.where(jnp.arange(sp * rows, dtype=jnp.int32) < height, 0.0, MASKED).astype(F32)
    return jnp.concatenate([valid, count[None], held, held[x][None], bias])


def local_moments(rows, field, mask, held):
    (total,) = column_sums(rows, lambda r: (field(r),))
    total = lane_groups(total)
    mean = (total / jnp.maximum(held, 1.0))[:1]

    def centred(r):
        v = (field(r) - mean) * mask(r)
        return (v * v,)

    (square,) = column_sums(rows, centred)
    return stack_rows(total, lane_groups(square))


def joint_moments(members, counts, count):
    mean = members[0][:1]
    for m in members[1:]:
        mean = mean + m[:1]
    mean = mean / count
    square = None
    for m, n in zip(members, counts, strict=True):
        off = m[:1] / jnp.maximum(n, 1.0) - mean
        term = m[1:2] + n * off * off
        square = term if square is None else square + term
    return mean, lax.rsqrt(square / count + EPSILON)


def forward_kernel(dims, fsdp, sp, shapes, kinds, plan, *refs):
    n = len(shapes)
    (nums, image, tiles, table), shards, refs = refs[:4], refs[4 : 4 + n], refs[4 + n :]
    (resid_out, normed, conv_out_out, s1_out, s2_out, stats, gains, scales, got), refs = (
        refs[:9],
        refs[9:],
    )
    outs, refs = refs[:n], refs[n:]
    (w1v, w2v), bufs, refs = refs[:2], refs[2:n], refs[n:]
    (edge1, edge2, acc, sums, part, part_in), refs = refs[:6], refs[6:]
    (resid, conv_out, s1, s2), refs = refs[:4], refs[4:]
    (ssem, hsem, wsem, lsem, tsem, psem, osem), sems = refs[:7], refs[7:]
    results = [
        pltpu.make_async_copy(src, dst, osem.at[i])
        for i, (src, dst) in enumerate(
            [(s1, s1_out), (conv_out, conv_out_out), (s2, s2_out), (resid, resid_out)]
        )
    ]
    sources, wholes = shards[:2] + bufs, (w1v, w2v) + outs[2:]
    entries = [(sources[a], wholes[a], h, r, at, shapes[a][0]) for a, h, r, at in plan]
    move = Gather(dims, sp, entries, sems)
    me, x = move.me, move.x
    first_of, second_of, late = (
        [e for e, p in enumerate(plan) if min(p[0], 2) == a] for a in range(3)
    )
    rows, columns = image.shape[0], image.shape[1]
    swap = Swap(sp, sums, ssem, hsem)
    homes = [wholes[a].at[span(me, shapes[a][0], shapes[a][0])] for a in range(n)]
    loads = [pltpu.make_async_copy(shards[a], homes[a], wsem.at[a]) for a in range(2)]
    staged = []
    for a in range(2, n):
        width = shapes[a][1] // kinds[a]
        for j in range(kinds[a]):
            if shards[a].shape[1] == shapes[a][1]:
                src = shards[a]
            else:
                start = pl.multiple_of((j * sp + x) * width, 128)
                src = shards[a].at[:, pl.ds(start, width)]
            dst = bufs[a - 2].at[:, j * width : (j + 1) * width]
            staged.append(pltpu.make_async_copy(src, dst, lsem.at[a, j]))
    for load in loads + staged:
        load.start()
    edge1[...] = jnp.zeros_like(edge1)
    edge2[...] = jnp.zeros_like(edge2)
    greet(swap.peers() + [((me + d) % fsdp, x) for d in range(1, fsdp)])
    first_tiles = tiles_start(
        fsdp, tiles, got, tsem.at[0], tsem.at[1], lambda ref, to: ref.at[to]
    )
    got[me] = tiles[me]
    for e in first_of:
        move.start_y(e)
        move.start_z(e)
    swap.edges_start(0, image.at[0], image.at[rows - 1], edge1)
    count = nums[rows + 2]
    counts = [nums[rows + 3 + i] for i in range(sp)]
    held = nums[rows + 3 + sp]

    def mask(r):
        return nums[r + 1]

    def masked(r):
        return image[r].astype(F32) * mask(r)

    swap.sums_start(0, local_moments(rows, masked, mask, held))
    for copy in staged:
        copy.wait()
    for e in first_of:
        move.relay(e, 1)
    stores = [pltpu.make_async_copy(bufs[a - 2], homes[a], wsem.at[a]) for a in range(2, n)]
    for copy in stores:
        copy.start()
    for copy in first_tiles:
        copy.wait_recv()
    share = C // fsdp
    many = 128 // share
    for b in range(C // 128):
        block = got[b * many]
        for f in range(b * many + 1, (b + 1) * many):
            block = block + got[f]
        gains[:, b * 128 : (b + 1) * 128] = block
    act = got[:, 0, :].astype(BF16)
    for j in range(8):
        part[:, j, :] = jnp.dot(
            act, table[:, j * 128 : (j + 1) * 128], preferred_element_type=F32
        )
    part_in[me] = part[me]
    second_tiles = tiles_start(
        fsdp, part, part_in, psem.at[0], psem.at[1], lambda ref, to: ref.at[to]
    )
    for e in second_of + late:
        move.start_z(e)
    mean1, inv1 = joint_moments(swap.sums_wait(0), counts, count)
    swap.edges_wait(0, image.at[0], image.at[rows - 1], edge1)
    g1, g2, g3 = gains[1:2], gains[2:3], gains[3:4]

    def first(at, value):
        m = nums[at]
        hidden = (value.astype(F32) * m - mean1) * m * inv1 * g1
        put_shifted(s1, at, hidden * jax.nn.sigmoid(hidden) * m)

    lax.fori_loop(0, rows, lambda r, _: (first(r + 1, image[r]), 0)[1], 0)
    first(0, edge1[0])
    first(rows + 1, edge1[1])
    results[0].start()
    for dz in range(2, dims[0] + 1):
        for e in first_of:
            move.relay(e, dz)
    for e in second_of:
        move.start_y(e)
        move.relay(e, 1)
    for e in first_of:
        move.over_x(e)
    loads[0].wait()
    for e in first_of:
        move.finish(e)
    pltpu.make_async_copy(w1v, outs[0], wsem.at[0]).start()

    def along(group, dz):
        for e in group:
            move.relay(e, dz)

    zs = dims[0]
    hooks = [functools.partial(along, second_of, dz) for dz in range(2, min(4, zs + 1))]
    taps(rows, columns, s1, w1v, acc, False, hooks)
    for dz in range(len(hooks) + 2, zs + 1):
        along(second_of, dz)
    for e in late:
        move.start_y(e)

    def keep(r, _):
        conv_out[r] = acc[r] * mask(r)
        return 0

    lax.fori_loop(0, rows, keep, 0)
    results[1].start()
    swap.edges_start(1, conv_out.at[0], conv_out.at[rows - 1], edge2)
    swap.sums_start(1, local_moments(rows, lambda r: conv_out[r], mask, held))
    along(late, 1)
    along(late, 2)
    mean2, inv2 = joint_moments(swap.sums_wait(1), counts, count)
    swap.edges_wait(1, conv_out.at[0], conv_out.at[rows - 1], edge2)
    for copy in second_tiles:
        copy.wait_recv()
    total = part_in[0]
    for f in range(1, fsdp):
        total = total + part_in[f]
    scales[...] = jnp.zeros_like(scales)
    for j in range(8):
        lanes = slice(j % 4 * 128, (j % 4 + 1) * 128)
        scales[j // 4 : j // 4 + 1, lanes] = total[j : j + 1]
    scale, shift = 1.0 + scales[0:1], scales[1:2]

    def second(at, value):
        m = nums[at]
        hidden = (value - mean2) * m * inv2 * g2 * scale + shift
        put_shifted(s2, at, hidden * jax.nn.sigmoid(hidden) * m)

    lax.fori_loop(0, rows, lambda r, _: (second(r + 1, conv_out[r]), 0)[1], 0)
    second(0, edge2[0])
    second(rows + 1, edge2[1])
    results[2].start()
    along(late, 3)
    for e in second_of:
        move.over_x(e)
    loads[1].wait()
    for e in second_of:
        move.finish(e)
    pltpu.make_async_copy(w2v, outs[1], wsem.at[1]).start()
    taps(rows, columns, s2, w2v, acc, False)
    for dz in range(4, zs + 1):
        along(late, dz)

    def add(r, _):
        resid[r] = masked(r) + acc[r] * mask(r)
        return 0

    lax.fori_loop(0, rows, add, 0)
    results[3].start()
    swap.sums_start(2, local_moments(rows, lambda r: resid[r], mask, held))
    mean3, inv3 = joint_moments(swap.sums_wait(2), counts, count)

    def third(r, _):
        normed[r] = ((resid[r] - mean3) * mask(r) * inv3 * g3).astype(BF16)
        return 0

    lax.fori_loop(0, rows, third, 0)
    stats[...] = stack_rows(mean1, inv1, mean2, inv2, mean3, inv3)
    for e in late:
        move.over_x(e)
    for e in late:
        move.finish(e)
    for copy in stores + results:
        copy.wait()
    for copy in first_tiles + second_tiles:
        copy.wait_send()
    move.drain()
    pltpu.make_async_copy(w1v, outs[0], wsem.at[0]).wait()
    pltpu.make_async_copy(w2v, outs[1], wsem.at[1]).wait()


def forward(nums, image, tiles, table, shards, kinds, fsdp, sp):
    rows, columns, _ = image.shape
    field = (rows, columns, C)
    shifted = (3, rows + 2, columns, C)
    dims = sizes_of(fsdp, sp)
    zs, ys, _ = dims
    n = len(shards)
    shapes, plan = [], []
    for a, (shard, kind) in enumerate(zip(shards, kinds, strict=True)):
        r, width = shard.shape
        shapes.append((r, width // sp if kind else width))
        h = 1 if kind else parts_of(r, sp)
        plan.append((a, h, r // h, 0))
    m = len(plan)
    wholes = [jax.ShapeDtypeStruct((fsdp * r, w), BF16) for r, w in shapes]
    staged = [pltpu.VMEM(shape, BF16) for shape in shapes[2:]]
    tile = pltpu.VMEM((fsdp, 8, 128), F32)
    return pl.pallas_call(
        functools.partial(
            forward_kernel, dims, fsdp, sp, shapes, [max(k, 1) for k in kinds], plan
        ),
        out_shape=[
            jax.ShapeDtypeStruct(field, F32),
            jax.ShapeDtypeStruct(field, BF16),
            jax.ShapeDtypeStruct(field, F32),
            jax.ShapeDtypeStruct(shifted, BF16),
            jax.ShapeDtypeStruct(shifted, BF16),
            jax.ShapeDtypeStruct((8, C), F32),
            jax.ShapeDtypeStruct((8, C), F32),
            jax.ShapeDtypeStruct((8, C), F32),
            jax.ShapeDtypeStruct((fsdp, 8, 128), F32),
        ]
        + wholes,
        in_specs=[SMEM] + [VMEM] * 3 + [ANY] * n,
        out_specs=[ANY, VMEM, ANY, ANY, ANY] + [VMEM] * 4 + [ANY] * n,
        scratch_shapes=[
            pltpu.VMEM(wholes[0].shape, BF16),
            pltpu.VMEM(wholes[1].shape, BF16),
        ]
        + staged
        + [
            pltpu.VMEM((2, columns, C), BF16),
            pltpu.VMEM((2, columns, C), F32),
            pltpu.VMEM(field, F32),
            pltpu.VMEM((3, sp, 8, C), F32),
            tile,
            tile,
            pltpu.VMEM(field, F32),
            pltpu.VMEM(field, F32),
            pltpu.VMEM(shifted, BF16),
            pltpu.VMEM(shifted, BF16),
            DMA((2, 3, sp)),
            DMA((2, 2, 2)),
            DMA((n,)),
            DMA((n, 3)),
            DMA((2, fsdp)),
            DMA((2, fsdp)),
            DMA((4,)),
            DMA((2, m, zs)),
            DMA((2, m, zs, ys)),
            DMA((2, m, zs, ys, sp)),
            DMA((2, m, zs, ys, sp)),
        ],
        compiler_params=params(1),
        name="forward",
    )(nums, image, tiles, table, *shards)


def attention_kernel(sp, heads, *refs):
    (nums, normed, text_in, wq, wt_in, wo, cot, resid_in), refs = refs[:8], refs[8:]
    (output_out, gnorm, gq_out, gt_out, go_out, gtext_out), refs = refs[:6], refs[6:]
    (nall, gown, gall, qkv, keys, values, dk, dv, att, attin, dqkv, gtkv, gpart, grecv, low), refs = (
        refs[:15],
        refs[15:],
    )
    (text, wt, resid, output, gq, gt, go, gtext), refs = refs[:8], refs[8:]
    nsem, gsem, asem, psem, isem, osem = refs
    load_text, load_wt, load_resid = (
        pltpu.make_async_copy(src, dst, isem.at[i])
        for i, (src, dst) in enumerate([(text_in, text), (wt_in, wt), (resid_in, resid)])
    )
    results = [
        pltpu.make_async_copy(src, dst, osem.at[i])
        for i, (src, dst) in enumerate(
            [(gtext, gtext_out), (output, output_out), (go, go_out), (gq, gq_out), (gt, gt_out)]
        )
    ]
    for load in (load_text, load_wt, load_resid):
        load.start()
    rows, columns = cot.shape[0], cot.shape[1]
    pixels = rows * columns
    width = heads * HEAD
    total_px = sp * pixels
    me, x = lax.axis_index("fsdp"), lax.axis_index("sp")
    factor = HEAD**-0.5
    greet([(me, (x + d) % sp) for d in range(1, sp)])

    def send(pair, src, dst):
        def copy(d):
            to = (x + d) % sp
            return remote(src(to), dst.at[x], pair.at[0, d], pair.at[1, d], (me, to))

        return [copy(d) for d in range(1, sp)]

    def start(copies):
        for copy in copies:
            copy.start()

    def wait(copies):
        for copy in copies:
            copy.wait()

    moves = send(nsem, lambda to: normed, nall)
    start(moves)

    def lower(r, _):
        low[r] = (cot[r].astype(F32) * nums[r + 1]).astype(BF16)
        return 0

    lax.fori_loop(0, rows, lower, 0)
    low2 = low[...].reshape(pixels, C)
    for k in range(sp):
        gown[k] = lax.dot_general(
            low2,
            wo[k * width : (k + 1) * width, :],
            (((1,), (1,)), ((), ())),
            preferred_element_type=F32,
        ).astype(BF16)
    gmoves = send(gsem, lambda to: gown.at[to], gall)
    start(gmoves)
    gall[x] = gown[x]
    nall[x] = normed[...]
    load_text.wait()
    load_wt.wait()
    text_kv = jnp.dot(text[...], wt[...], preferred_element_type=F32).astype(BF16)
    keys[total_px:, :] = text_kv[:, :width]
    values[total_px:, :] = text_kv[:, width:]

    def project(k):
        out = jnp.dot(nall[k], wq[...], preferred_element_type=F32).astype(BF16)
        at = pl.ds(pl.multiple_of(k * pixels, pixels), pixels)
        qkv[at, :] = out
        keys[at, :] = out[:, width : 2 * width]
        values[at, :] = out[:, 2 * width :]

    project(x)
    wait(moves)
    for d in range(1, sp):
        project((x + d) % sp)
    wait(gmoves)

    block = 256
    per = pixels // block
    for h in range(heads):
        lanes = slice(h * HEAD, (h + 1) * HEAD)
        kh, vh = keys[:, lanes], values[:, lanes]
        kt, vt = kh.T, vh.T
        dk[...] = jnp.zeros_like(dk)
        dv[...] = jnp.zeros_like(dv)

        def step(j, _, lanes=lanes, kh=kh, vh=vh, kt=kt, vt=vt):
            at = pl.ds(pl.multiple_of(j * block, block), block)
            inner = pl.ds(pl.multiple_of((j % per) * block, block), block)
            q = qkv[at, lanes]
            g = gall[j // per, inner, lanes]
            s = (
                lax.dot_general(kh, q, (((1,), (1,)), ((), ())), preferred_element_type=F32)
                * factor
            )
            pieces = [
                s[r * columns : (r + 1) * columns] + nums[rows + 4 + sp + r]
                for r in range(sp * rows)
            ]
            s = jnp.concatenate(pieces + [s[total_px:]], axis=0)
            raised = jnp.exp(s - jnp.max(s, axis=0, keepdims=True))
            chances = raised * (1.0 / jnp.sum(raised, axis=0, keepdims=True))
            short = chances.astype(BF16)
            att[j // per, inner, lanes] = jnp.dot(
                vt, short, preferred_element_type=F32
            ).T.astype(BF16)
            slope = lax.dot_general(vh, g, (((1,), (1,)), ((), ())), preferred_element_type=F32)
            mean = jnp.sum(chances * slope, axis=0, keepdims=True)
            grad = (chances * (slope - mean)).astype(BF16)
            dqkv[at, lanes] = (jnp.dot(kt, grad, preferred_element_type=F32) * factor).T.astype(
                BF16
            )
            dk[...] += jnp.dot(grad, q, preferred_element_type=F32)
            dv[...] += jnp.dot(short, g, preferred_element_type=F32)
            return 0

        lax.fori_loop(0, sp * per, step, 0)
        low_k = (dk[...] * factor).astype(BF16)
        low_v = dv[...].astype(BF16)
        dqkv[:, width + h * HEAD : width + (h + 1) * HEAD] = low_k[:total_px]
        dqkv[:, 2 * width + h * HEAD : 2 * width + (h + 1) * HEAD] = low_v[:total_px]
        gtkv[:, h * HEAD : (h + 1) * HEAD] = low_k[total_px:]
        gtkv[:, width + h * HEAD : width + (h + 1) * HEAD] = low_v[total_px:]

    amoves = send(asem, lambda to: att.at[to], attin)
    start(amoves)
    attin[x] = att[x]

    def to_normed(k):
        at = pl.ds(pl.multiple_of(k * pixels, pixels), pixels)
        return lax.dot_general(
            dqkv[at, :], wq[...], (((1,), (1,)), ((), ())), preferred_element_type=F32
        )

    for d in range(1, sp):
        to = (x + d) % sp
        gpart[to] = to_normed(to).astype(BF16)
    pmoves = send(psem, lambda to: gpart.at[to], grecv)
    start(pmoves)
    gtext[...] = lax.dot_general(
        gtkv[...], wt[...], (((1,), (1,)), ((), ())), preferred_element_type=F32
    ).astype(BF16)
    results[0].start()
    gnorm[...] = to_normed(x)
    load_resid.wait()
    wait(amoves)
    joined = jnp.concatenate([attin[k] for k in range(sp)], axis=1)
    branch = jnp.dot(joined, wo[...], preferred_element_type=F32)
    for r in range(rows):
        at = slice(r * columns, (r + 1) * columns)
        output[at, :] = (resid[at, :] + branch[at] * nums[r + 1]).astype(BF16)
    results[1].start()
    down = (((0,), (0,)), ((), ()))
    go[...] = lax.dot_general(joined, low2, down, preferred_element_type=F32).astype(BF16)
    results[2].start()
    gq[...] = lax.dot_general(
        nall[...].reshape(total_px, C), dqkv[...], down, preferred_element_type=F32
    ).astype(BF16)
    results[3].start()
    gt[...] = lax.dot_general(text[...], gtkv[...], down, preferred_element_type=F32).astype(BF16)
    results[4].start()
    wait(pmoves)
    for d in range(1, sp):
        gnorm[...] += grecv[(x + d) % sp].astype(F32)
    for copy in results:
        copy.wait()


def attention(nums, normed, text, wq, wt, wo, cot, resid, sp):
    rows, columns, _ = cot.shape
    pixels = rows * columns
    heads = C // HEAD // sp
    width = heads * HEAD
    tokens = text.shape[0]
    n_keys = sp * pixels + tokens
    return pl.pallas_call(
        functools.partial(attention_kernel, sp, heads),
        out_shape=[
            jax.ShapeDtypeStruct((pixels, C), BF16),
            jax.ShapeDtypeStruct((pixels, C), F32),
            jax.ShapeDtypeStruct(wq.shape, BF16),
            jax.ShapeDtypeStruct(wt.shape, BF16),
            jax.ShapeDtypeStruct(wo.shape, BF16),
            jax.ShapeDtypeStruct(text.shape, BF16),
        ],
        in_specs=[SMEM, VMEM, ANY, VMEM, ANY, VMEM, VMEM, ANY],
        out_specs=[ANY, VMEM, ANY, ANY, ANY, ANY],
        scratch_shapes=[
            pltpu.VMEM((sp, pixels, C), BF16),
            pltpu.VMEM((sp, pixels, width), BF16),
            pltpu.VMEM((sp, pixels, width), BF16),
            pltpu.VMEM((sp * pixels, 3 * width), BF16),
            pltpu.VMEM((n_keys, width), BF16),
            pltpu.VMEM((n_keys, width), BF16),
            pltpu.VMEM((n_keys, HEAD), F32),
            pltpu.VMEM((n_keys, HEAD), F32),
            pltpu.VMEM((sp, pixels, width), BF16),
            pltpu.VMEM((sp, pixels, width), BF16),
            pltpu.VMEM((sp * pixels, 3 * width), BF16),
            pltpu.VMEM((tokens, 2 * width), BF16),
            pltpu.VMEM((sp, pixels, C), BF16),
            pltpu.VMEM((sp, pixels, C), BF16),
            pltpu.VMEM((rows, columns, C), BF16),
            pltpu.VMEM(text.shape, BF16),
            pltpu.VMEM(wt.shape, BF16),
            pltpu.VMEM((pixels, C), F32),
            pltpu.VMEM((pixels, C), BF16),
            pltpu.VMEM(wq.shape, BF16),
            pltpu.VMEM(wt.shape, BF16),
            pltpu.VMEM(wo.shape, BF16),
            pltpu.VMEM(text.shape, BF16),
        ]
        + [DMA((2, sp))] * 4
        + [DMA((3,)), DMA((5,))],
        compiler_params=params(2),
        name="attention",
    )(nums, normed, text, wq, wt, wo, cot, resid)


def backward_kernel(dims, fsdp, sp, shapes, modes, *refs):
    n = len(shapes)
    (nums, image_in, gains, scales, stats, resid, conv_in, s1_in, s2_in, gnorm, cot), refs = (
        refs[:11],
        refs[11:],
    )
    (table, tpart, w1, w2), refs = refs[:4], refs[4:]
    attn, refs = refs[: n - 2], refs[n - 2 :]
    outs, gimage, gscales, etiles, gtotal, gtext, refs = refs[:n], *refs[n : n + 5], refs[n + 5 :]
    (w1v, w2v, out1, out2, p1, p2, edge1, edge2, gres, acc, sums, mine, every, pieces, got_e), refs = (
        refs[:15],
        refs[15:],
    )
    (ggains, got_g, gsmall, trecv, image, conv_out, s1, s2), refs = refs[:8], refs[8:]
    own, refs = (None, None) + tuple(refs[: n - 2]), refs[n - 2 :]
    bufs, refs = [refs[i * n : (i + 1) * n] for i in range(5)], refs[5 * n :]
    (ssem, hsem, wsem, tsem, esem, gsem, rsem, xsem, isem), sems = refs[:9], refs[9:]
    load_s2, load_conv, load_s1, load_image = (
        pltpu.make_async_copy(src, dst, isem.at[i])
        for i, (src, dst) in enumerate(
            [(s2_in, s2), (conv_in, conv_out), (s1_in, s1), (image_in, image)]
        )
    )
    load_s2.start()
    total_of = Sums(dims, sp, shapes, modes, (out1, out2) + tuple(attn), own, outs, bufs, sems)
    rows, columns = image.shape[0], image.shape[1]
    pixels = rows * columns
    me, x = lax.axis_index("fsdp"), lax.axis_index("sp")
    swap = Swap(sp, sums, ssem, hsem)
    load1 = pltpu.make_async_copy(w1, w1v, wsem.at[0])
    load2 = pltpu.make_async_copy(w2, w2v, wsem.at[1])
    load2.start()
    for load in (load_conv, load_s1, load1, load_image):
        load.start()
    edge1[...] = jnp.zeros_like(edge1)
    edge2[...] = jnp.zeros_like(edge2)
    greet(swap.peers() + [((me + d) % fsdp, x) for d in range(1, fsdp)])
    late = list(range(2, n))
    for a in late:
        total_of.start(a)
    count = nums[rows + 2]
    g1, g2, g3 = gains[1:2], gains[2:3], gains[3:4]
    mean1, inv1, mean2, inv2, mean3, inv3 = (stats[k : k + 1] for k in range(6))

    def mask(r):
        return nums[r + 1]

    def joint(k):
        members = swap.sums_wait(k)
        total = members[0]
        for m in members[1:]:
            total = total + m
        return total

    def weight_grad(shifted, padded, store):
        grad = padded[1, 1 : rows + 1].reshape(pixels, C)

        def body(t, _):
            for dc in range(3):
                lhs = shifted[dc, pl.ds(t, rows)].reshape(pixels, C)
                at = pl.ds(pl.multiple_of((3 * t + dc) * C, C), C)
                store[at, :] = lax.dot_general(
                    lhs, grad, (((0,), (0,)), ((), ())), preferred_element_type=F32
                ).astype(BF16)
            return 0

        lax.fori_loop(0, 3, body, 0)

    def hat3(r):
        return (resid[r] - mean3) * mask(r) * inv3

    def from_three(r):
        g = gnorm[r] * mask(r)
        return g, g * hat3(r)

    plain, crossed = column_sums(rows, from_three)
    gain3 = crossed
    swap.sums_start(0, stack_rows(lane_groups(plain * g3), lane_groups(crossed * g3)))
    total = joint(0) / count
    m1, m2 = total[0:1], total[1:2]

    def residual(r, _):
        m = mask(r)
        e = gnorm[r] * m * g3
        value = cot[r].astype(F32) * m + m * inv3 * (e - m1 - hat3(r) * m2)
        gres[r] = value
        put_shifted(p2, r + 1, value * m)
        return 0

    lax.fori_loop(0, rows, residual, 0)
    swap.edges_start(0, p2.at[1, 1], p2.at[1, rows], edge2)
    tmoves = []
    for d in range(1, sp):
        to = (me, (x + d) % sp)
        tmoves.append(remote(tpart, trecv.at[d - 1], xsem.at[0, d], xsem.at[1, d], to))
        tmoves[-1].start()
    load_s2.wait()
    weight_grad(s2, p2, out2)
    total_of.start(1)
    for a in late:
        total_of.over_c(a)
        if shapes[a][0] == 1:
            total_of.all_x(a)
    swap.edges_wait(0, p2.at[1, 1], p2.at[1, rows], edge2)
    put_shifted(p2, 0, edge2[0].astype(F32))
    put_shifted(p2, rows + 1, edge2[1].astype(F32))
    load2.wait()
    taps(rows, columns, p2, w2v, acc, True)
    total_of.over_c(1)
    total_of.all_x(1)
    scale, shift = 1.0 + scales[0:1], scales[1:2]

    def hat2(r):
        return (conv_out[r] - mean2) * mask(r) * inv2

    def slope(value):
        s = jax.nn.sigmoid(value)
        return s * (1.0 + value * (1.0 - s))

    def from_two(r):
        hat = hat2(r)
        g = acc[r] * mask(r) * slope(hat * g2 * scale + shift)
        acc[r] = g
        return g, g * hat

    load_conv.wait()
    plain, crossed = column_sums(rows, from_two)
    gain2 = crossed * scale
    swap.sums_start(
        1,
        stack_rows(
            lane_groups(plain * (scale * g2)),
            lane_groups(crossed * (scale * g2)),
            crossed * g2,
            plain,
        ),
    )
    total = joint(1)
    for k in range(8):
        row = 2 + k // 4
        lanes = slice((k % 4) * 128, (k % 4 + 1) * 128)
        mine[k : k + 1, :] = total[row : row + 1, lanes].astype(BF16).astype(F32)
    copies = tiles_start(fsdp, mine, every, tsem.at[0], tsem.at[1], lambda ref, to: ref)
    every[me] = mine[...]
    m1, m2 = total[0:1] / count, total[1:2] / count

    def middle(r, _):
        m = mask(r)
        value = m * inv2 * (acc[r] * (scale * g2) - m1 - hat2(r) * m2)
        put_shifted(p1, r + 1, value)
        return 0

    lax.fori_loop(0, rows, middle, 0)
    swap.edges_start(1, p1.at[1, 1], p1.at[1, rows], edge1)
    for a in late:
        if shapes[a][0] > 1:
            total_of.all_x(a)
    load_s1.wait()
    weight_grad(s1, p1, out1)
    total_of.start(0)
    for a in late:
        if shapes[a][0] == 1:
            total_of.all_y(a)
    swap.edges_wait(1, p1.at[1, 1], p1.at[1, rows], edge1)
    put_shifted(p1, 0, edge1[0].astype(F32))
    put_shifted(p1, rows + 1, edge1[1].astype(F32))
    load1.wait()
    total_of.over_c(0)
    taps(rows, columns, p1, w1v, acc, True)

    def hat1(r):
        return (image[r].astype(F32) * mask(r) - mean1) * mask(r) * inv1

    def from_one(r):
        hat = hat1(r)
        g = acc[r] * mask(r) * slope(hat * g1)
        acc[r] = g
        return g, g * hat

    load_image.wait()
    plain, crossed = column_sums(rows, from_one)
    swap.sums_start(2, stack_rows(lane_groups(plain * g1), lane_groups(crossed * g1)))
    ggains[...] = stack_rows(crossed, gain2, gain3)
    share = C // fsdp

    def gain_block(ref, to):
        return ref.at[:, pl.ds(pl.multiple_of((to * share) // 128 * 128, 128), 128)]

    gcopies = tiles_start(fsdp, ggains, got_g, gsem.at[0], gsem.at[1], gain_block)
    got_g[me] = ggains[:, pl.ds(pl.multiple_of((me * share) // 128 * 128, 128), 128)]
    total_of.all_y(1)
    for a in late:
        if shapes[a][0] > 1:
            total_of.all_y(a)
    for copy in copies:
        copy.wait()
    gscales[...] = every[...]
    piece = None
    for j in range(8):
        term = lax.dot_general(
            every[:, j, :].astype(BF16),
            table[:, j * 128 : (j + 1) * 128],
            (((1,), (1,)), ((), ())),
            preferred_element_type=F32,
        )
        piece = term if piece is None else piece + term
    pieces[...] = jnp.broadcast_to(piece[:, None, :], pieces.shape)
    ecopies = tiles_start(fsdp, pieces, got_e, esem.at[0], esem.at[1], lambda ref, to: ref.at[to])
    got_e[me] = pieces[me]
    total_of.both(0)
    for a in late:
        total_of.over_z(a)
    total = joint(2) / count
    m1, m2 = total[0:1], total[1:2]

    def final(r, _):
        m = mask(r)
        gimage[r] = (gres[r] + m * inv1 * (acc[r] * g1 - m1 - hat1(r) * m2)) * m
        return 0

    lax.fori_loop(0, rows, final, 0)
    total_of.over_z(1)
    for copy in tmoves:
        copy.wait()
    text_rows = 32

    def text_sum(r, _):
        at = span(r, text_rows, text_rows)
        value = tpart[at, :].astype(F32)
        for i in range(sp - 1):
            value = value + trecv[i, at, :].astype(F32)
        gtext[at, :] = value
        return 0

    lax.fori_loop(0, tpart.shape[0] // text_rows, text_sum, 0)
    for copy in gcopies:
        copy.wait()
    total = got_g[0]
    for f in range(1, fsdp):
        total = total + got_g[f]
    gsmall[x] = total

    def small_copy(d):
        to = (me, (x + d) % sp)
        return remote(gsmall.at[x], gsmall.at[x], rsem.at[0, d], rsem.at[1, d], to)

    for d in range(1, sp):
        small_copy(d).start()
    for a in late:
        total_of.finish(a)
    for copy in ecopies:
        copy.wait()
    etiles[...] = got_e[...]
    for d in range(1, sp):
        small_copy(d).wait()
    total = gsmall[0]
    for i in range(1, sp):
        total = total + gsmall[i]
    gtotal[...] = total
    total_of.over_z(0)
    total_of.finish(1)
    total_of.finish(0)
    total_of.drain()


def backward(
    nums, image, gains, scales, stats, resid, conv_out, s1, s2, gnorm, cot, table, tpart, w1, w2, attn, fsdp, sp
):
    rows, columns, _ = image.shape
    field = (rows, columns, C)
    shifted = (3, rows + 2, columns, C)
    dims = sizes_of(fsdp, sp)
    zs, ys, _ = dims
    shapes, outs = [], []
    grads = [w1, w2] + [g for g, _ in attn]
    modes = ["add", "add"] + [m for _, m in attn]
    for a, (grad, mode) in enumerate(zip(grads, modes, strict=True)):
        r, width = grad.shape[0] // fsdp, grad.shape[1]
        h = parts_of(r, sp) if mode == "add" and a != 1 else 1
        shapes.append((h, r // h, width))
        copies = 1 if mode == "add" and h == 1 else sp
        outs.append(jax.ShapeDtypeStruct((copies, r // h, width), F32))
    count = len(grads)

    def scratch(*shape):
        return pltpu.VMEM(shape, BF16)

    tile = jax.ShapeDtypeStruct((fsdp, 8, 128), F32)
    tiles = pltpu.VMEM((fsdp, 8, 128), F32)
    return pl.pallas_call(
        functools.partial(backward_kernel, dims, fsdp, sp, shapes, modes),
        out_shape=outs
        + [jax.ShapeDtypeStruct(field, F32), tile, tile, jax.ShapeDtypeStruct((8, 128), F32)]
        + [jax.ShapeDtypeStruct(tpart.shape, F32)],
        in_specs=[SMEM, ANY, VMEM, VMEM, VMEM, VMEM, ANY, ANY, ANY] + [VMEM] * 4 + [ANY] * count,
        out_specs=[VMEM] * (count + 5),
        scratch_shapes=[
            scratch(*w1.shape),
            scratch(*w2.shape),
            scratch(*w1.shape),
            scratch(*w2.shape),
            scratch(*shifted),
            scratch(*shifted),
            scratch(2, columns, C),
            scratch(2, columns, C),
            pltpu.VMEM(field, F32),
            pltpu.VMEM(field, F32),
            pltpu.VMEM((3, sp, 8, C), F32),
            pltpu.VMEM((8, 128), F32),
            tiles,
            tiles,
            tiles,
            pltpu.VMEM((8, C), F32),
            tiles,
            pltpu.VMEM((sp, 8, 128), F32),
            scratch(max(sp - 1, 1), *tpart.shape),
            scratch(*field),
            pltpu.VMEM(field, F32),
            scratch(*shifted),
            scratch(*shifted),
        ]
        + [scratch(zs, ys, s[0] * s[1], s[2]) for s in shapes[2:]]
        + [scratch(zs, ys, s[0] * s[1], s[2]) for s in shapes]
        + [
            scratch(zs, ys, sp - 1, *s[1:]) if s[0] > 1 else scratch(1, 1, 1, 16, 128)
            for s in shapes
        ]
        + [scratch(zs, max(ys - 1, 1), *s[1:]) for s in shapes]
        + [scratch(max(zs - 1, 1), *s[1:]) for s in shapes]
        + [scratch(sp, *s[1:]) for s in shapes]
        + [
            DMA((2, 3, sp)),
            DMA((2, 2, 2)),
            DMA((2,)),
            DMA((2, fsdp)),
            DMA((2, fsdp)),
            DMA((2, fsdp)),
            DMA((2, sp)),
            DMA((2, sp)),
            DMA((4,)),
            DMA((2, count, zs, ys)),
            DMA((2, count, zs, ys, sp)),
            DMA((2, count, zs, ys)),
            DMA((2, count, zs)),
            DMA((2, count, sp)),
            DMA((count, zs, ys)),
        ],
        compiler_params=params(3),
        name="backward",
    )(
        nums, image, gains, scales, stats, resid, conv_out, s1, s2, gnorm, cot, table, tpart, w1, w2,
        *[g for g, _ in attn],
    )


def per_device(
    image,
    embedding,
    text,
    heights,
    gain_one,
    conv_one,
    emb_proj,
    gain_two,
    conv_two,
    gain_three,
    qkv_proj,
    text_proj,
    out_proj,
    cotangent,
):
    rows, columns = image.shape[1], image.shape[2]
    fsdp, sp = lax.axis_size("fsdp"), lax.axis_size("sp")
    heads = C // HEAD // sp
    width = heads * HEAD
    share = gain_one.shape[0]
    emb_rows = emb_proj.shape[0]
    nums = numbers(heights[0], rows, columns, sp)
    emb_float = embedding.astype(F32)
    emb_act = jax.nn.silu(emb_float).astype(BF16)

    def lanes(array):
        return jnp.pad(array, [(0, 0)] * (array.ndim - 1) + [(0, 128 - array.shape[-1])])

    many = 128 // share
    place = lax.broadcasted_iota(jnp.int32, (3, 128), 1) // share == lax.axis_index("fsdp") % many
    gain_rows = jnp.stack([gain_one, gain_two, gain_three]).astype(F32)
    gain_rows = jnp.where(place, jnp.tile(gain_rows, (1, many)), 0.0)
    tiles = jnp.concatenate(
        [
            lanes(emb_act.astype(F32).reshape(fsdp, 1, emb_rows)),
            jnp.broadcast_to(gain_rows[None], (fsdp, 3, 128)),
            jnp.zeros((fsdp, 4, 128), F32),
        ],
        axis=1,
    )
    table = jnp.pad(emb_proj, ((0, 128 - emb_rows), (0, 0)))
    resid, normed, conv_out, s1, s2, stats, gains, scales, tiles_in, w1, w2, wt, wq, wo = forward(
        nums,
        image[0],
        tiles,
        table,
        [conv_one, conv_two, text_proj, qkv_proj, out_proj],
        [0, 0, 2, 3, 0],
        fsdp,
        sp,
    )
    emb_cols = tiles_in[:, 0, :emb_rows].astype(BF16)
    pixels = rows * columns
    output, gnorm, gq, gt, go, tpart = attention(
        nums,
        normed.reshape(pixels, C),
        text[0],
        wq,
        wt,
        wo,
        cotangent[0],
        resid.reshape(pixels, C),
        sp,
    )
    (r1, r2, rt, rq, ro, gimage, every, tiles_in, small, gtext) = backward(
        nums,
        image[0],
        gains,
        scales,
        stats,
        resid,
        conv_out,
        s1,
        s2,
        gnorm.reshape(rows, columns, C),
        cotangent[0],
        table,
        tpart,
        w1,
        w2,
        [(gt, "join"), (gq, "join"), (go, "add")],
        fsdp,
        sp,
    )
    grad_scales = every.reshape(fsdp, 2 * C).astype(BF16)
    grad_emb_proj = lax.dot_general(
        emb_cols, grad_scales, (((0,), (0,)), ((), ())), preferred_element_type=F32
    )

    def joined(result, kinds):
        n = result.shape[1]
        return result.reshape(sp, n, kinds, width).transpose(1, 2, 0, 3).reshape(n, kinds * C)

    grad_embedding = tiles_in[:, 0, :emb_rows].reshape(1, -1)
    sigmoid = jax.nn.sigmoid(emb_float)
    grad_embedding = grad_embedding * (sigmoid * (1.0 + emb_float * (1.0 - sigmoid)))
    lane = (lax.axis_index("fsdp") * share) % 128
    gain_sums = lax.dynamic_slice(small, (0, lane), (3, share))
    return (
        output.reshape(1, rows, columns, C),
        gimage[None],
        grad_embedding,
        gtext[None],
        gain_sums[0],
        r1.reshape(-1, C),
        grad_emb_proj,
        gain_sums[1],
        r2.reshape(-1, C),
        gain_sums[2],
        joined(rq, 3),
        joined(rt, 2),
        ro.reshape(-1, C),
    )


def solution(mesh):
    weight = P("fsdp", None)
    gain = P("fsdp")
    field = P("fsdp", "sp", None, None)
    in_specs = (
        field,
        P("fsdp", None),
        P("fsdp", None, None),
        gain,
        gain,
        weight,
        weight,
        gain,
        weight,
        gain,
        weight,
        weight,
        weight,
        field,
    )
    out_specs = (
        field,
        field,
        P("fsdp", None),
        P("fsdp", None, None),
        gain,
        weight,
        weight,
        gain,
        weight,
        gain,
        weight,
        weight,
        weight,
    )
    return jax.shard_map(
        per_device, mesh=mesh, in_specs=in_specs, out_specs=out_specs, check_vma=False
    )
```

```python
import functools

import jax
import jax.numpy as jnp
from jax import lax
from jax.experimental import pallas as pl
from jax.experimental.pallas import tpu as pltpu
from jax.sharding import PartitionSpec as P

C = 512
GROUPS = 32
HEAD = 64
EPSILON = 1e-05
MASKED = -1e30
LIMIT = 60 * 1024 * 1024

F32 = jnp.float32
BF16 = jnp.bfloat16
DMA = pltpu.SemaphoreType.DMA
ANY = pl.BlockSpec(memory_space=pl.ANY)
VMEM = pl.BlockSpec(memory_space=pltpu.VMEM)
SMEM = pl.BlockSpec(memory_space=pltpu.SMEM)


def sizes_of(fsdp, sp):
    lines = sp if fsdp % (2 * sp) == 0 else 1
    return fsdp // (2 * lines), lines, 2


def remote(src, dst, send, recv, device):
    return pltpu.make_async_remote_copy(
        src, dst, send, recv, device_id=device, device_id_type=pl.DeviceIdType.MESH
    )


def greet(peers):
    barrier = pltpu.get_barrier_semaphore()
    for peer in peers:
        pl.semaphore_signal(
            barrier, inc=1, device_id=peer, device_id_type=pl.DeviceIdType.MESH
        )
    pl.semaphore_wait(barrier, len(peers))


def params(cid):
    return pltpu.CompilerParams(
        collective_id=cid, has_side_effects=True, vmem_limit_bytes=LIMIT
    )


def tiles_start(fsdp, source, dest, send, recv, pick):
    me, x = lax.axis_index("fsdp"), lax.axis_index("sp")
    copies = []
    for d in range(1, fsdp):
        to = (me + d) % fsdp
        copy = remote(pick(source, to), dest.at[me], send.at[d], recv.at[d], (to, x))
        copy.start()
        copies.append(copy)
    return copies


def span(index, rows, size):
    return pl.ds(pl.multiple_of(index * rows, 16 if rows % 16 == 0 else 8), size)


def aligned(index, *steps):
    if isinstance(index, int):
        return index
    return pl.multiple_of(index, 16 if all(step % 16 == 0 for step in steps) else 8)


class Gather:
    def __init__(self, dims, sp, entries, sems):
        self.dims, self.sp, self.entries = dims, sp, entries
        self.zsem, self.ysem, self.xsem, self.csem = sems
        zs, ys, cs = dims
        self.me, self.x = lax.axis_index("fsdp"), lax.axis_index("sp")
        self.z, self.y, self.c = self.me // (ys * cs), (self.me // cs) % ys, self.me % cs
        self.flying = []

    def dev(self, zz, yy, cc):
        return ((zz * self.dims[1] + yy) * self.dims[2] + cc, self.x)

    def launch(self, make, *args):
        make(*args).start()
        self.flying.append((make, args))

    def owner(self, dz, dy):
        zs, ys, _ = self.dims
        return (self.z - dz + zs) % zs, (self.y - dy + ys) % ys

    def split(self, a):
        return self.entries[a][2] > 1

    def piece(self, a):
        return self.x if self.split(a) else 0

    def home(self, a, zz, yy, cc, k=None):
        _, whole, h, rows, offset, stride = self.entries[a]
        index = ((zz * self.dims[1] + yy) * self.dims[2] + cc) * stride + offset
        if k is None:
            return whole.at[pl.ds(aligned(index, stride, offset), h * rows)]
        return whole.at[pl.ds(aligned(index + k * rows, stride, offset, rows), rows)]

    def mine(self, a):
        shard, _, h, rows, offset, stride = self.entries[a]
        if h * rows == stride and h == 1:
            return shard
        return shard.at[pl.ds(aligned(offset + self.piece(a) * rows, offset, rows), rows)]

    def own(self, a):
        shard, _, h, rows, offset, stride = self.entries[a]
        return shard if h * rows == stride else shard.at[offset : offset + h * rows]

    def zcopy(self, a, dz):
        return remote(
            self.mine(a),
            self.home(a, self.z, self.y, self.c, self.piece(a)),
            self.zsem.at[0, a, dz],
            self.zsem.at[1, a, dz],
            self.dev((self.z + dz) % self.dims[0], self.y, self.c),
        )

    def ycopy(self, a, dz, dy):
        zz, _ = self.owner(dz, 0)
        place = self.home(a, zz, self.y, self.c, self.piece(a))
        return remote(
            self.mine(a) if dz == 0 else place,
            place,
            self.ysem.at[0, a, dz, dy],
            self.ysem.at[1, a, dz, dy],
            self.dev(self.z, (self.y + dy) % self.dims[1], self.c),
        )

    def xcopy(self, a, dz, dy, dx):
        zz, yy = self.owner(dz, dy)
        place = self.home(a, zz, yy, self.c, self.x)
        return remote(
            place,
            place,
            self.xsem.at[0, a, dz, dy, dx],
            self.xsem.at[1, a, dz, dy, dx],
            (self.me, (self.x + dx) % self.sp),
        )

    def ccopy(self, a, dz, dy, dx):
        zz, yy = self.owner(dz, dy)
        if dz == 0 and dy == 0:
            src, dst = self.own(a), self.home(a, zz, yy, self.c)
        else:
            k = (self.x - dx + self.sp) % self.sp if self.split(a) else 0
            src = dst = self.home(a, zz, yy, self.c, k)
        return remote(
            src,
            dst,
            self.csem.at[0, a, dz, dy, dx],
            self.csem.at[1, a, dz, dy, dx],
            self.dev(self.z, self.y, 1 - self.c),
        )

    def onward(self, a, dz, dy):
        if self.split(a):
            for dx in range(1, self.sp):
                self.launch(self.xcopy, a, dz, dy, dx)
        self.launch(self.ccopy, a, dz, dy, 0)

    def start_z(self, a):
        for dz in range(1, self.dims[0]):
            self.launch(self.zcopy, a, dz)

    def start_y(self, a):
        for dy in range(1, self.dims[1]):
            self.launch(self.ycopy, a, 0, dy)
        self.launch(self.ccopy, a, 0, 0, 0)

    def from_z(self, a, dz):
        self.zcopy(a, dz).wait_recv()
        for dy in range(1, self.dims[1]):
            self.launch(self.ycopy, a, dz, dy)
        self.onward(a, dz, 0)

    def from_y(self, a, dz):
        for dy in range(1, self.dims[1]):
            self.ycopy(a, dz, dy).wait_recv()
            self.onward(a, dz, dy)

    def relay(self, a, dz):
        if 0 < dz < self.dims[0]:
            self.from_z(a, dz)
        if 0 < dz <= self.dims[0]:
            self.from_y(a, dz - 1)

    def over_x(self, a):
        if self.split(a):
            for dz in range(self.dims[0]):
                for dy in range(self.dims[1]):
                    if dz + dy:
                        for dx in range(1, self.sp):
                            self.xcopy(a, dz, dy, dx).wait_recv()
                            self.launch(self.ccopy, a, dz, dy, dx)

    def finish(self, a):
        for dz in range(self.dims[0]):
            for dy in range(self.dims[1]):
                many = self.sp if self.split(a) and dz + dy else 1
                for dx in range(many):
                    self.ccopy(a, dz, dy, dx).wait_recv()

    def drain(self):
        for make, args in self.flying:
            make(*args).wait_send()


def parts_of(rows, sp):
    return sp if rows % (16 * sp) == 0 else 1


def add_rows(rows, first, second, put):
    step = 32 if rows % 32 == 0 else (16 if rows % 16 == 0 else 8)

    def body(i, _):
        at = pl.ds(pl.multiple_of(i * step, step), step)
        put(at, first[at, :].astype(F32) + second[at, :].astype(F32))
        return 0

    lax.fori_loop(0, rows // step, body, 0)


class Sums:
    def __init__(self, dims, sp, shapes, modes, grads, own, outs, bufs, sems):
        self.dims, self.sp, self.shapes, self.modes = dims, sp, shapes, modes
        self.grads, self.own, self.outs = grads, own, outs
        self.crecvd, self.xrecvd, self.yrecvd, self.zrecvd, self.last = bufs
        self.csem, self.xsem, self.ysem, self.zsem, self.fsem, self.lsem = sems
        zs, ys, cs = dims
        self.me, self.x = lax.axis_index("fsdp"), lax.axis_index("sp")
        self.z, self.y, self.c = self.me // (ys * cs), (self.me // cs) % ys, self.me % cs
        self.flying = []

    def dev(self, zz, yy, cc):
        return ((zz * self.dims[1] + yy) * self.dims[2] + cc, self.x)

    def launch(self, copy):
        copy.start()
        self.flying.append(copy)

    def order(self):
        zs, ys, _ = self.dims
        return [(dz, dy) for dz in range(zs - 1, -1, -1) for dy in range(ys - 1, -1, -1)]

    def grad(self, a, dz, dy, cc):
        zs, ys, cs = self.dims
        h, rows, _ = self.shapes[a]
        owner = (((self.z + dz) % zs) * ys + (self.y + dy) % ys) * cs + cc
        return self.grads[a].at[span(owner, h * rows, h * rows)]

    def part(self, a, dz, dy, k):
        zs, ys, cs = self.dims
        h, rows, _ = self.shapes[a]
        if self.own[a] is not None:
            return self.own[a].at[dz, dy, span(k, rows, rows)]
        owner = (((self.z + dz) % zs) * ys + (self.y + dy) % ys) * cs + self.c
        return self.grads[a].at[span(owner * h + k, rows, rows)]

    def piece(self, a):
        return self.x if self.shapes[a][0] > 1 else 0

    def ccopy(self, a, dz, dy):
        return remote(
            self.grad(a, dz, dy, 1 - self.c),
            self.crecvd[a].at[dz, dy],
            self.csem.at[0, a, dz, dy],
            self.csem.at[1, a, dz, dy],
            self.dev(self.z, self.y, 1 - self.c),
        )

    def mine(self, a, dz, dy):
        return pltpu.make_async_copy(
            self.grad(a, dz, dy, self.c), self.own[a].at[dz, dy], self.lsem.at[a, dz, dy]
        )

    def xcopy(self, a, dz, dy, dx):
        to = (self.x + dx) % self.sp
        return remote(
            self.part(a, dz, dy, to),
            self.xrecvd[a].at[dz, dy, dx - 1],
            self.xsem.at[0, a, dz, dy, dx],
            self.xsem.at[1, a, dz, dy, dx],
            (self.me, to),
        )

    def ycopy(self, a, dz, dy):
        return remote(
            self.part(a, dz, dy, self.piece(a)),
            self.yrecvd[a].at[dz, dy - 1],
            self.ysem.at[0, a, dz, dy],
            self.ysem.at[1, a, dz, dy],
            self.dev(self.z, (self.y + dy) % self.dims[1], self.c),
        )

    def zcopy(self, a, dz):
        return remote(
            self.part(a, dz, 0, self.piece(a)),
            self.zrecvd[a].at[dz - 1],
            self.zsem.at[0, a, dz],
            self.zsem.at[1, a, dz],
            self.dev((self.z + dz) % self.dims[0], self.y, self.c),
        )

    def fcopy(self, a, dx):
        return remote(
            self.last[a].at[self.x],
            self.last[a].at[self.x],
            self.fsem.at[0, a, dx],
            self.fsem.at[1, a, dx],
            (self.me, (self.x + dx) % self.sp),
        )

    def add(self, a, first, second, target):
        def put(at, value):
            target[at, :] = value.astype(BF16)

        add_rows(self.shapes[a][1], first, second, put)

    def start(self, a):
        for dz, dy in self.order():
            self.launch(self.ccopy(a, dz, dy))
            if self.own[a] is not None:
                self.mine(a, dz, dy).start()

    def over_c(self, a):
        h, rows, _ = self.shapes[a]
        for dz, dy in self.order():
            if self.own[a] is not None:
                self.mine(a, dz, dy).wait()
            self.ccopy(a, dz, dy).wait_recv()
            for k in range(h):
                ref = self.part(a, dz, dy, k)
                self.add(a, ref, self.crecvd[a].at[dz, dy, pl.ds(k * rows, rows)], ref)
            if h > 1:
                for dx in range(1, self.sp):
                    self.launch(self.xcopy(a, dz, dy, dx))

    def over_x(self, a, dz):
        for dy in range(self.dims[1] - 1, -1, -1):
            if self.shapes[a][0] > 1:
                ref = self.part(a, dz, dy, self.x)
                for dx in range(1, self.sp):
                    self.xcopy(a, dz, dy, dx).wait_recv()
                    self.add(a, ref, self.xrecvd[a].at[dz, dy, dx - 1], ref)
            if dy:
                self.launch(self.ycopy(a, dz, dy))

    def over_y(self, a, dz):
        ref = self.part(a, dz, 0, self.piece(a))
        for dy in range(1, self.dims[1]):
            self.ycopy(a, dz, dy).wait_recv()
            self.add(a, ref, self.yrecvd[a].at[dz, dy - 1], ref)
        if dz:
            self.launch(self.zcopy(a, dz))

    def over_z(self, a):
        zs = self.dims[0]
        ref = self.part(a, 0, 0, self.piece(a))
        for dz in range(1, zs):
            self.zcopy(a, dz).wait_recv()
            target = self.last[a].at[self.x] if dz == zs - 1 else ref
            self.add(a, ref, self.zrecvd[a].at[dz - 1], target)
        if zs == 1:
            self.last[a][self.x] = ref[...]
        for dx in range(1, self.sp):
            self.launch(self.fcopy(a, dx))

    def all_x(self, a):
        for dz in range(self.dims[0] - 1, -1, -1):
            self.over_x(a, dz)

    def all_y(self, a):
        for dz in range(self.dims[0] - 1, -1, -1):
            self.over_y(a, dz)

    def both(self, a):
        zs = self.dims[0]
        for dz in range(zs - 1, -2, -1):
            if dz >= 0:
                self.over_x(a, dz)
            if dz < zs - 1:
                self.over_y(a, dz + 1)

    def finish(self, a):
        for dx in range(1, self.sp):
            self.fcopy(a, dx).wait_recv()
        if self.modes[a] == "add" and self.shapes[a][0] == 1:
            value = self.last[a][0].astype(F32)
            for k in range(1, self.sp):
                value = value + self.last[a][k].astype(F32)
            self.outs[a][0] = value
        elif self.modes[a] != "add":
            kinds = self.modes[a]
            width = self.shapes[a][2] // kinds
            for k in range(self.sp):
                for j in range(kinds):
                    at = (j * self.sp + k) * width
                    self.outs[a][:, at : at + width] = self.last[a][
                        k, :, j * width : (j + 1) * width
                    ].astype(F32)
        else:
            for k in range(self.sp):
                self.outs[a][k] = self.last[a][k].astype(F32)

    def drain(self):
        for copy in self.flying:
            copy.wait_send()


def lane_groups(values):
    lane = lax.broadcasted_iota(jnp.int32, values.shape, 1)
    step = 1
    while step < C // GROUPS:
        up = pltpu.roll(values, step, 1)
        down = pltpu.roll(values, C - step, 1)
        values = values + jnp.where((lane & step) != 0, up, down)
        step *= 2
    return values


def column_sums(rows, fields):
    probe = jax.eval_shape(lambda: fields(0))

    def body(r, sums):
        return tuple(
            s + jnp.sum(v.reshape(-1, 8, C), axis=0) for s, v in zip(sums, fields(r), strict=True)
        )

    sums = lax.fori_loop(0, rows, body, tuple(jnp.zeros((8, C), F32) for _ in probe))
    return [jnp.broadcast_to(jnp.sum(s, axis=0, keepdims=True), (8, C)) for s in sums]


def stack_rows(*values):
    row = lax.broadcasted_iota(jnp.int32, (8, C), 0)
    out = jnp.zeros((8, C), F32)
    for k, value in enumerate(values):
        out = jnp.where(row == k, value, out)
    return out


class Swap:
    def __init__(self, sp, sums, ssem, hsem):
        self.sp, self.sums, self.ssem, self.hsem = sp, sums, ssem, hsem
        self.me, self.x = lax.axis_index("fsdp"), lax.axis_index("sp")

    def peers(self):
        return [(self.me, (self.x + d) % self.sp) for d in range(1, self.sp)]

    def _sums(self, k, d):
        return remote(
            self.sums.at[k, self.x],
            self.sums.at[k, self.x],
            self.ssem.at[0, k, d],
            self.ssem.at[1, k, d],
            (self.me, (self.x + d) % self.sp),
        )

    def sums_start(self, k, value):
        self.sums[k, self.x] = value
        for d in range(1, self.sp):
            self._sums(k, d).start()

    def sums_wait(self, k):
        for d in range(1, self.sp):
            self._sums(k, d).wait()
        return [self.sums[k, i] for i in range(self.sp)]

    def _up(self, k, src, dst):
        to = (self.x + self.sp - 1) % self.sp
        return remote(src, dst.at[1], self.hsem.at[0, k, 0], self.hsem.at[1, k, 0], (self.me, to))

    def _down(self, k, src, dst):
        to = (self.x + 1) % self.sp
        return remote(src, dst.at[0], self.hsem.at[0, k, 1], self.hsem.at[1, k, 1], (self.me, to))

    def edges_start(self, k, top, bottom, dst):
        @pl.when(self.x > 0)
        def _():
            self._up(k, top, dst).start()

        @pl.when(self.x < self.sp - 1)
        def _():
            self._down(k, bottom, dst).start()

    def edges_wait(self, k, top, bottom, dst):
        @pl.when(self.x > 0)
        def _():
            self._up(k, top, dst).wait_send()
            self._down(k, bottom, dst).wait_recv()

        @pl.when(self.x < self.sp - 1)
        def _():
            self._down(k, bottom, dst).wait_send()
            self._up(k, top, dst).wait_recv()


def put_shifted(dst, at, value):
    columns = value.shape[0]
    col = lax.broadcasted_iota(jnp.int32, value.shape, 0)
    dst[1, at] = value.astype(BF16)
    dst[0, at] = jnp.where(col == 0, 0.0, pltpu.roll(value, 1, 0)).astype(BF16)
    dst[2, at] = jnp.where(col == columns - 1, 0.0, pltpu.roll(value, columns - 1, 0)).astype(BF16)


def taps(rows, columns, shifted, weight, acc, back, hooks=()):
    pixels = rows * columns

    def body(t, _):
        for k, hook in enumerate(hooks):
            pl.when(t == k)(hook)
        total = None
        for dc in range(3):
            if back:
                lhs = shifted[2 - dc, pl.ds(2 - t, rows)].reshape(pixels, C)
            else:
                lhs = shifted[dc, pl.ds(t, rows)].reshape(pixels, C)
            rhs = weight[pl.ds(pl.multiple_of((3 * t + dc) * C, C), C), :]
            out = lax.dot_general(
                lhs, rhs, (((1,), (1 if back else 0,)), ((), ())), preferred_element_type=F32
            )
            total = out if total is None else total + out
        total = total.reshape(rows, columns, C)

        @pl.when(t == 0)
        def _():
            acc[...] = total

        @pl.when(t > 0)
        def _():
            acc[...] += total

        return 0

    lax.fori_loop(0, 3, body, 0)


def numbers(height, rows, columns, sp):
    x = lax.axis_index("sp")
    ids = x * rows + jnp.arange(-1, rows + 1, dtype=jnp.int32)
    valid = ((ids >= 0) & (ids < height)).astype(F32)
    count = (height * columns * (C // GROUPS)).astype(F32)
    held = jnp.clip(height - rows * jnp.arange(sp, dtype=jnp.int32), 0, rows)
    held = (held * columns * (C // GROUPS)).astype(F32)
    bias = jnp.where(jnp.arange(sp * rows, dtype=jnp.int32) < height, 0.0, MASKED).astype(F32)
    return jnp.concatenate([valid, count[None], held, held[x][None], bias])


def local_moments(rows, field, mask, held):
    (total,) = column_sums(rows, lambda r: (field(r),))
    total = lane_groups(total)
    mean = (total / jnp.maximum(held, 1.0))[:1]

    def centred(r):
        v = (field(r) - mean) * mask(r)
        return (v * v,)

    (square,) = column_sums(rows, centred)
    return stack_rows(total, lane_groups(square))


def joint_moments(members, counts, count):
    mean = members[0][:1]
    for m in members[1:]:
        mean = mean + m[:1]
    mean = mean / count
    square = None
    for m, n in zip(members, counts, strict=True):
        off = m[:1] / jnp.maximum(n, 1.0) - mean
        term = m[1:2] + n * off * off
        square = term if square is None else square + term
    return mean, lax.rsqrt(square / count + EPSILON)


def forward_kernel(dims, fsdp, sp, shapes, kinds, plan, *refs):
    n = len(shapes)
    (nums, image, tiles, table), shards, refs = refs[:4], refs[4 : 4 + n], refs[4 + n :]
    (resid_out, normed, conv_out_out, s1_out, s2_out, stats, gains, scales, got), refs = (
        refs[:9],
        refs[9:],
    )
    outs, refs = refs[:n], refs[n:]
    (w1v, w2v), bufs, refs = refs[:2], refs[2:n], refs[n:]
    (edge1, edge2, acc, sums, part, part_in), refs = refs[:6], refs[6:]
    (resid, conv_out, s1, s2), refs = refs[:4], refs[4:]
    (ssem, hsem, wsem, lsem, tsem, psem, osem), sems = refs[:7], refs[7:]
    results = [
        pltpu.make_async_copy(src, dst, osem.at[i])
        for i, (src, dst) in enumerate(
            [(s1, s1_out), (conv_out, conv_out_out), (s2, s2_out), (resid, resid_out)]
        )
    ]
    sources, wholes = shards[:2] + bufs, (w1v, w2v) + outs[2:]
    entries = [(sources[a], wholes[a], h, r, at, shapes[a][0]) for a, h, r, at in plan]
    move = Gather(dims, sp, entries, sems)
    me, x = move.me, move.x
    first_of, second_of, late = (
        [e for e, p in enumerate(plan) if min(p[0], 2) == a] for a in range(3)
    )
    rows, columns = image.shape[0], image.shape[1]
    swap = Swap(sp, sums, ssem, hsem)
    homes = [wholes[a].at[span(me, shapes[a][0], shapes[a][0])] for a in range(n)]
    loads = [pltpu.make_async_copy(shards[a], homes[a], wsem.at[a]) for a in range(2)]
    staged = []
    for a in range(2, n):
        width = shapes[a][1] // kinds[a]
        for j in range(kinds[a]):
            if shards[a].shape[1] == shapes[a][1]:
                src = shards[a]
            else:
                start = pl.multiple_of((j * sp + x) * width, 128)
                src = shards[a].at[:, pl.ds(start, width)]
            dst = bufs[a - 2].at[:, j * width : (j + 1) * width]
            staged.append(pltpu.make_async_copy(src, dst, lsem.at[a, j]))
    for load in loads + staged:
        load.start()
    edge1[...] = jnp.zeros_like(edge1)
    edge2[...] = jnp.zeros_like(edge2)
    greet(swap.peers() + [((me + d) % fsdp, x) for d in range(1, fsdp)])
    first_tiles = tiles_start(
        fsdp, tiles, got, tsem.at[0], tsem.at[1], lambda ref, to: ref.at[to]
    )
    got[me] = tiles[me]
    for e in first_of:
        move.start_y(e)
        move.start_z(e)
    swap.edges_start(0, image.at[0], image.at[rows - 1], edge1)
    count = nums[rows + 2]
    counts = [nums[rows + 3 + i] for i in range(sp)]
    held = nums[rows + 3 + sp]

    def mask(r):
        return nums[r + 1]

    def masked(r):
        return image[r].astype(F32) * mask(r)

    swap.sums_start(0, local_moments(rows, masked, mask, held))
    for copy in staged:
        copy.wait()
    for e in first_of:
        move.relay(e, 1)
    stores = [pltpu.make_async_copy(bufs[a - 2], homes[a], wsem.at[a]) for a in range(2, n)]
    for copy in stores:
        copy.start()
    for copy in first_tiles:
        copy.wait_recv()
    share = C // fsdp
    many = 128 // share
    for b in range(C // 128):
        block = got[b * many]
        for f in range(b * many + 1, (b + 1) * many):
            block = block + got[f]
        gains[:, b * 128 : (b + 1) * 128] = block
    act = got[:, 0, :].astype(BF16)
    for j in range(8):
        part[:, j, :] = jnp.dot(
            act, table[:, j * 128 : (j + 1) * 128], preferred_element_type=F32
        )
    part_in[me] = part[me]
    second_tiles = tiles_start(
        fsdp, part, part_in, psem.at[0], psem.at[1], lambda ref, to: ref.at[to]
    )
    for e in second_of + late:
        move.start_z(e)
    mean1, inv1 = joint_moments(swap.sums_wait(0), counts, count)
    swap.edges_wait(0, image.at[0], image.at[rows - 1], edge1)
    g1, g2, g3 = gains[1:2], gains[2:3], gains[3:4]

    def first(at, value):
        m = nums[at]
        hidden = (value.astype(F32) * m - mean1) * m * inv1 * g1
        put_shifted(s1, at, hidden * jax.nn.sigmoid(hidden) * m)

    lax.fori_loop(0, rows, lambda r, _: (first(r + 1, image[r]), 0)[1], 0)
    first(0, edge1[0])
    first(rows + 1, edge1[1])
    results[0].start()
    for dz in range(2, dims[0] + 1):
        for e in first_of:
            move.relay(e, dz)
    for e in second_of:
        move.start_y(e)
        move.relay(e, 1)
    for e in first_of:
        move.over_x(e)
    loads[0].wait()
    for e in first_of:
        move.finish(e)
    pltpu.make_async_copy(w1v, outs[0], wsem.at[0]).start()

    def along(group, dz):
        for e in group:
            move.relay(e, dz)

    zs = dims[0]
    hooks = [functools.partial(along, second_of, dz) for dz in range(2, min(4, zs + 1))]
    taps(rows, columns, s1, w1v, acc, False, hooks)
    for dz in range(len(hooks) + 2, zs + 1):
        along(second_of, dz)
    for e in late:
        move.start_y(e)

    def keep(r, _):
        conv_out[r] = acc[r] * mask(r)
        return 0

    lax.fori_loop(0, rows, keep, 0)
    results[1].start()
    swap.edges_start(1, conv_out.at[0], conv_out.at[rows - 1], edge2)
    swap.sums_start(1, local_moments(rows, lambda r: conv_out[r], mask, held))
    along(late, 1)
    along(late, 2)
    mean2, inv2 = joint_moments(swap.sums_wait(1), counts, count)
    swap.edges_wait(1, conv_out.at[0], conv_out.at[rows - 1], edge2)
    for copy in second_tiles:
        copy.wait_recv()
    total = part_in[0]
    for f in range(1, fsdp):
        total = total + part_in[f]
    scales[...] = jnp.zeros_like(scales)
    for j in range(8):
        lanes = slice(j % 4 * 128, (j % 4 + 1) * 128)
        scales[j // 4 : j // 4 + 1, lanes] = total[j : j + 1]
    scale, shift = 1.0 + scales[0:1], scales[1:2]

    def second(at, value):
        m = nums[at]
        hidden = (value - mean2) * m * inv2 * g2 * scale + shift
        put_shifted(s2, at, hidden * jax.nn.sigmoid(hidden) * m)

    lax.fori_loop(0, rows, lambda r, _: (second(r + 1, conv_out[r]), 0)[1], 0)
    second(0, edge2[0])
    second(rows + 1, edge2[1])
    results[2].start()
    along(late, 3)
    for e in second_of:
        move.over_x(e)
    loads[1].wait()
    for e in second_of:
        move.finish(e)
    pltpu.make_async_copy(w2v, outs[1], wsem.at[1]).start()
    taps(rows, columns, s2, w2v, acc, False)
    for dz in range(4, zs + 1):
        along(late, dz)

    def add(r, _):
        resid[r] = masked(r) + acc[r] * mask(r)
        return 0

    lax.fori_loop(0, rows, add, 0)
    results[3].start()
    swap.sums_start(2, local_moments(rows, lambda r: resid[r], mask, held))
    mean3, inv3 = joint_moments(swap.sums_wait(2), counts, count)

    def third(r, _):
        normed[r] = ((resid[r] - mean3) * mask(r) * inv3 * g3).astype(BF16)
        return 0

    lax.fori_loop(0, rows, third, 0)
    stats[...] = stack_rows(mean1, inv1, mean2, inv2, mean3, inv3)
    for e in late:
        move.over_x(e)
    for e in late:
        move.finish(e)
    for copy in stores + results:
        copy.wait()
    for copy in first_tiles + second_tiles:
        copy.wait_send()
    move.drain()
    pltpu.make_async_copy(w1v, outs[0], wsem.at[0]).wait()
    pltpu.make_async_copy(w2v, outs[1], wsem.at[1]).wait()


def forward(nums, image, tiles, table, shards, kinds, fsdp, sp):
    rows, columns, _ = image.shape
    field = (rows, columns, C)
    shifted = (3, rows + 2, columns, C)
    dims = sizes_of(fsdp, sp)
    zs, ys, _ = dims
    n = len(shards)
    shapes, plan = [], []
    for a, (shard, kind) in enumerate(zip(shards, kinds, strict=True)):
        r, width = shard.shape
        shapes.append((r, width // sp if kind else width))
        h = 1 if kind else parts_of(r, sp)
        plan.append((a, h, r // h, 0))
    m = len(plan)
    wholes = [jax.ShapeDtypeStruct((fsdp * r, w), BF16) for r, w in shapes]
    staged = [pltpu.VMEM(shape, BF16) for shape in shapes[2:]]
    tile = pltpu.VMEM((fsdp, 8, 128), F32)
    return pl.pallas_call(
        functools.partial(
            forward_kernel, dims, fsdp, sp, shapes, [max(k, 1) for k in kinds], plan
        ),
        out_shape=[
            jax.ShapeDtypeStruct(field, F32),
            jax.ShapeDtypeStruct(field, BF16),
            jax.ShapeDtypeStruct(field, F32),
            jax.ShapeDtypeStruct(shifted, BF16),
            jax.ShapeDtypeStruct(shifted, BF16),
            jax.ShapeDtypeStruct((8, C), F32),
            jax.ShapeDtypeStruct((8, C), F32),
            jax.ShapeDtypeStruct((8, C), F32),
            jax.ShapeDtypeStruct((fsdp, 8, 128), F32),
        ]
        + wholes,
        in_specs=[SMEM] + [VMEM] * 3 + [ANY] * n,
        out_specs=[ANY, VMEM, ANY, ANY, ANY] + [VMEM] * 4 + [ANY] * n,
        scratch_shapes=[
            pltpu.VMEM(wholes[0].shape, BF16),
            pltpu.VMEM(wholes[1].shape, BF16),
        ]
        + staged
        + [
            pltpu.VMEM((2, columns, C), BF16),
            pltpu.VMEM((2, columns, C), F32),
            pltpu.VMEM(field, F32),
            pltpu.VMEM((3, sp, 8, C), F32),
            tile,
            tile,
            pltpu.VMEM(field, F32),
            pltpu.VMEM(field, F32),
            pltpu.VMEM(shifted, BF16),
            pltpu.VMEM(shifted, BF16),
            DMA((2, 3, sp)),
            DMA((2, 2, 2)),
            DMA((n,)),
            DMA((n, 3)),
            DMA((2, fsdp)),
            DMA((2, fsdp)),
            DMA((4,)),
            DMA((2, m, zs)),
            DMA((2, m, zs, ys)),
            DMA((2, m, zs, ys, sp)),
            DMA((2, m, zs, ys, sp)),
        ],
        compiler_params=params(1),
        name="forward",
    )(nums, image, tiles, table, *shards)


def attention_kernel(sp, heads, *refs):
    (nums, normed, text_in, wq, wt_in, wo, cot, resid_in), refs = refs[:8], refs[8:]
    (output_out, gnorm, gq_out, gt_out, go_out, gtext_out), refs = refs[:6], refs[6:]
    (nall, gown, gall, qkv, keys, values, dk, dv, att, attin, dqkv, gtkv, gpart, grecv, low), refs = (
        refs[:15],
        refs[15:],
    )
    (text, wt, resid, output, gq, gt, go, gtext), refs = refs[:8], refs[8:]
    nsem, gsem, asem, psem, isem, osem = refs
    load_text, load_wt, load_resid = (
        pltpu.make_async_copy(src, dst, isem.at[i])
        for i, (src, dst) in enumerate([(text_in, text), (wt_in, wt), (resid_in, resid)])
    )
    results = [
        pltpu.make_async_copy(src, dst, osem.at[i])
        for i, (src, dst) in enumerate(
            [(gtext, gtext_out), (output, output_out), (go, go_out), (gq, gq_out), (gt, gt_out)]
        )
    ]
    for load in (load_text, load_wt, load_resid):
        load.start()
    rows, columns = cot.shape[0], cot.shape[1]
    pixels = rows * columns
    width = heads * HEAD
    total_px = sp * pixels
    me, x = lax.axis_index("fsdp"), lax.axis_index("sp")
    factor = HEAD**-0.5
    greet([(me, (x + d) % sp) for d in range(1, sp)])

    def send(pair, src, dst):
        def copy(d):
            to = (x + d) % sp
            return remote(src(to), dst.at[x], pair.at[0, d], pair.at[1, d], (me, to))

        return [copy(d) for d in range(1, sp)]

    def start(copies):
        for copy in copies:
            copy.start()

    def wait(copies):
        for copy in copies:
            copy.wait()

    moves = send(nsem, lambda to: normed, nall)
    start(moves)

    def lower(r, _):
        low[r] = (cot[r].astype(F32) * nums[r + 1]).astype(BF16)
        return 0

    lax.fori_loop(0, rows, lower, 0)
    low2 = low[...].reshape(pixels, C)
    for k in range(sp):
        gown[k] = lax.dot_general(
            low2,
            wo[k * width : (k + 1) * width, :],
            (((1,), (1,)), ((), ())),
            preferred_element_type=F32,
        ).astype(BF16)
    gmoves = send(gsem, lambda to: gown.at[to], gall)
    start(gmoves)
    gall[x] = gown[x]
    nall[x] = normed[...]
    load_text.wait()
    load_wt.wait()
    text_kv = jnp.dot(text[...], wt[...], preferred_element_type=F32).astype(BF16)
    keys[total_px:, :] = text_kv[:, :width]
    values[total_px:, :] = text_kv[:, width:]

    def project(k):
        out = jnp.dot(nall[k], wq[...], preferred_element_type=F32).astype(BF16)
        at = pl.ds(pl.multiple_of(k * pixels, pixels), pixels)
        qkv[at, :] = out
        keys[at, :] = out[:, width : 2 * width]
        values[at, :] = out[:, 2 * width :]

    project(x)
    wait(moves)
    for d in range(1, sp):
        project((x + d) % sp)
    wait(gmoves)

    block = 256
    per = pixels // block
    for h in range(heads):
        lanes = slice(h * HEAD, (h + 1) * HEAD)
        kh, vh = keys[:, lanes], values[:, lanes]
        kt, vt = kh.T, vh.T
        dk[...] = jnp.zeros_like(dk)
        dv[...] = jnp.zeros_like(dv)

        def step(j, _, lanes=lanes, kh=kh, vh=vh, kt=kt, vt=vt):
            at = pl.ds(pl.multiple_of(j * block, block), block)
            inner = pl.ds(pl.multiple_of((j % per) * block, block), block)
            q = qkv[at, lanes]
            g = gall[j // per, inner, lanes]
            s = (
                lax.dot_general(kh, q, (((1,), (1,)), ((), ())), preferred_element_type=F32)
                * factor
            )
            pieces = [
                s[r * columns : (r + 1) * columns] + nums[rows + 4 + sp + r]
                for r in range(sp * rows)
            ]
            s = jnp.concatenate(pieces + [s[total_px:]], axis=0)
            raised = jnp.exp(s - jnp.max(s, axis=0, keepdims=True))
            chances = raised * (1.0 / jnp.sum(raised, axis=0, keepdims=True))
            short = chances.astype(BF16)
            att[j // per, inner, lanes] = jnp.dot(
                vt, short, preferred_element_type=F32
            ).T.astype(BF16)
            slope = lax.dot_general(vh, g, (((1,), (1,)), ((), ())), preferred_element_type=F32)
            mean = jnp.sum(chances * slope, axis=0, keepdims=True)
            grad = (chances * (slope - mean)).astype(BF16)
            dqkv[at, lanes] = (jnp.dot(kt, grad, preferred_element_type=F32) * factor).T.astype(
                BF16
            )
            dk[...] += jnp.dot(grad, q, preferred_element_type=F32)
            dv[...] += jnp.dot(short, g, preferred_element_type=F32)
            return 0

        lax.fori_loop(0, sp * per, step, 0)
        low_k = (dk[...] * factor).astype(BF16)
        low_v = dv[...].astype(BF16)
        dqkv[:, width + h * HEAD : width + (h + 1) * HEAD] = low_k[:total_px]
        dqkv[:, 2 * width + h * HEAD : 2 * width + (h + 1) * HEAD] = low_v[:total_px]
        gtkv[:, h * HEAD : (h + 1) * HEAD] = low_k[total_px:]
        gtkv[:, width + h * HEAD : width + (h + 1) * HEAD] = low_v[total_px:]

    amoves = send(asem, lambda to: att.at[to], attin)
    start(amoves)
    attin[x] = att[x]

    def to_normed(k):
        at = pl.ds(pl.multiple_of(k * pixels, pixels), pixels)
        return lax.dot_general(
            dqkv[at, :], wq[...], (((1,), (1,)), ((), ())), preferred_element_type=F32
        )

    for d in range(1, sp):
        to = (x + d) % sp
        gpart[to] = to_normed(to).astype(BF16)
    pmoves = send(psem, lambda to: gpart.at[to], grecv)
    start(pmoves)
    gtext[...] = lax.dot_general(
        gtkv[...], wt[...], (((1,), (1,)), ((), ())), preferred_element_type=F32
    ).astype(BF16)
    results[0].start()
    gnorm[...] = to_normed(x)
    load_resid.wait()
    wait(amoves)
    joined = jnp.concatenate([attin[k] for k in range(sp)], axis=1)
    branch = jnp.dot(joined, wo[...], preferred_element_type=F32)
    for r in range(rows):
        at = slice(r * columns, (r + 1) * columns)
        output[at, :] = (resid[at, :] + branch[at] * nums[r + 1]).astype(BF16)
    results[1].start()
    down = (((0,), (0,)), ((), ()))
    go[...] = lax.dot_general(joined, low2, down, preferred_element_type=F32).astype(BF16)
    results[2].start()
    gq[...] = lax.dot_general(
        nall[...].reshape(total_px, C), dqkv[...], down, preferred_element_type=F32
    ).astype(BF16)
    results[3].start()
    gt[...] = lax.dot_general(text[...], gtkv[...], down, preferred_element_type=F32).astype(BF16)
    results[4].start()
    wait(pmoves)
    for d in range(1, sp):
        gnorm[...] += grecv[(x + d) % sp].astype(F32)
    for copy in results:
        copy.wait()


def attention(nums, normed, text, wq, wt, wo, cot, resid, sp):
    rows, columns, _ = cot.shape
    pixels = rows * columns
    heads = C // HEAD // sp
    width = heads * HEAD
    tokens = text.shape[0]
    n_keys = sp * pixels + tokens
    return pl.pallas_call(
        functools.partial(attention_kernel, sp, heads),
        out_shape=[
            jax.ShapeDtypeStruct((pixels, C), BF16),
            jax.ShapeDtypeStruct((pixels, C), F32),
            jax.ShapeDtypeStruct(wq.shape, BF16),
            jax.ShapeDtypeStruct(wt.shape, BF16),
            jax.ShapeDtypeStruct(wo.shape, BF16),
            jax.ShapeDtypeStruct(text.shape, BF16),
        ],
        in_specs=[SMEM, VMEM, ANY, VMEM, ANY, VMEM, VMEM, ANY],
        out_specs=[ANY, VMEM, ANY, ANY, ANY, ANY],
        scratch_shapes=[
            pltpu.VMEM((sp, pixels, C), BF16),
            pltpu.VMEM((sp, pixels, width), BF16),
            pltpu.VMEM((sp, pixels, width), BF16),
            pltpu.VMEM((sp * pixels, 3 * width), BF16),
            pltpu.VMEM((n_keys, width), BF16),
            pltpu.VMEM((n_keys, width), BF16),
            pltpu.VMEM((n_keys, HEAD), F32),
            pltpu.VMEM((n_keys, HEAD), F32),
            pltpu.VMEM((sp, pixels, width), BF16),
            pltpu.VMEM((sp, pixels, width), BF16),
            pltpu.VMEM((sp * pixels, 3 * width), BF16),
            pltpu.VMEM((tokens, 2 * width), BF16),
            pltpu.VMEM((sp, pixels, C), BF16),
            pltpu.VMEM((sp, pixels, C), BF16),
            pltpu.VMEM((rows, columns, C), BF16),
            pltpu.VMEM(text.shape, BF16),
            pltpu.VMEM(wt.shape, BF16),
            pltpu.VMEM((pixels, C), F32),
            pltpu.VMEM((pixels, C), BF16),
            pltpu.VMEM(wq.shape, BF16),
            pltpu.VMEM(wt.shape, BF16),
            pltpu.VMEM(wo.shape, BF16),
            pltpu.VMEM(text.shape, BF16),
        ]
        + [DMA((2, sp))] * 4
        + [DMA((3,)), DMA((5,))],
        compiler_params=params(2),
        name="attention",
    )(nums, normed, text, wq, wt, wo, cot, resid)


def backward_kernel(dims, fsdp, sp, shapes, modes, *refs):
    n = len(shapes)
    (nums, image_in, gains, scales, stats, resid, conv_in, s1_in, s2_in, gnorm, cot), refs = (
        refs[:11],
        refs[11:],
    )
    (table, tpart, w1, w2), refs = refs[:4], refs[4:]
    attn, refs = refs[: n - 2], refs[n - 2 :]
    outs, gimage, gscales, etiles, gtotal, gtext, refs = refs[:n], *refs[n : n + 5], refs[n + 5 :]
    (w1v, w2v, out1, out2, p1, p2, edge1, edge2, gres, acc, sums, mine, every, pieces, got_e), refs = (
        refs[:15],
        refs[15:],
    )
    (ggains, got_g, gsmall, trecv, image, conv_out, s1, s2), refs = refs[:8], refs[8:]
    own, refs = (None, None) + tuple(refs[: n - 2]), refs[n - 2 :]
    bufs, refs = [refs[i * n : (i + 1) * n] for i in range(5)], refs[5 * n :]
    (ssem, hsem, wsem, tsem, esem, gsem, rsem, xsem, isem), sems = refs[:9], refs[9:]
    load_s2, load_conv, load_s1, load_image = (
        pltpu.make_async_copy(src, dst, isem.at[i])
        for i, (src, dst) in enumerate(
            [(s2_in, s2), (conv_in, conv_out), (s1_in, s1), (image_in, image)]
        )
    )
    load_s2.start()
    total_of = Sums(dims, sp, shapes, modes, (out1, out2) + tuple(attn), own, outs, bufs, sems)
    rows, columns = image.shape[0], image.shape[1]
    pixels = rows * columns
    me, x = lax.axis_index("fsdp"), lax.axis_index("sp")
    swap = Swap(sp, sums, ssem, hsem)
    load1 = pltpu.make_async_copy(w1, w1v, wsem.at[0])
    load2 = pltpu.make_async_copy(w2, w2v, wsem.at[1])
    load2.start()
    for load in (load_conv, load_s1, load1, load_image):
        load.start()
    edge1[...] = jnp.zeros_like(edge1)
    edge2[...] = jnp.zeros_like(edge2)
    greet(swap.peers() + [((me + d) % fsdp, x) for d in range(1, fsdp)])
    late = list(range(2, n))
    for a in late:
        total_of.start(a)
    count = nums[rows + 2]
    g1, g2, g3 = gains[1:2], gains[2:3], gains[3:4]
    mean1, inv1, mean2, inv2, mean3, inv3 = (stats[k : k + 1] for k in range(6))

    def mask(r):
        return nums[r + 1]

    def joint(k):
        members = swap.sums_wait(k)
        total = members[0]
        for m in members[1:]:
            total = total + m
        return total

    def weight_grad(shifted, padded, store):
        grad = padded[1, 1 : rows + 1].reshape(pixels, C)

        def body(t, _):
            for dc in range(3):
                lhs = shifted[dc, pl.ds(t, rows)].reshape(pixels, C)
                at = pl.ds(pl.multiple_of((3 * t + dc) * C, C), C)
                store[at, :] = lax.dot_general(
                    lhs, grad, (((0,), (0,)), ((), ())), preferred_element_type=F32
                ).astype(BF16)
            return 0

        lax.fori_loop(0, 3, body, 0)

    def hat3(r):
        return (resid[r] - mean3) * mask(r) * inv3

    def from_three(r):
        g = gnorm[r] * mask(r)
        return g, g * hat3(r)

    plain, crossed = column_sums(rows, from_three)
    gain3 = crossed
    swap.sums_start(0, stack_rows(lane_groups(plain * g3), lane_groups(crossed * g3)))
    total = joint(0) / count
    m1, m2 = total[0:1], total[1:2]

    def residual(r, _):
        m = mask(r)
        e = gnorm[r] * m * g3
        value = cot[r].astype(F32) * m + m * inv3 * (e - m1 - hat3(r) * m2)
        gres[r] = value
        put_shifted(p2, r + 1, value * m)
        return 0

    lax.fori_loop(0, rows, residual, 0)
    swap.edges_start(0, p2.at[1, 1], p2.at[1, rows], edge2)
    tmoves = []
    for d in range(1, sp):
        to = (me, (x + d) % sp)
        tmoves.append(remote(tpart, trecv.at[d - 1], xsem.at[0, d], xsem.at[1, d], to))
        tmoves[-1].start()
    load_s2.wait()
    weight_grad(s2, p2, out2)
    total_of.start(1)
    for a in late:
        total_of.over_c(a)
        if shapes[a][0] == 1:
            total_of.all_x(a)
    swap.edges_wait(0, p2.at[1, 1], p2.at[1, rows], edge2)
    put_shifted(p2, 0, edge2[0].astype(F32))
    put_shifted(p2, rows + 1, edge2[1].astype(F32))
    load2.wait()
    taps(rows, columns, p2, w2v, acc, True)
    total_of.over_c(1)
    total_of.all_x(1)
    scale, shift = 1.0 + scales[0:1], scales[1:2]

    def hat2(r):
        return (conv_out[r] - mean2) * mask(r) * inv2

    def slope(value):
        s = jax.nn.sigmoid(value)
        return s * (1.0 + value * (1.0 - s))

    def from_two(r):
        hat = hat2(r)
        g = acc[r] * mask(r) * slope(hat * g2 * scale + shift)
        acc[r] = g
        return g, g * hat

    load_conv.wait()
    plain, crossed = column_sums(rows, from_two)
    gain2 = crossed * scale
    swap.sums_start(
        1,
        stack_rows(
            lane_groups(plain * (scale * g2)),
            lane_groups(crossed * (scale * g2)),
            crossed * g2,
            plain,
        ),
    )
    total = joint(1)
    for k in range(8):
        row = 2 + k // 4
        lanes = slice((k % 4) * 128, (k % 4 + 1) * 128)
        mine[k : k + 1, :] = total[row : row + 1, lanes].astype(BF16).astype(F32)
    copies = tiles_start(fsdp, mine, every, tsem.at[0], tsem.at[1], lambda ref, to: ref)
    every[me] = mine[...]
    m1, m2 = total[0:1] / count, total[1:2] / count

    def middle(r, _):
        m = mask(r)
        value = m * inv2 * (acc[r] * (scale * g2) - m1 - hat2(r) * m2)
        put_shifted(p1, r + 1, value)
        return 0

    lax.fori_loop(0, rows, middle, 0)
    swap.edges_start(1, p1.at[1, 1], p1.at[1, rows], edge1)
    for a in late:
        if shapes[a][0] > 1:
            total_of.all_x(a)
    load_s1.wait()
    weight_grad(s1, p1, out1)
    total_of.start(0)
    for a in late:
        if shapes[a][0] == 1:
            total_of.all_y(a)
    swap.edges_wait(1, p1.at[1, 1], p1.at[1, rows], edge1)
    put_shifted(p1, 0, edge1[0].astype(F32))
    put_shifted(p1, rows + 1, edge1[1].astype(F32))
    load1.wait()
    total_of.over_c(0)
    taps(rows, columns, p1, w1v, acc, True)

    def hat1(r):
        return (image[r].astype(F32) * mask(r) - mean1) * mask(r) * inv1

    def from_one(r):
        hat = hat1(r)
        g = acc[r] * mask(r) * slope(hat * g1)
        acc[r] = g
        return g, g * hat

    load_image.wait()
    plain, crossed = column_sums(rows, from_one)
    swap.sums_start(2, stack_rows(lane_groups(plain * g1), lane_groups(crossed * g1)))
    ggains[...] = stack_rows(crossed, gain2, gain3)
    share = C // fsdp

    def gain_block(ref, to):
        return ref.at[:, pl.ds(pl.multiple_of((to * share) // 128 * 128, 128), 128)]

    gcopies = tiles_start(fsdp, ggains, got_g, gsem.at[0], gsem.at[1], gain_block)
    got_g[me] = ggains[:, pl.ds(pl.multiple_of((me * share) // 128 * 128, 128), 128)]
    total_of.all_y(1)
    for a in late:
        if shapes[a][0] > 1:
            total_of.all_y(a)
    for copy in copies:
        copy.wait()
    gscales[...] = every[...]
    piece = None
    for j in range(8):
        term = lax.dot_general(
            every[:, j, :].astype(BF16),
            table[:, j * 128 : (j + 1) * 128],
            (((1,), (1,)), ((), ())),
            preferred_element_type=F32,
        )
        piece = term if piece is None else piece + term
    pieces[...] = jnp.broadcast_to(piece[:, None, :], pieces.shape)
    ecopies = tiles_start(fsdp, pieces, got_e, esem.at[0], esem.at[1], lambda ref, to: ref.at[to])
    got_e[me] = pieces[me]
    total_of.both(0)
    for a in late:
        total_of.over_z(a)
    total = joint(2) / count
    m1, m2 = total[0:1], total[1:2]

    def final(r, _):
        m = mask(r)
        gimage[r] = (gres[r] + m * inv1 * (acc[r] * g1 - m1 - hat1(r) * m2)) * m
        return 0

    lax.fori_loop(0, rows, final, 0)
    total_of.over_z(1)
    total_of.over_z(0)
    for copy in tmoves:
        copy.wait()
    text_rows = 32

    def text_sum(r, _):
        at = span(r, text_rows, text_rows)
        value = tpart[at, :].astype(F32)
        for i in range(sp - 1):
            value = value + trecv[i, at, :].astype(F32)
        gtext[at, :] = value
        return 0

    lax.fori_loop(0, tpart.shape[0] // text_rows, text_sum, 0)
    for copy in gcopies:
        copy.wait()
    total = got_g[0]
    for f in range(1, fsdp):
        total = total + got_g[f]
    gsmall[x] = total

    def small_copy(d):
        to = (me, (x + d) % sp)
        return remote(gsmall.at[x], gsmall.at[x], rsem.at[0, d], rsem.at[1, d], to)

    for d in range(1, sp):
        small_copy(d).start()
    for a in late:
        total_of.finish(a)
    for copy in ecopies:
        copy.wait()
    etiles[...] = got_e[...]
    for d in range(1, sp):
        small_copy(d).wait()
    total = gsmall[0]
    for i in range(1, sp):
        total = total + gsmall[i]
    gtotal[...] = total
    total_of.finish(1)
    total_of.finish(0)
    total_of.drain()


def backward(
    nums, image, gains, scales, stats, resid, conv_out, s1, s2, gnorm, cot, table, tpart, w1, w2, attn, fsdp, sp
):
    rows, columns, _ = image.shape
    field = (rows, columns, C)
    shifted = (3, rows + 2, columns, C)
    dims = sizes_of(fsdp, sp)
    zs, ys, _ = dims
    shapes, outs = [], []
    grads = [w1, w2] + [g for g, _ in attn]
    modes = ["add", "add"] + [m for _, m in attn]
    for a, (grad, mode) in enumerate(zip(grads, modes, strict=True)):
        r, width = grad.shape[0] // fsdp, grad.shape[1]
        h = parts_of(r, sp) if mode == "add" and a != 1 else 1
        shapes.append((h, r // h, width))
        if mode == "add":
            outs.append(jax.ShapeDtypeStruct((h, r // h, width), F32))
        else:
            outs.append(jax.ShapeDtypeStruct((r, sp * width), F32))
    count = len(grads)

    def scratch(*shape):
        return pltpu.VMEM(shape, BF16)

    tile = jax.ShapeDtypeStruct((fsdp, 8, 128), F32)
    tiles = pltpu.VMEM((fsdp, 8, 128), F32)
    return pl.pallas_call(
        functools.partial(backward_kernel, dims, fsdp, sp, shapes, modes),
        out_shape=outs
        + [jax.ShapeDtypeStruct(field, F32), tile, tile, jax.ShapeDtypeStruct((8, 128), F32)]
        + [jax.ShapeDtypeStruct(tpart.shape, F32)],
        in_specs=[SMEM, ANY, VMEM, VMEM, VMEM, VMEM, ANY, ANY, ANY] + [VMEM] * 4 + [ANY] * count,
        out_specs=[VMEM] * (count + 5),
        scratch_shapes=[
            scratch(*w1.shape),
            scratch(*w2.shape),
            scratch(*w1.shape),
            scratch(*w2.shape),
            scratch(*shifted),
            scratch(*shifted),
            scratch(2, columns, C),
            scratch(2, columns, C),
            pltpu.VMEM(field, F32),
            pltpu.VMEM(field, F32),
            pltpu.VMEM((3, sp, 8, C), F32),
            pltpu.VMEM((8, 128), F32),
            tiles,
            tiles,
            tiles,
            pltpu.VMEM((8, C), F32),
            tiles,
            pltpu.VMEM((sp, 8, 128), F32),
            scratch(max(sp - 1, 1), *tpart.shape),
            scratch(*field),
            pltpu.VMEM(field, F32),
            scratch(*shifted),
            scratch(*shifted),
        ]
        + [scratch(zs, ys, s[0] * s[1], s[2]) for s in shapes[2:]]
        + [scratch(zs, ys, s[0] * s[1], s[2]) for s in shapes]
        + [
            scratch(zs, ys, sp - 1, *s[1:]) if s[0] > 1 else scratch(1, 1, 1, 16, 128)
            for s in shapes
        ]
        + [scratch(zs, max(ys - 1, 1), *s[1:]) for s in shapes]
        + [scratch(max(zs - 1, 1), *s[1:]) for s in shapes]
        + [scratch(sp, *s[1:]) for s in shapes]
        + [
            DMA((2, 3, sp)),
            DMA((2, 2, 2)),
            DMA((2,)),
            DMA((2, fsdp)),
            DMA((2, fsdp)),
            DMA((2, fsdp)),
            DMA((2, sp)),
            DMA((2, sp)),
            DMA((4,)),
            DMA((2, count, zs, ys)),
            DMA((2, count, zs, ys, sp)),
            DMA((2, count, zs, ys)),
            DMA((2, count, zs)),
            DMA((2, count, sp)),
            DMA((count, zs, ys)),
        ],
        compiler_params=params(3),
        name="backward",
    )(
        nums, image, gains, scales, stats, resid, conv_out, s1, s2, gnorm, cot, table, tpart, w1, w2,
        *[g for g, _ in attn],
    )


def per_device(
    image,
    embedding,
    text,
    heights,
    gain_one,
    conv_one,
    emb_proj,
    gain_two,
    conv_two,
    gain_three,
    qkv_proj,
    text_proj,
    out_proj,
    cotangent,
):
    rows, columns = image.shape[1], image.shape[2]
    fsdp, sp = lax.axis_size("fsdp"), lax.axis_size("sp")
    heads = C // HEAD // sp
    width = heads * HEAD
    share = gain_one.shape[0]
    emb_rows = emb_proj.shape[0]
    nums = numbers(heights[0], rows, columns, sp)
    emb_float = embedding.astype(F32)
    emb_act = jax.nn.silu(emb_float).astype(BF16)

    def lanes(array):
        return jnp.pad(array, [(0, 0)] * (array.ndim - 1) + [(0, 128 - array.shape[-1])])

    many = 128 // share
    place = lax.broadcasted_iota(jnp.int32, (3, 128), 1) // share == lax.axis_index("fsdp") % many
    gain_rows = jnp.stack([gain_one, gain_two, gain_three]).astype(F32)
    gain_rows = jnp.where(place, jnp.tile(gain_rows, (1, many)), 0.0)
    tiles = jnp.concatenate(
        [
            lanes(emb_act.astype(F32).reshape(fsdp, 1, emb_rows)),
            jnp.broadcast_to(gain_rows[None], (fsdp, 3, 128)),
            jnp.zeros((fsdp, 4, 128), F32),
        ],
        axis=1,
    )
    table = jnp.pad(emb_proj, ((0, 128 - emb_rows), (0, 0)))
    resid, normed, conv_out, s1, s2, stats, gains, scales, tiles_in, w1, w2, wt, wq, wo = forward(
        nums,
        image[0],
        tiles,
        table,
        [conv_one, conv_two, text_proj, qkv_proj, out_proj],
        [0, 0, 2, 3, 0],
        fsdp,
        sp,
    )
    emb_cols = tiles_in[:, 0, :emb_rows].astype(BF16)
    pixels = rows * columns
    output, gnorm, gq, gt, go, tpart = attention(
        nums,
        normed.reshape(pixels, C),
        text[0],
        wq,
        wt,
        wo,
        cotangent[0],
        resid.reshape(pixels, C),
        sp,
    )
    (r1, r2, rt, rq, ro, gimage, every, tiles_in, small, gtext) = backward(
        nums,
        image[0],
        gains,
        scales,
        stats,
        resid,
        conv_out,
        s1,
        s2,
        gnorm.reshape(rows, columns, C),
        cotangent[0],
        table,
        tpart,
        w1,
        w2,
        [(gt, 2), (gq, 3), (go, "add")],
        fsdp,
        sp,
    )
    grad_scales = every.reshape(fsdp, 2 * C).astype(BF16)
    grad_emb_proj = lax.dot_general(
        emb_cols, grad_scales, (((0,), (0,)), ((), ())), preferred_element_type=F32
    )

    grad_embedding = tiles_in[:, 0, :emb_rows].reshape(1, -1)
    sigmoid = jax.nn.sigmoid(emb_float)
    grad_embedding = grad_embedding * (sigmoid * (1.0 + emb_float * (1.0 - sigmoid)))
    lane = (lax.axis_index("fsdp") * share) % 128
    gain_sums = lax.dynamic_slice(small, (0, lane), (3, share))
    return (
        output.reshape(1, rows, columns, C),
        gimage[None],
        grad_embedding,
        gtext[None],
        gain_sums[0],
        r1.reshape(-1, C),
        grad_emb_proj,
        gain_sums[1],
        r2.reshape(-1, C),
        gain_sums[2],
        rq,
        rt,
        ro.reshape(-1, C),
    )


def solution(mesh):
    weight = P("fsdp", None)
    gain = P("fsdp")
    field = P("fsdp", "sp", None, None)
    in_specs = (
        field,
        P("fsdp", None),
        P("fsdp", None, None),
        gain,
        gain,
        weight,
        weight,
        gain,
        weight,
        gain,
        weight,
        weight,
        weight,
        field,
    )
    out_specs = (
        field,
        field,
        P("fsdp", None),
        P("fsdp", None, None),
        gain,
        weight,
        weight,
        gain,
        weight,
        gain,
        weight,
        weight,
        weight,
    )
    return jax.shard_map(
        per_device, mesh=mesh, in_specs=in_specs, out_specs=out_specs, check_vma=False
    )
```
